32 devices in a mesh: pipe: 4 (over z), ctx: 8 (over y, x, core).
Axes of the slice: x: 2, y: 2, z: 4, core: 2. Of those that a mesh axis runs over, the one named last changes fastest.
Arguments:
- queries: bfloat16 [4, 2048, 2048], P('pipe', 'ctx'), may hold values from -120 to 120
- keys: bfloat16 [4, 2048, 512], P('pipe', 'ctx'), may hold values from -6.5 to 6.5
- values: bfloat16 [4, 2048, 512], P('pipe', 'ctx'), may hold values from -24 to 24
- out_weight: bfloat16 [4, 2048, 4096], P('pipe'), may hold values from -0.125 to 0.125
Outputs:
- handed: bfloat16 [4, 2048, 4096], P('pipe', 'ctx')
The draws below stay inside these ranges and needn't reach their ends.
All inputs are finite; a program needn't handle non-finite values.
Results may differ from the reference program's by a relative error of at most 0.0065.
Values may be sent and summed in bfloat16 or wider, within the bound.
A program may use at most 128 MiB of HBM per device.

```python
import math
import jax
import jax.numpy as jnp
from jax import lax

D = 4096
QUERY_HEADS = 16
KEY_VALUE_HEADS = 4
HEAD_SIZE = 128
SEQUENCE_TOKENS = 2048
RELAY_SECTIONS = 4


def draw_pairs(key):
    folded = jax.random.fold_in(key, 11)
    random_query_split, random_key_split = jax.random.split(folded, 2)
    query_group_size = QUERY_HEADS // KEY_VALUE_HEADS
    random_rows_split = jnp.clip(jax.random.normal(random_key_split, (RELAY_SECTIONS, SEQUENCE_TOKENS, KEY_VALUE_HEADS, HEAD_SIZE), jnp.float32), -6.0, 6.0)
    rows_of_queries = 2.0 * jnp.clip(jax.random.normal(random_query_split, (RELAY_SECTIONS, SEQUENCE_TOKENS, KEY_VALUE_HEADS, query_group_size, HEAD_SIZE), jnp.float32), -6.0, 6.0)
    return (rows_of_queries.reshape(RELAY_SECTIONS, SEQUENCE_TOKENS, QUERY_HEADS * HEAD_SIZE), random_rows_split.reshape(RELAY_SECTIONS, SEQUENCE_TOKENS, KEY_VALUE_HEADS * HEAD_SIZE))


def draw_queries(key, part):
    return draw_pairs(key)[0].astype(jnp.bfloat16)


def draw_keys(key, part):
    return draw_pairs(key)[1].astype(jnp.bfloat16)


def block_levels(own_key, shape, pieces, smallest, largest):
    gain, own = 1.0, jax.random.fold_in(own_key, 6)
    for axis_at, blocks in pieces:
        steps = jnp.exp(jax.random.uniform(jax.random.fold_in(own, axis_at), (blocks,), jnp.float32, smallest / len(pieces), largest / len(pieces)))
        gain = gain * jnp.repeat(steps, shape[axis_at] // blocks).reshape([-1 if axis == axis_at else 1 for axis in range(len(shape))])
    return gain


def gaussian(stream_key, extent, width, limit, cuts=(), held_as=jnp.bfloat16):
    gain = block_levels(stream_key, extent, cuts, -0.22, 0.18) if cuts else 1.0
    array = jax.random.normal(stream_key, extent, jnp.float32) * width * gain
    return jnp.minimum(jnp.maximum(array, -limit), limit).astype(held_as)


def setup_inputs(seed: int = 0) -> dict:
    splits = jax.random.split(jax.random.key(seed), 5)
    return {
        "queries": draw_queries(jax.random.fold_in(splits[4], 71), 0),
        "keys": draw_keys(jax.random.fold_in(splits[4], 71), 0),
        "values": gaussian(splits[2], (RELAY_SECTIONS, SEQUENCE_TOKENS, KEY_VALUE_HEADS * HEAD_SIZE), 4.0, 24.0, ((0, 4), (1, 8))),
        "out_weight": gaussian(splits[3], (RELAY_SECTIONS, QUERY_HEADS * HEAD_SIZE, D), (QUERY_HEADS * HEAD_SIZE) ** -0.5, 0.125, ((0, 4),)),
    }


def attend_section(operands):
    queries, keys, values, out_weight = operands
    query_group_size = QUERY_HEADS // KEY_VALUE_HEADS
    heads_of_queries = queries.reshape(SEQUENCE_TOKENS, KEY_VALUE_HEADS, query_group_size, HEAD_SIZE).astype(jnp.float32)
    heads_of_keys = keys.reshape(SEQUENCE_TOKENS, KEY_VALUE_HEADS, HEAD_SIZE).astype(jnp.float32)
    heads_of_values = values.reshape(SEQUENCE_TOKENS, KEY_VALUE_HEADS, HEAD_SIZE).astype(jnp.float32)
    block_len = min(SEQUENCE_TOKENS, 1024)
    scale = 1.0 / math.sqrt(HEAD_SIZE)
    pieces_out = []
    for block_id in range(SEQUENCE_TOKENS // block_len):
        finish = (block_id + 1) * block_len
        scores = jnp.einsum('rhgd,khd->hgrk', heads_of_queries[block_id * block_len:finish], heads_of_keys[:finish]) * scale
        query_positions = block_id * block_len + jnp.arange(block_len)
        visible = jnp.arange(finish)[None, :] <= query_positions[:, None]
        scores = jnp.where(visible, scores, -jnp.inf)
        highest = lax.optimization_barrier(jnp.max(scores, axis=-1, keepdims=True))
        weights = jnp.exp(scores - highest).astype(jnp.bfloat16)
        totals = lax.optimization_barrier(jnp.sum(weights.astype(jnp.float32), axis=-1))
        summed = jnp.einsum('hgrk,khd->hgrd', weights.astype(jnp.float32), heads_of_values[:finish])
        result = summed / totals[..., None]
        pieces_out.append(jnp.transpose(result, (2, 0, 1, 3)).reshape(block_len, QUERY_HEADS * HEAD_SIZE).astype(jnp.bfloat16))
    attended = jnp.concatenate(pieces_out, axis=0)
    return jnp.dot(attended, out_weight, preferred_element_type=jnp.float32).astype(jnp.bfloat16)

def reference(queries, keys, values, out_weight):
    section_out = lax.map(attend_section, (queries, keys, values, out_weight))
    return jnp.roll(section_out, 1, axis=0)
```

```python
import functools
import math

import jax
import jax.numpy as jnp
from jax import lax
from jax.experimental import pallas as pl
from jax.experimental.pallas import tpu as pltpu
from jax.sharding import PartitionSpec as P

HEAD_SIZE = 128
COLUMNS = 256
MOVED = 2
HANDED_OVER = (0, 1, 1, 2)
EXTRA = 16
VMEM_LIMIT = 50 * 1024 * 1024
MESH = pl.DeviceIdType.MESH


def general_kernel(sections, spans, across, q_ref, k_ref, v_ref, w_ref, o_ref, held, weight, stacked, acc, top,
           attended, projected, pair_send, far_send, pass_send, relay_send, span_recv, weight_sem, out_send, out_recv, own_sem, query_sem,
           aside, landed, aside_recv, cross_send, cross_recv, final_send):
    rows, kv_width = k_ref.shape
    q_width = q_ref.shape[1]
    heads = kv_width // HEAD_SIZE
    group = q_width // kv_width
    chips = spans // 2
    pieces = weight.shape[0]
    section = lax.axis_index("pipe")
    me = lax.axis_index("ctx")
    chip, core = me // 2, lax.rem(me, 2)
    line, column = chip // across, lax.rem(chip, across)
    lines = chips // across
    following = lax.rem(section + 1, sections)
    before = lax.rem(section + sections - 1, sections)
    factor = math.log2(math.e) / math.sqrt(HEAD_SIZE)

    barrier = pltpu.get_barrier_semaphore()

    @pl.loop(1, spans)
    def _(step):
        pl.semaphore_signal(barrier, inc=1, device_id={"ctx": lax.rem(me + step, spans)}, device_id_type=MESH)

    for neighbour in (before, following):
        pl.semaphore_signal(barrier, inc=1, device_id={"pipe": neighbour}, device_id_type=MESH)

    def weight_copy(piece):
        return pltpu.make_async_copy(
            w_ref.at[:, pl.ds(pl.multiple_of(piece * COLUMNS, COLUMNS), COLUMNS)],
            weight.at[piece], weight_sem.at[piece])

    def place(owner, side, which):
        return held.at[owner, which, pl.ds(pl.multiple_of(side * rows, rows), rows), :]

    def own_copy(which):
        return pltpu.make_async_copy((k_ref, v_ref)[which], place(chip, core, which), own_sem.at[which])

    def query_copy(head, member):
        at = head * group + member
        return pltpu.make_async_copy(
            q_ref.at[:, at * HEAD_SIZE:(at + 1) * HEAD_SIZE],
            stacked.at[head, member * rows:(member + 1) * rows, :], query_sem.at[at])

    for which in range(2):
        own_copy(which).start()
    for head in range(heads):
        for member in range(group):
            query_copy(head, member).start()

    @pl.loop(0, pieces)
    def _(piece):
        weight_copy(piece).start()

    for which in range(2):
        own_copy(which).wait()

    def pair_copy(which):
        return pltpu.make_async_remote_copy(
            place(chip, core, which), place(chip, core, which), pair_send.at[which],
            span_recv.at[chip, core, which], device_id={"ctx": chip * 2 + 1 - core}, device_id_type=MESH)

    def far_copy(target, which):
        return pltpu.make_async_remote_copy(
            place(chip, core, which), place(chip, core, which), far_send.at[target, which],
            span_recv.at[chip, core, which], device_id={"ctx": target * 2 + core}, device_id_type=MESH)

    def pass_copy(owner, which):
        return pltpu.make_async_remote_copy(
            place(owner, core, which), place(owner, core, which), pass_send.at[owner, which],
            span_recv.at[owner, core, which], device_id={"ctx": chip * 2 + 1 - core}, device_id_type=MESH)

    def relay_copy(owner, target, which):
        return pltpu.make_async_remote_copy(
            place(owner, core, which), place(owner, core, which), relay_send.at[owner, target],
            span_recv.at[owner, core, which], device_id={"ctx": target * 2 + core}, device_id_type=MESH)

    def each_own(act):
        @pl.loop(1, across)
        def _(step):
            other = lax.rem(column + step, across)

            @pl.when((line < lines - 1) | (other > column))
            def _():
                act(line * across + other, 0)

        @pl.loop(line + 1, lines)
        def _(other):
            act(other * across + column, 1)
            act(other * across + column, 0)

        @pl.loop(column + 1, across)
        def _(other):
            act(line * across + other, 1)

    def each_key_source(act):
        @pl.when(line < lines - 1)
        def _():
            @pl.loop(1, across)
            def _(step):
                act(line * across + lax.rem(column + step, across))

    def each_key_relay(owner, act):
        @pl.loop(line + 1, lines)
        def _(other):
            act(owner, other * across + column, 0)

    def each_value_source(act):
        @pl.loop(0, line)
        def _(other):
            act(other * across + column)

    def each_value_relay(owner, act):
        @pl.loop(1, across)
        def _(step):
            act(owner, line * across + lax.rem(column + step, across), 1)

    def wait_span(owner, side, which):
        pltpu.make_async_remote_copy(
            place(owner, side, which), place(owner, side, which), pair_send.at[which],
            span_recv.at[owner, side, which], device_id={"ctx": chip * 2 + 1 - core}, device_id_type=MESH).wait_recv()

    pl.semaphore_wait(barrier, spans + 1)
    for which in range(2):
        pair_copy(which).start()

    each_own(lambda target, which: far_copy(target, which).start())

    for head in range(heads):
        for member in range(group):
            query_copy(head, member).wait()

    def block(owner, head, first):
        lanes = slice(head * HEAD_SIZE, (head + 1) * HEAD_SIZE)
        scores = lax.dot_general(
            held[owner, 0, :, lanes], stacked[head], (((1,), (1,)), ((), ())),
            preferred_element_type=jnp.float32)
        if first:
            key = lax.broadcasted_iota(jnp.int32, scores.shape, 0)
            row = lax.rem(lax.broadcasted_iota(jnp.int32, scores.shape, 1), rows) + core * rows
            scores = jnp.where(key <= row, scores, -1e30)
        highest = jnp.max(scores, axis=0, keepdims=True)
        if not first:
            previous = top[head]
            highest = jnp.maximum(previous, highest)
            rescale = jnp.exp2((previous - highest) * factor)
        top[head] = highest
        weights = jnp.exp2((scores - highest) * factor).astype(jnp.bfloat16)
        values = held[owner, 1, :, lanes].T
        values = jnp.concatenate([values, jnp.ones((EXTRA, values.shape[1]), values.dtype)], axis=0)
        summed = jnp.dot(values, weights, preferred_element_type=jnp.float32)
        if first:
            acc[head] = summed
        else:
            acc[head] = acc[head] * rescale + summed

    for which in range(2):
        wait_span(chip, 1 - core, which)

    for head in range(heads):
        block(chip, head, True)

    def relay_keys(owner):
        wait_span(owner, core, 0)
        each_key_relay(owner, lambda *at: relay_copy(*at).start())

        @pl.when(owner < chip)
        def _():
            pass_copy(owner, 0).start()

    def relay_values(owner):
        wait_span(owner, core, 1)
        each_value_relay(owner, lambda *at: relay_copy(*at).start())
        pass_copy(owner, 1).start()

    each_value_source(relay_values)
    each_key_source(relay_keys)

    @pl.loop(0, chip)
    def _(step):
        owner = chip - 1 - step

        @pl.when((owner // across != line) | (line == lines - 1))
        def _():
            wait_span(owner, core, 0)
            pass_copy(owner, 0).start()

        @pl.when((lax.rem(owner, across) != column) | (owner // across == line))
        def _():
            wait_span(owner, core, 1)
            pass_copy(owner, 1).start()

        for which in range(2):
            wait_span(owner, 1 - core, which)

        for head in range(heads):
            block(owner, head, False)

    for head in range(heads):
        for member in range(group):
            part = acc[head, :, member * rows:(member + 1) * rows]
            attended[:, (head * group + member) * HEAD_SIZE:(head * group + member + 1) * HEAD_SIZE] = (
                part[:HEAD_SIZE] / part[HEAD_SIZE:HEAD_SIZE + 1]).T.astype(jnp.bfloat16)

    def out_copy(piece):
        return pltpu.make_async_remote_copy(
            projected.at[piece],
            o_ref.at[:, pl.ds(pl.multiple_of(piece * COLUMNS, COLUMNS), COLUMNS)],
            out_send.at[piece], out_recv.at[piece], device_id={"pipe": following}, device_id_type=MESH)

    late = chips - chips // 2
    heavy = chip >= late
    slot_of = lax.rem(chip + 2 * chips - late, 2)

    def aside_copy(piece):
        return pltpu.make_async_remote_copy(
            projected.at[piece], aside.at[slot_of, piece], out_send.at[piece],
            aside_recv.at[slot_of, piece],
            device_id={"ctx": (chip - late) // 2 * 2 + core}, device_id_type=MESH)

    def cross_copy(slot, piece):
        return pltpu.make_async_remote_copy(
            aside.at[slot, piece], landed.at[slot, piece], cross_send.at[slot, piece],
            cross_recv.at[slot, piece], device_id={"pipe": following}, device_id_type=MESH)

    def final_copy(slot, piece):
        return pltpu.make_async_remote_copy(
            landed.at[slot, piece],
            o_ref.at[:, pl.ds(pl.multiple_of(piece * COLUMNS, COLUMNS), COLUMNS)],
            final_send.at[slot, piece], out_recv.at[piece],
            device_id={"ctx": (late + chip * 2 + slot) * 2 + core}, device_id_type=MESH)

    def each_carried(act):
        @pl.loop(0, jnp.clip(chips // 2 - chip * 2, 0, 2))
        def _(slot):
            @pl.loop(0, MOVED)
            def _(piece):
                act(slot, piece)

    def carry(slot, piece):
        pltpu.make_async_remote_copy(
            aside.at[slot, piece], aside.at[slot, piece], cross_send.at[slot, piece],
            aside_recv.at[slot, piece], device_id={"pipe": following}, device_id_type=MESH).wait_recv()
        cross_copy(slot, piece).start()

    def deliver(slot, piece):
        cross_copy(slot, piece).wait_recv()
        final_copy(slot, piece).start()

    def settle(slot, piece):
        cross_copy(slot, piece).wait_send()
        final_copy(slot, piece).wait_send()

    @pl.loop(0, pieces)
    def _(piece):
        weight_copy(piece).wait()
        projected[piece] = jnp.dot(
            attended[...], weight[piece], preferred_element_type=jnp.float32).astype(jnp.bfloat16)

        @pl.when(heavy & (piece < MOVED))
        def _():
            aside_copy(piece).start()

        @pl.when(jnp.logical_not(heavy & (piece < MOVED)))
        def _():
            out_copy(piece).start()

    each_carried(carry)
    each_carried(deliver)

    for which in range(2):
        pair_copy(which).wait_send()

    each_own(lambda target, which: far_copy(target, which).wait_send())
    each_key_source(lambda owner: each_key_relay(
        owner, lambda *at: relay_copy(*at).wait_send()))
    each_value_source(lambda owner: each_value_relay(
        owner, lambda *at: relay_copy(*at).wait_send()))

    @pl.loop(0, chip)
    def _(owner):
        for which in range(2):
            pass_copy(owner, which).wait_send()

    each_carried(settle)

    @pl.loop(0, pieces)
    def _(piece):
        out_copy(piece).wait()


def square_kernel(sections, q_ref, k_ref, v_ref, w_ref, o_ref, held, weight, query, acc, top, attended, projected, aside,
                  far_send, span_recv, pass_send, relay_send, own_sem, query_sem, weight_sem, out_send, out_recv,
                  aside_recv, deliver_send):
    rows, kv_width = k_ref.shape
    heads = kv_width // HEAD_SIZE
    group = q_ref.shape[1] // kv_width
    pieces = weight.shape[0]
    section = lax.axis_index("pipe")
    me = lax.axis_index("ctx")
    chip, core = me // 2, lax.rem(me, 2)
    sibling = chip * 2 + 1 - core
    beside = (chip + 1 - 2 * lax.rem(chip, 2)) * 2 + core
    across = lax.rem(chip + 2, 4) * 2 + core
    opposite = (3 - chip) * 2 + core
    following = lax.rem(section + 1, sections)
    before = lax.rem(section + sections - 1, sections)
    factor = math.log2(math.e) / math.sqrt(HEAD_SIZE)

    barrier = pltpu.get_barrier_semaphore()
    for other in (sibling, beside, across, opposite):
        pl.semaphore_signal(barrier, inc=1, device_id={"ctx": other}, device_id_type=MESH)
    for neighbour in (before, following):
        pl.semaphore_signal(barrier, inc=1, device_id={"pipe": neighbour}, device_id_type=MESH)

    @pl.when(chip > 0)
    def _():
        pl.semaphore_signal(barrier, inc=1, device_id={"pipe": before, "ctx": core}, device_id_type=MESH)

    def lanes(head):
        return slice(head * HEAD_SIZE, (head + 1) * HEAD_SIZE)

    def own_copy(which):
        return pltpu.make_async_copy((k_ref, v_ref)[which], held.at[chip, core, which], own_sem.at[which])

    def query_copy(head):
        wide = group * HEAD_SIZE
        return pltpu.make_async_copy(
            q_ref.at[:, head * wide:(head + 1) * wide], query.at[:, head * wide:(head + 1) * wide], query_sem.at[head])

    def weight_copy(piece):
        return pltpu.make_async_copy(
            w_ref.at[:, pl.ds(pl.multiple_of(piece * COLUMNS, COLUMNS), COLUMNS)],
            weight.at[piece], weight_sem.at[piece])

    for which in range(2):
        own_copy(which).start()
    for head in range(heads):
        query_copy(head).start()

    def at_head(head):
        return pl.ds(pl.multiple_of(head * HEAD_SIZE, HEAD_SIZE), HEAD_SIZE)

    def span_copy(owner, head, side, send_sem, target):
        chunk = held.at[owner, side, :, :, at_head(head)]
        return pltpu.make_async_remote_copy(
            chunk, chunk, send_sem, span_recv.at[owner, side, head], device_id={"ctx": target}, device_id_type=MESH)

    def first_copy(head, way, target):
        return span_copy(chip, head, core, far_send.at[way, head], target)

    def each_first(act):
        for head in range(heads):
            @pl.when(core == 0)
            def _():
                act(head, 0, sibling)

            @pl.when(lax.rem(chip, 2) == 0)
            def _():
                act(head, 1, beside)

            @pl.when(chip < 2)
            def _():
                act(head, 2, across)

        @pl.when(chip == 0)
        def _():
            for head in range(heads // 2):
                act(head, 3, opposite)

    pl.semaphore_wait(barrier, jnp.where(chip == 0, 9, 6))

    for which in range(2):
        own_copy(which).wait()
    each_first(lambda *way: first_copy(*way).start())

    def stacked(head):
        return jnp.concatenate(
            [query[:, at_head(head * group + member)] for member in range(group)], axis=0)

    def block(keys, values, head, first):
        scores = lax.dot_general(
            keys, stacked(head), (((1,), (1,)), ((), ())), preferred_element_type=jnp.float32)
        if first:
            key = lax.broadcasted_iota(jnp.int32, scores.shape, 0)
            row = lax.rem(lax.broadcasted_iota(jnp.int32, scores.shape, 1), rows)
            scores = jnp.where(key <= row, scores, -1e30)
        highest = jnp.max(scores, axis=0, keepdims=True)
        if not first:
            previous = top[head]
            highest = jnp.maximum(previous, highest)
            rescale = jnp.exp2((previous - highest) * factor)
        top[head] = highest
        weights = jnp.exp2((scores - highest) * factor).astype(jnp.bfloat16)
        values = values.T
        values = jnp.concatenate([values, jnp.ones((EXTRA, values.shape[1]), values.dtype)], axis=0)
        summed = jnp.dot(values, weights, preferred_element_type=jnp.float32)
        if first:
            acc[head] = summed
        else:
            acc[head] = acc[head] * rescale + summed

    for head in range(heads):
        query_copy(head).wait()

    @pl.loop(0, pieces)
    def _(piece):
        weight_copy(piece).start()

    for head in range(heads):
        block(held[chip, core, 0, :, lanes(head)], held[chip, core, 1, :, lanes(head)], head, True)

    @pl.when(core == 1)
    def _():
        for head in range(heads):
            span_copy(chip, head, 0, far_send.at[0, head], sibling).wait_recv()
        for head in range(heads):
            block(held[chip, 0, 0, :, lanes(head)], held[chip, 0, 1, :, lanes(head)], head, False)

    steps = chip * heads

    def at(step):
        later = step - 2 * heads
        owner_last = jnp.where(later < 0, 1 + lax.rem(step, 2), 0)
        head_last = jnp.where(later < 0, step // 2, lax.rem(later, 2) * (heads // 2) + later // 2)
        second = (step == 3) | (step > 4)
        head_third = jnp.where(second, jnp.where(step == 3, 0, step - heads), jnp.where(step == 4, step - 1, step))
        owner = jnp.where(chip == 3, owner_last, jnp.where((chip == 2) & second, 1, 0))
        head = jnp.where(chip == 3, head_last, jnp.where(chip == 2, head_third, step))
        return owner, head

    def relayed(owner, head):
        return ((chip == 2) & (owner == 0) & (head >= heads // 2)) | ((chip == 3) & (owner == 1))

    def arrive(step):
        owner, head = at(step)
        span_copy(owner, head, core, pass_send.at[owner, head], sibling).wait_recv()

        @pl.when(relayed(owner, head))
        def _():
            span_copy(owner, head, core, relay_send.at[head], beside).start()

        span_copy(owner, head, core, pass_send.at[owner, head], sibling).start()

    @pl.when(chip > 0)
    def _():
        arrive(0)

    @pl.loop(0, steps)
    def _(step):
        @pl.when(step + 1 < steps)
        def _():
            arrive(step + 1)

        owner, head = at(step)
        span_copy(owner, head, 1 - core, pass_send.at[owner, head], sibling).wait_recv()
        keys = held[owner, :, 0, :, at_head(head)].reshape(2 * rows, HEAD_SIZE)
        values = held[owner, :, 1, :, at_head(head)].reshape(2 * rows, HEAD_SIZE)
        block(keys, values, head, False)

    for head in range(heads):
        for member in range(group):
            part = acc[head, :, member * rows:(member + 1) * rows]
            attended[:, lanes(head * group + member)] = (
                part[:HEAD_SIZE] / part[HEAD_SIZE:HEAD_SIZE + 1]).T.astype(jnp.bfloat16)

    moved, base = 0, 0
    slots = []
    for origin, count in enumerate(HANDED_OVER):
        moved = jnp.where(chip == origin, count, moved)
        base = jnp.where(chip == origin, len(slots), base)
        slots += [(origin, pieces - count + each) for each in range(count)]
    kept = pieces - moved

    def columns(piece):
        return o_ref.at[:, pl.ds(pl.multiple_of(piece * COLUMNS, COLUMNS), COLUMNS)]

    def out_copy(piece):
        return pltpu.make_async_remote_copy(
            projected.at[piece], columns(piece), out_send.at[piece], out_recv.at[piece],
            device_id={"pipe": following}, device_id_type=MESH)

    def aside_copy(piece):
        slot = base + piece - kept
        return pltpu.make_async_remote_copy(
            projected.at[piece], aside.at[slot], out_send.at[piece], aside_recv.at[slot],
            device_id={"ctx": core}, device_id_type=MESH)

    def deliver_copy(slot):
        origin, piece = slots[slot]
        return pltpu.make_async_remote_copy(
            aside.at[slot], columns(piece), deliver_send.at[slot], out_recv.at[piece],
            device_id={"pipe": following, "ctx": origin * 2 + core}, device_id_type=MESH)

    @pl.loop(0, pieces)
    def _(piece):
        weight_copy(piece).wait()
        projected[piece] = jnp.dot(
            attended[...], weight[piece], preferred_element_type=jnp.float32).astype(jnp.bfloat16)

        @pl.when(piece < kept)
        def _():
            out_copy(piece).start()

        @pl.when(piece >= kept)
        def _():
            aside_copy(piece).start()

    @pl.when(chip == 0)
    def _():
        for slot in range(len(slots)):
            pltpu.make_async_remote_copy(
                aside.at[slot], aside.at[slot], deliver_send.at[slot], aside_recv.at[slot],
                device_id={"ctx": sibling}, device_id_type=MESH).wait_recv()
            deliver_copy(slot).start()

    each_first(lambda *way: first_copy(*way).wait_send())

    @pl.loop(0, steps)
    def _(step):
        owner, head = at(step)
        span_copy(owner, head, core, pass_send.at[owner, head], sibling).wait_send()

        @pl.when(relayed(owner, head))
        def _():
            span_copy(owner, head, core, relay_send.at[head], beside).wait_send()

    @pl.when(chip == 0)
    def _():
        for slot in range(len(slots)):
            deliver_copy(slot).wait_send()

    @pl.loop(0, pieces)
    def _(piece):
        out_copy(piece).wait()


def general_device(sections, spans, queries, keys, values, out_weight):
    rows, q_width = queries.shape[1:]
    kv_width = keys.shape[2]
    width = out_weight.shape[2]
    heads = kv_width // HEAD_SIZE
    stack = q_width // kv_width * rows
    pieces = width // COLUMNS
    chips = spans // 2
    across = math.isqrt(chips)
    across = across if chips % across == 0 else chips
    hbm = pl.BlockSpec(memory_space=pltpu.HBM)
    handed = pl.pallas_call(
        functools.partial(general_kernel, sections, spans, across),
        out_shape=jax.ShapeDtypeStruct((rows, width), jnp.bfloat16),
        in_specs=[hbm] * 4,
        out_specs=pl.BlockSpec(memory_space=pl.ANY),
        scratch_shapes=[
            pltpu.VMEM((chips, 2, 2 * rows, kv_width), jnp.bfloat16),
            pltpu.VMEM((pieces, q_width, COLUMNS), jnp.bfloat16),
            pltpu.VMEM((heads, stack, HEAD_SIZE), jnp.bfloat16),
            pltpu.VMEM((heads, HEAD_SIZE + EXTRA, stack), jnp.float32),
            pltpu.VMEM((heads, 1, stack), jnp.float32),
            pltpu.VMEM((rows, q_width), jnp.bfloat16),
            pltpu.VMEM((pieces, rows, COLUMNS), jnp.bfloat16),
            pltpu.SemaphoreType.DMA((2,)),
            pltpu.SemaphoreType.DMA((chips, 2)),
            pltpu.SemaphoreType.DMA((chips, 2)),
            pltpu.SemaphoreType.DMA((chips, chips)),
            pltpu.SemaphoreType.DMA((chips, 2, 2)),
            pltpu.SemaphoreType.DMA((pieces,)),
            pltpu.SemaphoreType.DMA((pieces,)),
            pltpu.SemaphoreType.DMA((pieces,)),
            pltpu.SemaphoreType.DMA((2,)),
            pltpu.SemaphoreType.DMA((q_width // HEAD_SIZE,)),
            pltpu.VMEM((2, MOVED, rows, COLUMNS), jnp.bfloat16),
            pltpu.VMEM((2, MOVED, rows, COLUMNS), jnp.bfloat16),
            pltpu.SemaphoreType.DMA((2, MOVED)),
            pltpu.SemaphoreType.DMA((2, MOVED)),
            pltpu.SemaphoreType.DMA((2, MOVED)),
            pltpu.SemaphoreType.DMA((2, MOVED)),
        ],
        compiler_params=pltpu.CompilerParams(
            collective_id=0, has_side_effects=True, vmem_limit_bytes=VMEM_LIMIT),
    )(*(pltpu.with_memory_space_constraint(each[0], pltpu.HBM) for each in (queries, keys, values, out_weight)))
    return handed[None]


def square_device(sections, queries, keys, values, out_weight):
    rows, q_width = queries.shape[1:]
    kv_width = keys.shape[2]
    width = out_weight.shape[2]
    heads = kv_width // HEAD_SIZE
    stack = q_width // kv_width * rows
    pieces = width // COLUMNS
    slots = sum(HANDED_OVER)
    hbm = pl.BlockSpec(memory_space=pltpu.HBM)
    handed = pl.pallas_call(
        functools.partial(square_kernel, sections),
        out_shape=jax.ShapeDtypeStruct((rows, width), jnp.bfloat16),
        in_specs=[hbm] * 4,
        out_specs=pl.BlockSpec(memory_space=pl.ANY),
        scratch_shapes=[
            pltpu.VMEM((4, 2, 2, rows, kv_width), jnp.bfloat16),
            pltpu.VMEM((pieces, q_width, COLUMNS), jnp.bfloat16),
            pltpu.VMEM((rows, q_width), jnp.bfloat16),
            pltpu.VMEM((heads, HEAD_SIZE + EXTRA, stack), jnp.float32),
            pltpu.VMEM((heads, 1, stack), jnp.float32),
            pltpu.VMEM((rows, q_width), jnp.bfloat16),
            pltpu.VMEM((pieces, rows, COLUMNS), jnp.bfloat16),
            pltpu.VMEM((slots, rows, COLUMNS), jnp.bfloat16),
            pltpu.SemaphoreType.DMA((4, heads)),
            pltpu.SemaphoreType.DMA((4, 2, heads)),
            pltpu.SemaphoreType.DMA((4, heads)),
            pltpu.SemaphoreType.DMA((heads,)),
            pltpu.SemaphoreType.DMA((2,)),
            pltpu.SemaphoreType.DMA((heads,)),
            pltpu.SemaphoreType.DMA((pieces,)),
            pltpu.SemaphoreType.DMA((pieces,)),
            pltpu.SemaphoreType.DMA((pieces,)),
            pltpu.SemaphoreType.DMA((slots,)),
            pltpu.SemaphoreType.DMA((slots,)),
        ],
        compiler_params=pltpu.CompilerParams(
            collective_id=1, has_side_effects=True, vmem_limit_bytes=VMEM_LIMIT),
    )(*(pltpu.with_memory_space_constraint(each[0], pltpu.HBM) for each in (queries, keys, values, out_weight)))
    return handed[None]


def per_device(sections, spans, *operands):
    if spans == 8:
        return square_device(sections, *operands)
    return general_device(sections, spans, *operands)


def solution(mesh):
    placed = (
        P("pipe", "ctx", None),
        P("pipe", "ctx", None),
        P("pipe", "ctx", None),
        P("pipe", None, None),
    )
    return jax.shard_map(
        functools.partial(per_device, mesh.shape["pipe"], mesh.shape["ctx"]),
        mesh=mesh, in_specs=placed, out_specs=P("pipe", "ctx", None), check_vma=False
    )
```

```python
import functools
import math

import jax
import jax.numpy as jnp
from jax import lax
from jax.experimental import pallas as pl
from jax.experimental.pallas import tpu as pltpu
from jax.sharding import PartitionSpec as P

HEAD_SIZE = 128
COLUMNS = 256
MOVED = 2
HANDED_OVER = ((0, 0), (1, 0), (1, 1), (2, 3))
EXTRA = 16
VMEM_LIMIT = 50 * 1024 * 1024
MESH = pl.DeviceIdType.MESH


def general_kernel(sections, spans, across, q_ref, k_ref, v_ref, w_ref, o_ref, held, weight, stacked, acc, top,
           attended, projected, pair_send, far_send, pass_send, relay_send, span_recv, weight_sem, out_send, out_recv, own_sem, query_sem,
           aside, landed, aside_recv, cross_send, cross_recv, final_send):
    rows, kv_width = k_ref.shape
    q_width = q_ref.shape[1]
    heads = kv_width // HEAD_SIZE
    group = q_width // kv_width
    chips = spans // 2
    pieces = weight.shape[0]
    section = lax.axis_index("pipe")
    me = lax.axis_index("ctx")
    chip, core = me // 2, lax.rem(me, 2)
    line, column = chip // across, lax.rem(chip, across)
    lines = chips // across
    following = lax.rem(section + 1, sections)
    before = lax.rem(section + sections - 1, sections)
    factor = math.log2(math.e) / math.sqrt(HEAD_SIZE)

    barrier = pltpu.get_barrier_semaphore()

    @pl.loop(1, spans)
    def _(step):
        pl.semaphore_signal(barrier, inc=1, device_id={"ctx": lax.rem(me + step, spans)}, device_id_type=MESH)

    for neighbour in (before, following):
        pl.semaphore_signal(barrier, inc=1, device_id={"pipe": neighbour}, device_id_type=MESH)

    def weight_copy(piece):
        return pltpu.make_async_copy(
            w_ref.at[:, pl.ds(pl.multiple_of(piece * COLUMNS, COLUMNS), COLUMNS)],
            weight.at[piece], weight_sem.at[piece])

    def place(owner, side, which):
        return held.at[owner, which, pl.ds(pl.multiple_of(side * rows, rows), rows), :]

    def own_copy(which):
        return pltpu.make_async_copy((k_ref, v_ref)[which], place(chip, core, which), own_sem.at[which])

    def query_copy(head, member):
        at = head * group + member
        return pltpu.make_async_copy(
            q_ref.at[:, at * HEAD_SIZE:(at + 1) * HEAD_SIZE],
            stacked.at[head, member * rows:(member + 1) * rows, :], query_sem.at[at])

    for which in range(2):
        own_copy(which).start()
    for head in range(heads):
        for member in range(group):
            query_copy(head, member).start()

    @pl.loop(0, pieces)
    def _(piece):
        weight_copy(piece).start()

    for which in range(2):
        own_copy(which).wait()

    def pair_copy(which):
        return pltpu.make_async_remote_copy(
            place(chip, core, which), place(chip, core, which), pair_send.at[which],
            span_recv.at[chip, core, which], device_id={"ctx": chip * 2 + 1 - core}, device_id_type=MESH)

    def far_copy(target, which):
        return pltpu.make_async_remote_copy(
            place(chip, core, which), place(chip, core, which), far_send.at[target, which],
            span_recv.at[chip, core, which], device_id={"ctx": target * 2 + core}, device_id_type=MESH)

    def pass_copy(owner, which):
        return pltpu.make_async_remote_copy(
            place(owner, core, which), place(owner, core, which), pass_send.at[owner, which],
            span_recv.at[owner, core, which], device_id={"ctx": chip * 2 + 1 - core}, device_id_type=MESH)

    def relay_copy(owner, target, which):
        return pltpu.make_async_remote_copy(
            place(owner, core, which), place(owner, core, which), relay_send.at[owner, target],
            span_recv.at[owner, core, which], device_id={"ctx": target * 2 + core}, device_id_type=MESH)

    def each_own(act):
        @pl.loop(1, across)
        def _(step):
            other = lax.rem(column + step, across)

            @pl.when((line < lines - 1) | (other > column))
            def _():
                act(line * across + other, 0)

        @pl.loop(line + 1, lines)
        def _(other):
            act(other * across + column, 1)
            act(other * across + column, 0)

        @pl.loop(column + 1, across)
        def _(other):
            act(line * across + other, 1)

    def each_key_source(act):
        @pl.when(line < lines - 1)
        def _():
            @pl.loop(1, across)
            def _(step):
                act(line * across + lax.rem(column + step, across))

    def each_key_relay(owner, act):
        @pl.loop(line + 1, lines)
        def _(other):
            act(owner, other * across + column, 0)

    def each_value_source(act):
        @pl.loop(0, line)
        def _(other):
            act(other * across + column)

    def each_value_relay(owner, act):
        @pl.loop(1, across)
        def _(step):
            act(owner, line * across + lax.rem(column + step, across), 1)

    def wait_span(owner, side, which):
        pltpu.make_async_remote_copy(
            place(owner, side, which), place(owner, side, which), pair_send.at[which],
            span_recv.at[owner, side, which], device_id={"ctx": chip * 2 + 1 - core}, device_id_type=MESH).wait_recv()

    pl.semaphore_wait(barrier, spans + 1)
    for which in range(2):
        pair_copy(which).start()

    each_own(lambda target, which: far_copy(target, which).start())

    for head in range(heads):
        for member in range(group):
            query_copy(head, member).wait()

    def block(owner, head, first):
        lanes = slice(head * HEAD_SIZE, (head + 1) * HEAD_SIZE)
        scores = lax.dot_general(
            held[owner, 0, :, lanes], stacked[head], (((1,), (1,)), ((), ())),
            preferred_element_type=jnp.float32)
        if first:
            key = lax.broadcasted_iota(jnp.int32, scores.shape, 0)
            row = lax.rem(lax.broadcasted_iota(jnp.int32, scores.shape, 1), rows) + core * rows
            scores = jnp.where(key <= row, scores, -1e30)
        highest = jnp.max(scores, axis=0, keepdims=True)
        if not first:
            previous = top[head]
            highest = jnp.maximum(previous, highest)
            rescale = jnp.exp2((previous - highest) * factor)
        top[head] = highest
        weights = jnp.exp2((scores - highest) * factor).astype(jnp.bfloat16)
        values = held[owner, 1, :, lanes].T
        values = jnp.concatenate([values, jnp.ones((EXTRA, values.shape[1]), values.dtype)], axis=0)
        summed = jnp.dot(values, weights, preferred_element_type=jnp.float32)
        if first:
            acc[head] = summed
        else:
            acc[head] = acc[head] * rescale + summed

    for which in range(2):
        wait_span(chip, 1 - core, which)

    for head in range(heads):
        block(chip, head, True)

    def relay_keys(owner):
        wait_span(owner, core, 0)
        each_key_relay(owner, lambda *at: relay_copy(*at).start())

        @pl.when(owner < chip)
        def _():
            pass_copy(owner, 0).start()

    def relay_values(owner):
        wait_span(owner, core, 1)
        each_value_relay(owner, lambda *at: relay_copy(*at).start())
        pass_copy(owner, 1).start()

    each_value_source(relay_values)
    each_key_source(relay_keys)

    @pl.loop(0, chip)
    def _(step):
        owner = chip - 1 - step

        @pl.when((owner // across != line) | (line == lines - 1))
        def _():
            wait_span(owner, core, 0)
            pass_copy(owner, 0).start()

        @pl.when((lax.rem(owner, across) != column) | (owner // across == line))
        def _():
            wait_span(owner, core, 1)
            pass_copy(owner, 1).start()

        for which in range(2):
            wait_span(owner, 1 - core, which)

        for head in range(heads):
            block(owner, head, False)

    for head in range(heads):
        for member in range(group):
            part = acc[head, :, member * rows:(member + 1) * rows]
            attended[:, (head * group + member) * HEAD_SIZE:(head * group + member + 1) * HEAD_SIZE] = (
                part[:HEAD_SIZE] / part[HEAD_SIZE:HEAD_SIZE + 1]).T.astype(jnp.bfloat16)

    def out_copy(piece):
        return pltpu.make_async_remote_copy(
            projected.at[piece],
            o_ref.at[:, pl.ds(pl.multiple_of(piece * COLUMNS, COLUMNS), COLUMNS)],
            out_send.at[piece], out_recv.at[piece], device_id={"pipe": following}, device_id_type=MESH)

    late = chips - chips // 2
    heavy = chip >= late
    slot_of = lax.rem(chip + 2 * chips - late, 2)

    def aside_copy(piece):
        return pltpu.make_async_remote_copy(
            projected.at[piece], aside.at[slot_of, piece], out_send.at[piece],
            aside_recv.at[slot_of, piece],
            device_id={"ctx": (chip - late) // 2 * 2 + core}, device_id_type=MESH)

    def cross_copy(slot, piece):
        return pltpu.make_async_remote_copy(
            aside.at[slot, piece], landed.at[slot, piece], cross_send.at[slot, piece],
            cross_recv.at[slot, piece], device_id={"pipe": following}, device_id_type=MESH)

    def final_copy(slot, piece):
        return pltpu.make_async_remote_copy(
            landed.at[slot, piece],
            o_ref.at[:, pl.ds(pl.multiple_of(piece * COLUMNS, COLUMNS), COLUMNS)],
            final_send.at[slot, piece], out_recv.at[piece],
            device_id={"ctx": (late + chip * 2 + slot) * 2 + core}, device_id_type=MESH)

    def each_carried(act):
        @pl.loop(0, jnp.clip(chips // 2 - chip * 2, 0, 2))
        def _(slot):
            @pl.loop(0, MOVED)
            def _(piece):
                act(slot, piece)

    def carry(slot, piece):
        pltpu.make_async_remote_copy(
            aside.at[slot, piece], aside.at[slot, piece], cross_send.at[slot, piece],
            aside_recv.at[slot, piece], device_id={"pipe": following}, device_id_type=MESH).wait_recv()
        cross_copy(slot, piece).start()

    def deliver(slot, piece):
        cross_copy(slot, piece).wait_recv()
        final_copy(slot, piece).start()

    def settle(slot, piece):
        cross_copy(slot, piece).wait_send()
        final_copy(slot, piece).wait_send()

    @pl.loop(0, pieces)
    def _(piece):
        weight_copy(piece).wait()
        projected[piece] = jnp.dot(
            attended[...], weight[piece], preferred_element_type=jnp.float32).astype(jnp.bfloat16)

        @pl.when(heavy & (piece < MOVED))
        def _():
            aside_copy(piece).start()

        @pl.when(jnp.logical_not(heavy & (piece < MOVED)))
        def _():
            out_copy(piece).start()

    each_carried(carry)
    each_carried(deliver)

    for which in range(2):
        pair_copy(which).wait_send()

    each_own(lambda target, which: far_copy(target, which).wait_send())
    each_key_source(lambda owner: each_key_relay(
        owner, lambda *at: relay_copy(*at).wait_send()))
    each_value_source(lambda owner: each_value_relay(
        owner, lambda *at: relay_copy(*at).wait_send()))

    @pl.loop(0, chip)
    def _(owner):
        for which in range(2):
            pass_copy(owner, which).wait_send()

    each_carried(settle)

    @pl.loop(0, pieces)
    def _(piece):
        out_copy(piece).wait()


def square_kernel(sections, q_ref, k_ref, v_ref, w_ref, o_ref, held, weight, query, acc, top, attended, projected, aside,
                  far_send, span_recv, pass_send, relay_send, own_sem, query_sem, weight_sem, out_send, out_recv,
                  aside_recv, deliver_send):
    rows, kv_width = k_ref.shape
    heads = kv_width // HEAD_SIZE
    group = q_ref.shape[1] // kv_width
    pieces = weight.shape[0]
    section = lax.axis_index("pipe")
    me = lax.axis_index("ctx")
    chip, core = me // 2, lax.rem(me, 2)
    sibling = chip * 2 + 1 - core
    beside = (chip + 1 - 2 * lax.rem(chip, 2)) * 2 + core
    across = lax.rem(chip + 2, 4) * 2 + core
    opposite = (3 - chip) * 2 + core
    following = lax.rem(section + 1, sections)
    before = lax.rem(section + sections - 1, sections)
    factor = math.log2(math.e) / math.sqrt(HEAD_SIZE)

    barrier = pltpu.get_barrier_semaphore()
    for other in (sibling, beside, across, opposite):
        pl.semaphore_signal(barrier, inc=1, device_id={"ctx": other}, device_id_type=MESH)
    for neighbour in (before, following):
        pl.semaphore_signal(barrier, inc=1, device_id={"pipe": neighbour}, device_id_type=MESH)

    @pl.when(chip > 0)
    def _():
        pl.semaphore_signal(barrier, inc=1, device_id={"pipe": before, "ctx": core}, device_id_type=MESH)

    def lanes(head):
        return slice(head * HEAD_SIZE, (head + 1) * HEAD_SIZE)

    def own_copy(which):
        return pltpu.make_async_copy((k_ref, v_ref)[which], held.at[chip, core, which], own_sem.at[which])

    def query_copy(head):
        wide = group * HEAD_SIZE
        return pltpu.make_async_copy(
            q_ref.at[:, head * wide:(head + 1) * wide], query.at[:, head * wide:(head + 1) * wide], query_sem.at[head])

    def weight_copy(piece):
        return pltpu.make_async_copy(
            w_ref.at[:, pl.ds(pl.multiple_of(piece * COLUMNS, COLUMNS), COLUMNS)],
            weight.at[piece], weight_sem.at[piece])

    for which in range(2):
        own_copy(which).start()
    for head in range(heads):
        query_copy(head).start()

    def at_head(head):
        return pl.ds(pl.multiple_of(head * HEAD_SIZE, HEAD_SIZE), HEAD_SIZE)

    def span_copy(owner, head, side, send_sem, target):
        chunk = held.at[owner, side, :, :, at_head(head)]
        return pltpu.make_async_remote_copy(
            chunk, chunk, send_sem, span_recv.at[owner, side, head], device_id={"ctx": target}, device_id_type=MESH)

    def first_copy(head, way, target):
        return span_copy(chip, head, core, far_send.at[way, head], target)

    def early_copy(head, way, target):
        for which in range(2):
            pltpu.make_async_remote_copy(
                (k_ref, v_ref)[which].at[:, lanes(head)], held.at[chip, core, which, :, lanes(head)],
                far_send.at[way, head], span_recv.at[chip, core, head],
                device_id={"ctx": target}, device_id_type=MESH).start()

    def each_far(act):
        for head in range(heads):
            @pl.when(lax.rem(chip, 2) == 0)
            def _():
                act(head, 1, beside)

            @pl.when(chip < 2)
            def _():
                act(head, 2, across)

        @pl.when(chip == 1)
        def _():
            act(heads - 1, 3, opposite)

    def each_late(act):
        @pl.when(chip == 0)
        def _():
            for head in range(heads // 2, heads):
                act(head, 3, opposite)

    def each_pair(act):
        @pl.when(core == 0)
        def _():
            for head in range(heads):
                act(head, 0, sibling)

    pl.semaphore_wait(barrier, jnp.where(chip == 0, 9, 6))

    each_far(early_copy)
    for which in range(2):
        own_copy(which).wait()
    each_pair(lambda *way: first_copy(*way).start())

    def stacked(head):
        return jnp.concatenate(
            [query[:, at_head(head * group + member)] for member in range(group)], axis=0)

    def block(keys, values, head, first):
        scores = lax.dot_general(
            keys, stacked(head), (((1,), (1,)), ((), ())), preferred_element_type=jnp.float32)
        if first:
            key = lax.broadcasted_iota(jnp.int32, scores.shape, 0)
            row = lax.rem(lax.broadcasted_iota(jnp.int32, scores.shape, 1), rows)
            scores = jnp.where(key <= row, scores, -1e30)
        highest = jnp.max(scores, axis=0, keepdims=True)
        if not first:
            previous = top[head]
            highest = jnp.maximum(previous, highest)
            rescale = jnp.exp2((previous - highest) * factor)
        top[head] = highest
        weights = jnp.exp2((scores - highest) * factor).astype(jnp.bfloat16)
        values = values.T
        values = jnp.concatenate([values, jnp.ones((EXTRA, values.shape[1]), values.dtype)], axis=0)
        summed = jnp.dot(values, weights, preferred_element_type=jnp.float32)
        if first:
            acc[head] = summed
        else:
            acc[head] = acc[head] * rescale + summed

    for head in range(heads):
        query_copy(head).wait()

    @pl.loop(0, pieces)
    def _(piece):
        weight_copy(piece).start()

    for head in range(heads):
        block(held[chip, core, 0, :, lanes(head)], held[chip, core, 1, :, lanes(head)], head, True)

    @pl.when(core == 1)
    def _():
        for head in range(heads):
            span_copy(chip, head, 0, far_send.at[0, head], sibling).wait_recv()
        for head in range(heads):
            block(held[chip, 0, 0, :, lanes(head)], held[chip, 0, 1, :, lanes(head)], head, False)

    steps = chip * heads

    def at(step):
        later = step - 2 * heads
        owner_last = jnp.where(later < 0, 1 + lax.rem(step, 2), 0)
        head_last = jnp.where(later < 0, step // 2, lax.rem(later, 2) * (heads // 2) + later // 2)
        own_third = (step == 0) | ((step > 1) & (lax.rem(step, 2) == 1))
        head_third = jnp.where(step == 1, heads - 1, jnp.where(own_third, step // 2, step // 2 - 1))
        owner = jnp.where(chip == 3, owner_last, jnp.where((chip == 2) & jnp.logical_not(own_third), 1, 0))
        head = jnp.where(chip == 3, head_last, jnp.where(chip == 2, head_third, step))
        return owner, head

    def relayed(owner, head):
        return ((chip == 2) & (owner == 0) & (head < heads // 2)) | ((chip == 3) & (owner == 1) & (head < heads - 1))

    def arrive(step):
        owner, head = at(step)
        span_copy(owner, head, core, pass_send.at[owner, head], sibling).wait_recv()

        @pl.when(relayed(owner, head))
        def _():
            span_copy(owner, head, core, relay_send.at[head], beside).start()

        span_copy(owner, head, core, pass_send.at[owner, head], sibling).start()

    @pl.when(chip > 0)
    def _():
        arrive(0)

    @pl.loop(0, steps)
    def _(step):
        @pl.when(step + 1 < steps)
        def _():
            arrive(step + 1)

        owner, head = at(step)
        span_copy(owner, head, 1 - core, pass_send.at[owner, head], sibling).wait_recv()
        keys = held[owner, :, 0, :, at_head(head)].reshape(2 * rows, HEAD_SIZE)
        values = held[owner, :, 1, :, at_head(head)].reshape(2 * rows, HEAD_SIZE)
        block(keys, values, head, False)

    for head in range(heads):
        for member in range(group):
            part = acc[head, :, member * rows:(member + 1) * rows]
            attended[:, lanes(head * group + member)] = (
                part[:HEAD_SIZE] / part[HEAD_SIZE:HEAD_SIZE + 1]).T.astype(jnp.bfloat16)

    moved, base = 0, 0
    slots = [[], []]
    for side in range(2):
        for origin, counts in reversed(list(enumerate(HANDED_OVER))):
            here = (chip == origin) & (core == side)
            moved = jnp.where(here, counts[side], moved)
            base = jnp.where(here, len(slots[side]), base)
            slots[side] += [(origin, pieces - counts[side] + each) for each in range(counts[side])]
    kept = pieces - moved

    def columns(piece):
        return o_ref.at[:, pl.ds(pl.multiple_of(piece * COLUMNS, COLUMNS), COLUMNS)]

    def out_copy(piece):
        return pltpu.make_async_remote_copy(
            projected.at[piece], columns(piece), out_send.at[piece], out_recv.at[piece],
            device_id={"pipe": following}, device_id_type=MESH)

    def aside_copy(piece):
        slot = base + piece - kept
        return pltpu.make_async_remote_copy(
            projected.at[piece], aside.at[slot], out_send.at[piece], aside_recv.at[slot],
            device_id={"ctx": core}, device_id_type=MESH)

    def deliver_copy(slot, origin, piece):
        return pltpu.make_async_remote_copy(
            aside.at[slot], columns(piece), deliver_send.at[slot], out_recv.at[piece],
            device_id={"pipe": following, "ctx": origin * 2 + core}, device_id_type=MESH)

    def each_delivered(act):
        for side in range(2):
            @pl.when((chip == 0) & (core == side))
            def _():
                for slot, place in enumerate(slots[side]):
                    act(slot, *place)

    def deliver(slot, origin, piece):
        pltpu.make_async_remote_copy(
            aside.at[slot], aside.at[slot], deliver_send.at[slot], aside_recv.at[slot],
            device_id={"ctx": sibling}, device_id_type=MESH).wait_recv()
        deliver_copy(slot, origin, piece).start()

    @pl.loop(0, pieces)
    def _(piece):
        weight_copy(piece).wait()
        projected[piece] = jnp.dot(
            attended[...], weight[piece], preferred_element_type=jnp.float32).astype(jnp.bfloat16)

        @pl.when(piece < kept)
        def _():
            out_copy(piece).start()

        @pl.when(piece >= kept)
        def _():
            aside_copy(piece).start()

    each_late(early_copy)

    each_delivered(deliver)

    each_far(lambda *way: first_copy(*way).wait_send())
    each_late(lambda *way: first_copy(*way).wait_send())
    each_pair(lambda *way: first_copy(*way).wait_send())

    @pl.loop(0, steps)
    def _(step):
        owner, head = at(step)
        span_copy(owner, head, core, pass_send.at[owner, head], sibling).wait_send()

        @pl.when(relayed(owner, head))
        def _():
            span_copy(owner, head, core, relay_send.at[head], beside).wait_send()

    each_delivered(lambda *place: deliver_copy(*place).wait_send())

    @pl.loop(0, pieces)
    def _(piece):
        out_copy(piece).wait()


def general_device(sections, spans, queries, keys, values, out_weight):
    rows, q_width = queries.shape[1:]
    kv_width = keys.shape[2]
    width = out_weight.shape[2]
    heads = kv_width // HEAD_SIZE
    stack = q_width // kv_width * rows
    pieces = width // COLUMNS
    chips = spans // 2
    across = math.isqrt(chips)
    across = across if chips % across == 0 else chips
    hbm = pl.BlockSpec(memory_space=pltpu.HBM)
    handed = pl.pallas_call(
        functools.partial(general_kernel, sections, spans, across),
        out_shape=jax.ShapeDtypeStruct((rows, width), jnp.bfloat16),
        in_specs=[hbm] * 4,
        out_specs=pl.BlockSpec(memory_space=pl.ANY),
        scratch_shapes=[
            pltpu.VMEM((chips, 2, 2 * rows, kv_width), jnp.bfloat16),
            pltpu.VMEM((pieces, q_width, COLUMNS), jnp.bfloat16),
            pltpu.VMEM((heads, stack, HEAD_SIZE), jnp.bfloat16),
            pltpu.VMEM((heads, HEAD_SIZE + EXTRA, stack), jnp.float32),
            pltpu.VMEM((heads, 1, stack), jnp.float32),
            pltpu.VMEM((rows, q_width), jnp.bfloat16),
            pltpu.VMEM((pieces, rows, COLUMNS), jnp.bfloat16),
            pltpu.SemaphoreType.DMA((2,)),
            pltpu.SemaphoreType.DMA((chips, 2)),
            pltpu.SemaphoreType.DMA((chips, 2)),
            pltpu.SemaphoreType.DMA((chips, chips)),
            pltpu.SemaphoreType.DMA((chips, 2, 2)),
            pltpu.SemaphoreType.DMA((pieces,)),
            pltpu.SemaphoreType.DMA((pieces,)),
            pltpu.SemaphoreType.DMA((pieces,)),
            pltpu.SemaphoreType.DMA((2,)),
            pltpu.SemaphoreType.DMA((q_width // HEAD_SIZE,)),
            pltpu.VMEM((2, MOVED, rows, COLUMNS), jnp.bfloat16),
            pltpu.VMEM((2, MOVED, rows, COLUMNS), jnp.bfloat16),
            pltpu.SemaphoreType.DMA((2, MOVED)),
            pltpu.SemaphoreType.DMA((2, MOVED)),
            pltpu.SemaphoreType.DMA((2, MOVED)),
            pltpu.SemaphoreType.DMA((2, MOVED)),
        ],
        compiler_params=pltpu.CompilerParams(
            collective_id=0, has_side_effects=True, vmem_limit_bytes=VMEM_LIMIT),
    )(*(pltpu.with_memory_space_constraint(each[0], pltpu.HBM) for each in (queries, keys, values, out_weight)))
    return handed[None]


def square_device(sections, queries, keys, values, out_weight):
    rows, q_width = queries.shape[1:]
    kv_width = keys.shape[2]
    width = out_weight.shape[2]
    heads = kv_width // HEAD_SIZE
    stack = q_width // kv_width * rows
    pieces = width // COLUMNS
    slots = max(sum(counts[side] for counts in HANDED_OVER) for side in range(2))
    hbm = pl.BlockSpec(memory_space=pltpu.HBM)
    handed = pl.pallas_call(
        functools.partial(square_kernel, sections),
        out_shape=jax.ShapeDtypeStruct((rows, width), jnp.bfloat16),
        in_specs=[hbm] * 4,
        out_specs=pl.BlockSpec(memory_space=pl.ANY),
        scratch_shapes=[
            pltpu.VMEM((4, 2, 2, rows, kv_width), jnp.bfloat16),
            pltpu.VMEM((pieces, q_width, COLUMNS), jnp.bfloat16),
            pltpu.VMEM((rows, q_width), jnp.bfloat16),
            pltpu.VMEM((heads, HEAD_SIZE + EXTRA, stack), jnp.float32),
            pltpu.VMEM((heads, 1, stack), jnp.float32),
            pltpu.VMEM((rows, q_width), jnp.bfloat16),
            pltpu.VMEM((pieces, rows, COLUMNS), jnp.bfloat16),
            pltpu.VMEM((slots, rows, COLUMNS), jnp.bfloat16),
            pltpu.SemaphoreType.DMA((4, heads)),
            pltpu.SemaphoreType.DMA((4, 2, heads)),
            pltpu.SemaphoreType.DMA((4, heads)),
            pltpu.SemaphoreType.DMA((heads,)),
            pltpu.SemaphoreType.DMA((2,)),
            pltpu.SemaphoreType.DMA((heads,)),
            pltpu.SemaphoreType.DMA((pieces,)),
            pltpu.SemaphoreType.DMA((pieces,)),
            pltpu.SemaphoreType.DMA((pieces,)),
            pltpu.SemaphoreType.DMA((slots,)),
            pltpu.SemaphoreType.DMA((slots,)),
        ],
        compiler_params=pltpu.CompilerParams(
            collective_id=1, has_side_effects=True, vmem_limit_bytes=VMEM_LIMIT),
    )(*(pltpu.with_memory_space_constraint(each[0], pltpu.HBM) for each in (queries, keys, values, out_weight)))
    return handed[None]


def per_device(sections, spans, *operands):
    if spans == 8:
        return square_device(sections, *operands)
    return general_device(sections, spans, *operands)


def solution(mesh):
    placed = (
        P("pipe", "ctx", None),
        P("pipe", "ctx", None),
        P("pipe", "ctx", None),
        P("pipe", None, None),
    )
    return jax.shard_map(
        functools.partial(per_device, mesh.shape["pipe"], mesh.shape["ctx"]),
        mesh=mesh, in_specs=placed, out_specs=P("pipe", "ctx", None), check_vma=False
    )
```

```python
import functools
import math

import jax
import jax.numpy as jnp
from jax import lax
from jax.experimental import pallas as pl
from jax.experimental.pallas import tpu as pltpu
from jax.sharding import PartitionSpec as P

HEAD_SIZE = 128
COLUMNS = 256
MOVED = 2
HANDED_OVER = ((6, 6), (5, 4), (2, 2), (3, 3))
EXTRA = 16
VMEM_LIMIT = 50 * 1024 * 1024
MESH = pl.DeviceIdType.MESH


def general_kernel(sections, spans, across, q_ref, k_ref, v_ref, w_ref, o_ref, held, weight, stacked, acc, top,
           attended, projected, pair_send, far_send, pass_send, relay_send, span_recv, weight_sem, out_send, out_recv, own_sem, query_sem,
           aside, landed, aside_recv, cross_send, cross_recv, final_send):
    rows, kv_width = k_ref.shape
    q_width = q_ref.shape[1]
    heads = kv_width // HEAD_SIZE
    group = q_width // kv_width
    chips = spans // 2
    pieces = weight.shape[0]
    section = lax.axis_index("pipe")
    me = lax.axis_index("ctx")
    chip, core = me // 2, lax.rem(me, 2)
    line, column = chip // across, lax.rem(chip, across)
    lines = chips // across
    following = lax.rem(section + 1, sections)
    before = lax.rem(section + sections - 1, sections)
    factor = math.log2(math.e) / math.sqrt(HEAD_SIZE)

    barrier = pltpu.get_barrier_semaphore()

    @pl.loop(1, spans)
    def _(step):
        pl.semaphore_signal(barrier, inc=1, device_id={"ctx": lax.rem(me + step, spans)}, device_id_type=MESH)

    for neighbour in (before, following):
        pl.semaphore_signal(barrier, inc=1, device_id={"pipe": neighbour}, device_id_type=MESH)

    def weight_copy(piece):
        return pltpu.make_async_copy(
            w_ref.at[:, pl.ds(pl.multiple_of(piece * COLUMNS, COLUMNS), COLUMNS)],
            weight.at[piece], weight_sem.at[piece])

    def place(owner, side, which):
        return held.at[owner, which, pl.ds(pl.multiple_of(side * rows, rows), rows), :]

    def own_copy(which):
        return pltpu.make_async_copy((k_ref, v_ref)[which], place(chip, core, which), own_sem.at[which])

    def query_copy(head, member):
        at = head * group + member
        return pltpu.make_async_copy(
            q_ref.at[:, at * HEAD_SIZE:(at + 1) * HEAD_SIZE],
            stacked.at[head, member * rows:(member + 1) * rows, :], query_sem.at[at])

    for which in range(2):
        own_copy(which).start()
    for head in range(heads):
        for member in range(group):
            query_copy(head, member).start()

    @pl.loop(0, pieces)
    def _(piece):
        weight_copy(piece).start()

    for which in range(2):
        own_copy(which).wait()

    def pair_copy(which):
        return pltpu.make_async_remote_copy(
            place(chip, core, which), place(chip, core, which), pair_send.at[which],
            span_recv.at[chip, core, which], device_id={"ctx": chip * 2 + 1 - core}, device_id_type=MESH)

    def far_copy(target, which):
        return pltpu.make_async_remote_copy(
            place(chip, core, which), place(chip, core, which), far_send.at[target, which],
            span_recv.at[chip, core, which], device_id={"ctx": target * 2 + core}, device_id_type=MESH)

    def pass_copy(owner, which):
        return pltpu.make_async_remote_copy(
            place(owner, core, which), place(owner, core, which), pass_send.at[owner, which],
            span_recv.at[owner, core, which], device_id={"ctx": chip * 2 + 1 - core}, device_id_type=MESH)

    def relay_copy(owner, target, which):
        return pltpu.make_async_remote_copy(
            place(owner, core, which), place(owner, core, which), relay_send.at[owner, target],
            span_recv.at[owner, core, which], device_id={"ctx": target * 2 + core}, device_id_type=MESH)

    def each_own(act):
        @pl.loop(1, across)
        def _(step):
            other = lax.rem(column + step, across)

            @pl.when((line < lines - 1) | (other > column))
            def _():
                act(line * across + other, 0)

        @pl.loop(line + 1, lines)
        def _(other):
            act(other * across + column, 1)
            act(other * across + column, 0)

        @pl.loop(column + 1, across)
        def _(other):
            act(line * across + other, 1)

    def each_key_source(act):
        @pl.when(line < lines - 1)
        def _():
            @pl.loop(1, across)
            def _(step):
                act(line * across + lax.rem(column + step, across))

    def each_key_relay(owner, act):
        @pl.loop(line + 1, lines)
        def _(other):
            act(owner, other * across + column, 0)

    def each_value_source(act):
        @pl.loop(0, line)
        def _(other):
            act(other * across + column)

    def each_value_relay(owner, act):
        @pl.loop(1, across)
        def _(step):
            act(owner, line * across + lax.rem(column + step, across), 1)

    def wait_span(owner, side, which):
        pltpu.make_async_remote_copy(
            place(owner, side, which), place(owner, side, which), pair_send.at[which],
            span_recv.at[owner, side, which], device_id={"ctx": chip * 2 + 1 - core}, device_id_type=MESH).wait_recv()

    pl.semaphore_wait(barrier, spans + 1)
    for which in range(2):
        pair_copy(which).start()

    each_own(lambda target, which: far_copy(target, which).start())

    for head in range(heads):
        for member in range(group):
            query_copy(head, member).wait()

    def block(owner, head, first):
        lanes = slice(head * HEAD_SIZE, (head + 1) * HEAD_SIZE)
        scores = lax.dot_general(
            held[owner, 0, :, lanes], stacked[head], (((1,), (1,)), ((), ())),
            preferred_element_type=jnp.float32)
        if first:
            key = lax.broadcasted_iota(jnp.int32, scores.shape, 0)
            row = lax.rem(lax.broadcasted_iota(jnp.int32, scores.shape, 1), rows) + core * rows
            scores = jnp.where(key <= row, scores, -1e30)
        highest = jnp.max(scores, axis=0, keepdims=True)
        if not first:
            previous = top[head]
            highest = jnp.maximum(previous, highest)
            rescale = jnp.exp2((previous - highest) * factor)
        top[head] = highest
        weights = jnp.exp2((scores - highest) * factor).astype(jnp.bfloat16)
        values = held[owner, 1, :, lanes].T
        values = jnp.concatenate([values, jnp.ones((EXTRA, values.shape[1]), values.dtype)], axis=0)
        summed = jnp.dot(values, weights, preferred_element_type=jnp.float32)
        if first:
            acc[head] = summed
        else:
            acc[head] = acc[head] * rescale + summed

    for which in range(2):
        wait_span(chip, 1 - core, which)

    for head in range(heads):
        block(chip, head, True)

    def relay_keys(owner):
        wait_span(owner, core, 0)
        each_key_relay(owner, lambda *at: relay_copy(*at).start())

        @pl.when(owner < chip)
        def _():
            pass_copy(owner, 0).start()

    def relay_values(owner):
        wait_span(owner, core, 1)
        each_value_relay(owner, lambda *at: relay_copy(*at).start())
        pass_copy(owner, 1).start()

    each_value_source(relay_values)
    each_key_source(relay_keys)

    @pl.loop(0, chip)
    def _(step):
        owner = chip - 1 - step

        @pl.when((owner // across != line) | (line == lines - 1))
        def _():
            wait_span(owner, core, 0)
            pass_copy(owner, 0).start()

        @pl.when((lax.rem(owner, across) != column) | (owner // across == line))
        def _():
            wait_span(owner, core, 1)
            pass_copy(owner, 1).start()

        for which in range(2):
            wait_span(owner, 1 - core, which)

        for head in range(heads):
            block(owner, head, False)

    for head in range(heads):
        for member in range(group):
            part = acc[head, :, member * rows:(member + 1) * rows]
            attended[:, (head * group + member) * HEAD_SIZE:(head * group + member + 1) * HEAD_SIZE] = (
                part[:HEAD_SIZE] / part[HEAD_SIZE:HEAD_SIZE + 1]).T.astype(jnp.bfloat16)

    def out_copy(piece):
        return pltpu.make_async_remote_copy(
            projected.at[piece],
            o_ref.at[:, pl.ds(pl.multiple_of(piece * COLUMNS, COLUMNS), COLUMNS)],
            out_send.at[piece], out_recv.at[piece], device_id={"pipe": following}, device_id_type=MESH)

    late = chips - chips // 2
    heavy = chip >= late
    slot_of = lax.rem(chip + 2 * chips - late, 2)

    def aside_copy(piece):
        return pltpu.make_async_remote_copy(
            projected.at[piece], aside.at[slot_of, piece], out_send.at[piece],
            aside_recv.at[slot_of, piece],
            device_id={"ctx": (chip - late) // 2 * 2 + core}, device_id_type=MESH)

    def cross_copy(slot, piece):
        return pltpu.make_async_remote_copy(
            aside.at[slot, piece], landed.at[slot, piece], cross_send.at[slot, piece],
            cross_recv.at[slot, piece], device_id={"pipe": following}, device_id_type=MESH)

    def final_copy(slot, piece):
        return pltpu.make_async_remote_copy(
            landed.at[slot, piece],
            o_ref.at[:, pl.ds(pl.multiple_of(piece * COLUMNS, COLUMNS), COLUMNS)],
            final_send.at[slot, piece], out_recv.at[piece],
            device_id={"ctx": (late + chip * 2 + slot) * 2 + core}, device_id_type=MESH)

    def each_carried(act):
        @pl.loop(0, jnp.clip(chips // 2 - chip * 2, 0, 2))
        def _(slot):
            @pl.loop(0, MOVED)
            def _(piece):
                act(slot, piece)

    def carry(slot, piece):
        pltpu.make_async_remote_copy(
            aside.at[slot, piece], aside.at[slot, piece], cross_send.at[slot, piece],
            aside_recv.at[slot, piece], device_id={"pipe": following}, device_id_type=MESH).wait_recv()
        cross_copy(slot, piece).start()

    def deliver(slot, piece):
        cross_copy(slot, piece).wait_recv()
        final_copy(slot, piece).start()

    def settle(slot, piece):
        cross_copy(slot, piece).wait_send()
        final_copy(slot, piece).wait_send()

    @pl.loop(0, pieces)
    def _(piece):
        weight_copy(piece).wait()
        projected[piece] = jnp.dot(
            attended[...], weight[piece], preferred_element_type=jnp.float32).astype(jnp.bfloat16)

        @pl.when(heavy & (piece < MOVED))
        def _():
            aside_copy(piece).start()

        @pl.when(jnp.logical_not(heavy & (piece < MOVED)))
        def _():
            out_copy(piece).start()

    each_carried(carry)
    each_carried(deliver)

    for which in range(2):
        pair_copy(which).wait_send()

    each_own(lambda target, which: far_copy(target, which).wait_send())
    each_key_source(lambda owner: each_key_relay(
        owner, lambda *at: relay_copy(*at).wait_send()))
    each_value_source(lambda owner: each_value_relay(
        owner, lambda *at: relay_copy(*at).wait_send()))

    @pl.loop(0, chip)
    def _(owner):
        for which in range(2):
            pass_copy(owner, which).wait_send()

    each_carried(settle)

    @pl.loop(0, pieces)
    def _(piece):
        out_copy(piece).wait()


def square_kernel(sections, q_ref, k_ref, v_ref, w_ref, o_ref, held, weight, query, acc, top, attended, projected, aside,
                  far_send, span_recv, pass_send, relay_send, own_sem, query_sem, weight_sem, out_send, out_recv,
                  aside_recv, deliver_send):
    rows, kv_width = k_ref.shape
    heads = kv_width // HEAD_SIZE
    group = q_ref.shape[1] // kv_width
    pieces = weight.shape[0]
    section = lax.axis_index("pipe")
    me = lax.axis_index("ctx")
    chip, core = me // 2, lax.rem(me, 2)
    sibling = chip * 2 + 1 - core
    beside = (chip + 1 - 2 * lax.rem(chip, 2)) * 2 + core
    across = lax.rem(chip + 2, 4) * 2 + core
    opposite = (3 - chip) * 2 + core
    following = lax.rem(section + 1, sections)
    before = lax.rem(section + sections - 1, sections)
    factor = math.log2(math.e) / math.sqrt(HEAD_SIZE)

    barrier = pltpu.get_barrier_semaphore()
    for other in (sibling, beside, across, opposite):
        pl.semaphore_signal(barrier, inc=1, device_id={"ctx": other}, device_id_type=MESH)
    for neighbour in (before, following):
        pl.semaphore_signal(barrier, inc=1, device_id={"pipe": neighbour}, device_id_type=MESH)

    pl.semaphore_signal(
        barrier, inc=1, device_id={"pipe": before, "ctx": jnp.where(chip > 0, core, 2 + core)}, device_id_type=MESH)

    def lanes(head):
        return slice(head * HEAD_SIZE, (head + 1) * HEAD_SIZE)

    def own_copy(which):
        return pltpu.make_async_copy((k_ref, v_ref)[which], held.at[chip, core, which], own_sem.at[which])

    def query_copy(head):
        wide = group * HEAD_SIZE
        return pltpu.make_async_copy(
            q_ref.at[:, head * wide:(head + 1) * wide], query.at[:, head * wide:(head + 1) * wide], query_sem.at[head])

    def weight_copy(piece):
        return pltpu.make_async_copy(
            w_ref.at[:, pl.ds(pl.multiple_of(piece * COLUMNS, COLUMNS), COLUMNS)],
            weight.at[piece], weight_sem.at[piece])

    for which in range(2):
        own_copy(which).start()
    for head in range(heads):
        query_copy(head).start()

    def at_head(head):
        return pl.ds(pl.multiple_of(head * HEAD_SIZE, HEAD_SIZE), HEAD_SIZE)

    def span_copy(owner, head, side, send_sem, target):
        chunk = held.at[owner, side, :, :, at_head(head)]
        return pltpu.make_async_remote_copy(
            chunk, chunk, send_sem, span_recv.at[owner, side, head], device_id={"ctx": target}, device_id_type=MESH)

    def first_copy(head, way, target):
        return span_copy(chip, head, core, far_send.at[way, head], target)

    def early_copy(head, way, target):
        for which in range(2):
            pltpu.make_async_remote_copy(
                (k_ref, v_ref)[which].at[:, lanes(head)], held.at[chip, core, which, :, lanes(head)],
                far_send.at[way, head], span_recv.at[chip, core, head],
                device_id={"ctx": target}, device_id_type=MESH).start()

    def each_far(act):
        for step in range(heads):
            head = (step + heads // 2) % heads

            @pl.when((chip == 2) | ((chip == 0) & (step < heads // 2)))
            def _():
                act(step, 1, beside)

            @pl.when(chip == 0)
            def _():
                act(head, 2, across)

            @pl.when(chip == 1)
            def _():
                act(step, 2, across)

        @pl.when(chip == 1)
        def _():
            act(heads - 1, 3, opposite)

    def each_pair(act):
        @pl.when(core == 0)
        def _():
            for head in range(heads):
                act(head, 0, sibling)

    pl.semaphore_wait(barrier, jnp.where(chip == 0, 9, jnp.where(chip == 1, 7, 6)))

    each_far(early_copy)
    for which in range(2):
        own_copy(which).wait()
    each_pair(lambda *way: first_copy(*way).start())

    def stacked(head):
        return jnp.concatenate(
            [query[:, at_head(head * group + member)] for member in range(group)], axis=0)

    def block(keys, values, head, first):
        scores = lax.dot_general(
            keys, stacked(head), (((1,), (1,)), ((), ())), preferred_element_type=jnp.float32)
        if first:
            key = lax.broadcasted_iota(jnp.int32, scores.shape, 0)
            row = lax.rem(lax.broadcasted_iota(jnp.int32, scores.shape, 1), rows)
            scores = jnp.where(key <= row, scores, -1e30)
        highest = jnp.max(scores, axis=0, keepdims=True)
        if not first:
            previous = top[head]
            highest = jnp.maximum(previous, highest)
            rescale = jnp.exp2((previous - highest) * factor)
        top[head] = highest
        weights = jnp.exp2((scores - highest) * factor).astype(jnp.bfloat16)
        values = values.T
        values = jnp.concatenate([values, jnp.ones((EXTRA, values.shape[1]), values.dtype)], axis=0)
        summed = jnp.dot(values, weights, preferred_element_type=jnp.float32)
        if first:
            acc[head] = summed
        else:
            acc[head] = acc[head] * rescale + summed

    for head in range(heads):
        query_copy(head).wait()

    @pl.loop(0, pieces)
    def _(piece):
        weight_copy(piece).start()

    for head in range(heads):
        block(held[chip, core, 0, :, lanes(head)], held[chip, core, 1, :, lanes(head)], head, True)

    @pl.when(core == 1)
    def _():
        for head in range(heads):
            span_copy(chip, head, 0, far_send.at[0, head], sibling).wait_recv()
        for head in range(heads):
            block(held[chip, 0, 0, :, lanes(head)], held[chip, 0, 1, :, lanes(head)], head, False)

    moved, base = 0, 0
    slots = [[], []]
    for side in range(2):
        for origin in (0, 2, 3, 1):
            count = HANDED_OVER[origin][side]
            here = (chip == origin) & (core == side)
            moved = jnp.where(here, count, moved)
            if origin > 0:
                base = jnp.where(here, len(slots[side]), base)
                slots[side] += [(origin, 2 * each + 1) for each in range(count)]
    fed = jnp.where(chip == 1, jnp.where(core == 0, *HANDED_OVER[0]), 0)

    def columns(piece):
        return o_ref.at[:, pl.ds(pl.multiple_of(piece * COLUMNS, COLUMNS), COLUMNS)]

    def out_copy(piece):
        return pltpu.make_async_remote_copy(
            projected.at[piece], columns(piece), out_send.at[piece], out_recv.at[piece],
            device_id={"pipe": following}, device_id_type=MESH)

    def aside_copy(piece):
        slot = base + piece // 2
        return pltpu.make_async_remote_copy(
            projected.at[piece], aside.at[slot], out_send.at[piece], aside_recv.at[slot],
            device_id={"ctx": jnp.where(chip == 0, 2 + core, core)}, device_id_type=MESH)

    def deliver_copy(slot, origin, piece):
        return pltpu.make_async_remote_copy(
            aside.at[slot], columns(piece), deliver_send.at[slot], out_recv.at[piece],
            device_id={"pipe": following, "ctx": origin * 2 + core}, device_id_type=MESH)

    def each_delivered(act):
        for side in range(2):
            @pl.when((chip == 0) & (core == side))
            def _():
                for slot, place in enumerate(slots[side]):
                    act(slot, *place)

    def deliver(slot, origin, piece):
        pltpu.make_async_remote_copy(
            aside.at[slot], aside.at[slot], deliver_send.at[slot], aside_recv.at[slot],
            device_id={"ctx": sibling}, device_id_type=MESH).wait_recv()
        deliver_copy(slot, origin, piece).start()

    def forward(slot):
        deliver(slot, 0, 2 * slot + 1)

    steps = chip * heads

    def at(step):
        later = step - 2 * heads
        owner_last = jnp.where(later < 0, 1 + lax.rem(step, 2), 0)
        head_last = jnp.where(later < 0, step // 2, (1 - lax.rem(later, 2)) * (heads // 2) + later // 2)
        own_third = (step == 0) | ((step > 1) & (lax.rem(step, 2) == 1))
        head_third = jnp.where(step == 1, heads - 1, jnp.where(own_third, lax.rem(step // 2 + heads // 2, heads), step // 2 - 1))
        owner = jnp.where(chip == 3, owner_last, jnp.where((chip == 2) & jnp.logical_not(own_third), 1, 0))
        head = jnp.where(chip == 3, head_last, jnp.where(chip == 2, head_third, step))
        return owner, head

    def relayed(owner, head):
        late = head >= heads // 2
        last = ((owner == 1) & (head < heads - 1)) | ((owner == 0) & late)
        return ((chip == 1) & jnp.logical_not(late)) | ((chip == 2) & (owner == 0) & late) | ((chip == 3) & last)

    def relay_copy(owner, head):
        target = jnp.where((chip == 1) | ((chip == 3) & (owner == 0)), across, beside)
        return span_copy(owner, head, core, relay_send.at[owner, head], target)

    def arrive(step):
        owner, head = at(step)
        span_copy(owner, head, core, pass_send.at[owner, head], sibling).wait_recv()

        @pl.when(relayed(owner, head))
        def _():
            relay_copy(owner, head).start()

        span_copy(owner, head, core, pass_send.at[owner, head], sibling).start()

    @pl.when(chip > 0)
    def _():
        arrive(0)

    @pl.loop(0, steps)
    def _(step):
        @pl.when((step + 1 < steps) & ((chip > 1) | (step == 0)))
        def _():
            arrive(step + 1)

        owner, head = at(step)
        span_copy(owner, head, 1 - core, pass_send.at[owner, head], sibling).wait_recv()
        keys = held[owner, :, 0, :, at_head(head)].reshape(2 * rows, HEAD_SIZE)
        values = held[owner, :, 1, :, at_head(head)].reshape(2 * rows, HEAD_SIZE)
        block(keys, values, head, False)

        @pl.when((chip == 1) & (step == 1))
        def _():
            @pl.loop(0, fed - 1)
            def _(slot):
                forward(slot)

            arrive(step + 1)
            forward(fed - 1)
            arrive(step + 2)

    for head in range(heads):
        for member in range(group):
            part = acc[head, :, member * rows:(member + 1) * rows]
            attended[:, lanes(head * group + member)] = (
                part[:HEAD_SIZE] / part[HEAD_SIZE:HEAD_SIZE + 1]).T.astype(jnp.bfloat16)

    @pl.loop(0, pieces)
    def _(piece):
        weight_copy(piece).wait()
        projected[piece] = jnp.dot(
            attended[...], weight[piece], preferred_element_type=jnp.float32).astype(jnp.bfloat16)

        handed = (lax.rem(piece, 2) == 1) & (piece < 2 * moved)

        @pl.when(jnp.logical_not(handed))
        def _():
            out_copy(piece).start()

        @pl.when(handed)
        def _():
            aside_copy(piece).start()

    each_delivered(deliver)

    each_far(lambda *way: first_copy(*way).wait_send())
    each_pair(lambda *way: first_copy(*way).wait_send())

    @pl.loop(0, steps)
    def _(step):
        owner, head = at(step)
        span_copy(owner, head, core, pass_send.at[owner, head], sibling).wait_send()

        @pl.when(relayed(owner, head))
        def _():
            relay_copy(owner, head).wait_send()

    each_delivered(lambda *place: deliver_copy(*place).wait_send())

    @pl.loop(0, fed)
    def _(slot):
        deliver_copy(slot, 0, 2 * slot + 1).wait_send()

    @pl.loop(0, pieces)
    def _(piece):
        out_copy(piece).wait()


def general_device(sections, spans, queries, keys, values, out_weight):
    rows, q_width = queries.shape[1:]
    kv_width = keys.shape[2]
    width = out_weight.shape[2]
    heads = kv_width // HEAD_SIZE
    stack = q_width // kv_width * rows
    pieces = width // COLUMNS
    chips = spans // 2
    across = math.isqrt(chips)
    across = across if chips % across == 0 else chips
    hbm = pl.BlockSpec(memory_space=pltpu.HBM)
    handed = pl.pallas_call(
        functools.partial(general_kernel, sections, spans, across),
        out_shape=jax.ShapeDtypeStruct((rows, width), jnp.bfloat16),
        in_specs=[hbm] * 4,
        out_specs=pl.BlockSpec(memory_space=pl.ANY),
        scratch_shapes=[
            pltpu.VMEM((chips, 2, 2 * rows, kv_width), jnp.bfloat16),
            pltpu.VMEM((pieces, q_width, COLUMNS), jnp.bfloat16),
            pltpu.VMEM((heads, stack, HEAD_SIZE), jnp.bfloat16),
            pltpu.VMEM((heads, HEAD_SIZE + EXTRA, stack), jnp.float32),
            pltpu.VMEM((heads, 1, stack), jnp.float32),
            pltpu.VMEM((rows, q_width), jnp.bfloat16),
            pltpu.VMEM((pieces, rows, COLUMNS), jnp.bfloat16),
            pltpu.SemaphoreType.DMA((2,)),
            pltpu.SemaphoreType.DMA((chips, 2)),
            pltpu.SemaphoreType.DMA((chips, 2)),
            pltpu.SemaphoreType.DMA((chips, chips)),
            pltpu.SemaphoreType.DMA((chips, 2, 2)),
            pltpu.SemaphoreType.DMA((pieces,)),
            pltpu.SemaphoreType.DMA((pieces,)),
            pltpu.SemaphoreType.DMA((pieces,)),
            pltpu.SemaphoreType.DMA((2,)),
            pltpu.SemaphoreType.DMA((q_width // HEAD_SIZE,)),
            pltpu.VMEM((2, MOVED, rows, COLUMNS), jnp.bfloat16),
            pltpu.VMEM((2, MOVED, rows, COLUMNS), jnp.bfloat16),
            pltpu.SemaphoreType.DMA((2, MOVED)),
            pltpu.SemaphoreType.DMA((2, MOVED)),
            pltpu.SemaphoreType.DMA((2, MOVED)),
            pltpu.SemaphoreType.DMA((2, MOVED)),
        ],
        compiler_params=pltpu.CompilerParams(
            collective_id=0, has_side_effects=True, vmem_limit_bytes=VMEM_LIMIT),
    )(*(pltpu.with_memory_space_constraint(each[0], pltpu.HBM) for each in (queries, keys, values, out_weight)))
    return handed[None]


def square_device(sections, queries, keys, values, out_weight):
    rows, q_width = queries.shape[1:]
    kv_width = keys.shape[2]
    width = out_weight.shape[2]
    heads = kv_width // HEAD_SIZE
    stack = q_width // kv_width * rows
    pieces = width // COLUMNS
    slots = max(max(HANDED_OVER[0]), *(sum(counts[side] for counts in HANDED_OVER[1:]) for side in range(2)))
    hbm = pl.BlockSpec(memory_space=pltpu.HBM)
    handed = pl.pallas_call(
        functools.partial(square_kernel, sections),
        out_shape=jax.ShapeDtypeStruct((rows, width), jnp.bfloat16),
        in_specs=[hbm] * 4,
        out_specs=pl.BlockSpec(memory_space=pl.ANY),
        scratch_shapes=[
            pltpu.VMEM((4, 2, 2, rows, kv_width), jnp.bfloat16),
            pltpu.VMEM((pieces, q_width, COLUMNS), jnp.bfloat16),
            pltpu.VMEM((rows, q_width), jnp.bfloat16),
            pltpu.VMEM((heads, HEAD_SIZE + EXTRA, stack), jnp.float32),
            pltpu.VMEM((heads, 1, stack), jnp.float32),
            pltpu.VMEM((rows, q_width), jnp.bfloat16),
            pltpu.VMEM((pieces, rows, COLUMNS), jnp.bfloat16),
            pltpu.VMEM((slots, rows, COLUMNS), jnp.bfloat16),
            pltpu.SemaphoreType.DMA((4, heads)),
            pltpu.SemaphoreType.DMA((4, 2, heads)),
            pltpu.SemaphoreType.DMA((4, heads)),
            pltpu.SemaphoreType.DMA((2, heads)),
            pltpu.SemaphoreType.DMA((2,)),
            pltpu.SemaphoreType.DMA((heads,)),
            pltpu.SemaphoreType.DMA((pieces,)),
            pltpu.SemaphoreType.DMA((pieces,)),
            pltpu.SemaphoreType.DMA((pieces,)),
            pltpu.SemaphoreType.DMA((slots,)),
            pltpu.SemaphoreType.DMA((slots,)),
        ],
        compiler_params=pltpu.CompilerParams(
            collective_id=1, has_side_effects=True, vmem_limit_bytes=VMEM_LIMIT),
    )(*(pltpu.with_memory_space_constraint(each[0], pltpu.HBM) for each in (queries, keys, values, out_weight)))
    return handed[None]


def per_device(sections, spans, *operands):
    if spans == 8:
        return square_device(sections, *operands)
    return general_device(sections, spans, *operands)


def solution(mesh):
    placed = (
        P("pipe", "ctx", None),
        P("pipe", "ctx", None),
        P("pipe", "ctx", None),
        P("pipe", None, None),
    )
    return jax.shard_map(
        functools.partial(per_device, mesh.shape["pipe"], mesh.shape["ctx"]),
        mesh=mesh, in_specs=placed, out_specs=P("pipe", "ctx", None), check_vma=False
    )
```

```python
import functools
import math

import jax
import jax.numpy as jnp
from jax import lax
from jax.experimental import pallas as pl
from jax.experimental.pallas import tpu as pltpu
from jax.sharding import PartitionSpec as P

HEAD_SIZE = 128
COLUMNS = 256
MOVED = 2
HANDED_OVER = ((6, 6), (5, 4), (2, 2), (3, 3))
EXTRA = 16
VMEM_LIMIT = 50 * 1024 * 1024
MESH = pl.DeviceIdType.MESH


def general_kernel(sections, spans, across, q_ref, k_ref, v_ref, w_ref, o_ref, held, weight, stacked, acc, top,
           attended, projected, pair_send, far_send, pass_send, relay_send, span_recv, weight_sem, out_send, out_recv, own_sem, query_sem,
           aside, landed, aside_recv, cross_send, cross_recv, final_send):
    rows, kv_width = k_ref.shape
    q_width = q_ref.shape[1]
    heads = kv_width // HEAD_SIZE
    group = q_width // kv_width
    chips = spans // 2
    pieces = weight.shape[0]
    section = lax.axis_index("pipe")
    me = lax.axis_index("ctx")
    chip, core = me // 2, lax.rem(me, 2)
    line, column = chip // across, lax.rem(chip, across)
    lines = chips // across
    following = lax.rem(section + 1, sections)
    before = lax.rem(section + sections - 1, sections)
    factor = math.log2(math.e) / math.sqrt(HEAD_SIZE)

    barrier = pltpu.get_barrier_semaphore()

    @pl.loop(1, spans)
    def _(step):
        pl.semaphore_signal(barrier, inc=1, device_id={"ctx": lax.rem(me + step, spans)}, device_id_type=MESH)

    for neighbour in (before, following):
        pl.semaphore_signal(barrier, inc=1, device_id={"pipe": neighbour}, device_id_type=MESH)

    def weight_copy(piece):
        return pltpu.make_async_copy(
            w_ref.at[:, pl.ds(pl.multiple_of(piece * COLUMNS, COLUMNS), COLUMNS)],
            weight.at[piece], weight_sem.at[piece])

    def place(owner, side, which):
        return held.at[owner, which, pl.ds(pl.multiple_of(side * rows, rows), rows), :]

    def own_copy(which):
        return pltpu.make_async_copy((k_ref, v_ref)[which], place(chip, core, which), own_sem.at[which])

    def query_copy(head, member):
        at = head * group + member
        return pltpu.make_async_copy(
            q_ref.at[:, at * HEAD_SIZE:(at + 1) * HEAD_SIZE],
            stacked.at[head, member * rows:(member + 1) * rows, :], query_sem.at[at])

    for which in range(2):
        own_copy(which).start()
    for head in range(heads):
        for member in range(group):
            query_copy(head, member).start()

    @pl.loop(0, pieces)
    def _(piece):
        weight_copy(piece).start()

    for which in range(2):
        own_copy(which).wait()

    def pair_copy(which):
        return pltpu.make_async_remote_copy(
            place(chip, core, which), place(chip, core, which), pair_send.at[which],
            span_recv.at[chip, core, which], device_id={"ctx": chip * 2 + 1 - core}, device_id_type=MESH)

    def far_copy(target, which):
        return pltpu.make_async_remote_copy(
            place(chip, core, which), place(chip, core, which), far_send.at[target, which],
            span_recv.at[chip, core, which], device_id={"ctx": target * 2 + core}, device_id_type=MESH)

    def pass_copy(owner, which):
        return pltpu.make_async_remote_copy(
            place(owner, core, which), place(owner, core, which), pass_send.at[owner, which],
            span_recv.at[owner, core, which], device_id={"ctx": chip * 2 + 1 - core}, device_id_type=MESH)

    def relay_copy(owner, target, which):
        return pltpu.make_async_remote_copy(
            place(owner, core, which), place(owner, core, which), relay_send.at[owner, target],
            span_recv.at[owner, core, which], device_id={"ctx": target * 2 + core}, device_id_type=MESH)

    def each_own(act):
        @pl.loop(1, across)
        def _(step):
            other = lax.rem(column + step, across)

            @pl.when((line < lines - 1) | (other > column))
            def _():
                act(line * across + other, 0)

        @pl.loop(line + 1, lines)
        def _(other):
            act(other * across + column, 1)
            act(other * across + column, 0)

        @pl.loop(column + 1, across)
        def _(other):
            act(line * across + other, 1)

    def each_key_source(act):
        @pl.when(line < lines - 1)
        def _():
            @pl.loop(1, across)
            def _(step):
                act(line * across + lax.rem(column + step, across))

    def each_key_relay(owner, act):
        @pl.loop(line + 1, lines)
        def _(other):
            act(owner, other * across + column, 0)

    def each_value_source(act):
        @pl.loop(0, line)
        def _(other):
            act(other * across + column)

    def each_value_relay(owner, act):
        @pl.loop(1, across)
        def _(step):
            act(owner, line * across + lax.rem(column + step, across), 1)

    def wait_span(owner, side, which):
        pltpu.make_async_remote_copy(
            place(owner, side, which), place(owner, side, which), pair_send.at[which],
            span_recv.at[owner, side, which], device_id={"ctx": chip * 2 + 1 - core}, device_id_type=MESH).wait_recv()

    pl.semaphore_wait(barrier, spans + 1)
    for which in range(2):
        pair_copy(which).start()

    each_own(lambda target, which: far_copy(target, which).start())

    for head in range(heads):
        for member in range(group):
            query_copy(head, member).wait()

    def block(owner, head, first):
        lanes = slice(head * HEAD_SIZE, (head + 1) * HEAD_SIZE)
        scores = lax.dot_general(
            held[owner, 0, :, lanes], stacked[head], (((1,), (1,)), ((), ())),
            preferred_element_type=jnp.float32)
        if first:
            key = lax.broadcasted_iota(jnp.int32, scores.shape, 0)
            row = lax.rem(lax.broadcasted_iota(jnp.int32, scores.shape, 1), rows) + core * rows
            scores = jnp.where(key <= row, scores, -1e30)
        highest = jnp.max(scores, axis=0, keepdims=True)
        if not first:
            previous = top[head]
            highest = jnp.maximum(previous, highest)
            rescale = jnp.exp2((previous - highest) * factor)
        top[head] = highest
        weights = jnp.exp2((scores - highest) * factor).astype(jnp.bfloat16)
        values = held[owner, 1, :, lanes].T
        values = jnp.concatenate([values, jnp.ones((EXTRA, values.shape[1]), values.dtype)], axis=0)
        summed = jnp.dot(values, weights, preferred_element_type=jnp.float32)
        if first:
            acc[head] = summed
        else:
            acc[head] = acc[head] * rescale + summed

    for which in range(2):
        wait_span(chip, 1 - core, which)

    for head in range(heads):
        block(chip, head, True)

    def relay_keys(owner):
        wait_span(owner, core, 0)
        each_key_relay(owner, lambda *at: relay_copy(*at).start())

        @pl.when(owner < chip)
        def _():
            pass_copy(owner, 0).start()

    def relay_values(owner):
        wait_span(owner, core, 1)
        each_value_relay(owner, lambda *at: relay_copy(*at).start())
        pass_copy(owner, 1).start()

    each_value_source(relay_values)
    each_key_source(relay_keys)

    @pl.loop(0, chip)
    def _(step):
        owner = chip - 1 - step

        @pl.when((owner // across != line) | (line == lines - 1))
        def _():
            wait_span(owner, core, 0)
            pass_copy(owner, 0).start()

        @pl.when((lax.rem(owner, across) != column) | (owner // across == line))
        def _():
            wait_span(owner, core, 1)
            pass_copy(owner, 1).start()

        for which in range(2):
            wait_span(owner, 1 - core, which)

        for head in range(heads):
            block(owner, head, False)

    for head in range(heads):
        for member in range(group):
            part = acc[head, :, member * rows:(member + 1) * rows]
            attended[:, (head * group + member) * HEAD_SIZE:(head * group + member + 1) * HEAD_SIZE] = (
                part[:HEAD_SIZE] / part[HEAD_SIZE:HEAD_SIZE + 1]).T.astype(jnp.bfloat16)

    def out_copy(piece):
        return pltpu.make_async_remote_copy(
            projected.at[piece],
            o_ref.at[:, pl.ds(pl.multiple_of(piece * COLUMNS, COLUMNS), COLUMNS)],
            out_send.at[piece], out_recv.at[piece], device_id={"pipe": following}, device_id_type=MESH)

    late = chips - chips // 2
    heavy = chip >= late
    slot_of = lax.rem(chip + 2 * chips - late, 2)

    def aside_copy(piece):
        return pltpu.make_async_remote_copy(
            projected.at[piece], aside.at[slot_of, piece], out_send.at[piece],
            aside_recv.at[slot_of, piece],
            device_id={"ctx": (chip - late) // 2 * 2 + core}, device_id_type=MESH)

    def cross_copy(slot, piece):
        return pltpu.make_async_remote_copy(
            aside.at[slot, piece], landed.at[slot, piece], cross_send.at[slot, piece],
            cross_recv.at[slot, piece], device_id={"pipe": following}, device_id_type=MESH)

    def final_copy(slot, piece):
        return pltpu.make_async_remote_copy(
            landed.at[slot, piece],
            o_ref.at[:, pl.ds(pl.multiple_of(piece * COLUMNS, COLUMNS), COLUMNS)],
            final_send.at[slot, piece], out_recv.at[piece],
            device_id={"ctx": (late + chip * 2 + slot) * 2 + core}, device_id_type=MESH)

    def each_carried(act):
        @pl.loop(0, jnp.clip(chips // 2 - chip * 2, 0, 2))
        def _(slot):
            @pl.loop(0, MOVED)
            def _(piece):
                act(slot, piece)

    def carry(slot, piece):
        pltpu.make_async_remote_copy(
            aside.at[slot, piece], aside.at[slot, piece], cross_send.at[slot, piece],
            aside_recv.at[slot, piece], device_id={"pipe": following}, device_id_type=MESH).wait_recv()
        cross_copy(slot, piece).start()

    def deliver(slot, piece):
        cross_copy(slot, piece).wait_recv()
        final_copy(slot, piece).start()

    def settle(slot, piece):
        cross_copy(slot, piece).wait_send()
        final_copy(slot, piece).wait_send()

    @pl.loop(0, pieces)
    def _(piece):
        weight_copy(piece).wait()
        projected[piece] = jnp.dot(
            attended[...], weight[piece], preferred_element_type=jnp.float32).astype(jnp.bfloat16)

        @pl.when(heavy & (piece < MOVED))
        def _():
            aside_copy(piece).start()

        @pl.when(jnp.logical_not(heavy & (piece < MOVED)))
        def _():
            out_copy(piece).start()

    each_carried(carry)
    each_carried(deliver)

    for which in range(2):
        pair_copy(which).wait_send()

    each_own(lambda target, which: far_copy(target, which).wait_send())
    each_key_source(lambda owner: each_key_relay(
        owner, lambda *at: relay_copy(*at).wait_send()))
    each_value_source(lambda owner: each_value_relay(
        owner, lambda *at: relay_copy(*at).wait_send()))

    @pl.loop(0, chip)
    def _(owner):
        for which in range(2):
            pass_copy(owner, which).wait_send()

    each_carried(settle)

    @pl.loop(0, pieces)
    def _(piece):
        out_copy(piece).wait()


def square_kernel(sections, q_ref, k_ref, v_ref, w_ref, o_ref, held, weight, query, acc, top, attended, projected, aside,
                  far_send, span_recv, pass_send, relay_send, own_sem, query_sem, weight_sem, out_send, out_recv,
                  aside_recv, deliver_send):
    rows, kv_width = k_ref.shape
    heads = kv_width // HEAD_SIZE
    group = q_ref.shape[1] // kv_width
    pieces = weight.shape[0]
    section = lax.axis_index("pipe")
    me = lax.axis_index("ctx")
    chip, core = me // 2, lax.rem(me, 2)
    sibling = chip * 2 + 1 - core
    beside = (chip + 1 - 2 * lax.rem(chip, 2)) * 2 + core
    across = lax.rem(chip + 2, 4) * 2 + core
    opposite = (3 - chip) * 2 + core
    following = lax.rem(section + 1, sections)
    before = lax.rem(section + sections - 1, sections)
    factor = math.log2(math.e) / math.sqrt(HEAD_SIZE)

    barrier = pltpu.get_barrier_semaphore()
    for other in (sibling, beside, across, opposite):
        pl.semaphore_signal(barrier, inc=1, device_id={"ctx": other}, device_id_type=MESH)
    for neighbour in (before, following):
        pl.semaphore_signal(barrier, inc=1, device_id={"pipe": neighbour}, device_id_type=MESH)

    pl.semaphore_signal(
        barrier, inc=1, device_id={"pipe": before, "ctx": jnp.where(chip > 0, core, 2 + core)}, device_id_type=MESH)

    def lanes(head):
        return slice(head * HEAD_SIZE, (head + 1) * HEAD_SIZE)

    def own_copy(which):
        return pltpu.make_async_copy((k_ref, v_ref)[which], held.at[chip, core, which], own_sem.at[which])

    def query_copy(head):
        wide = group * HEAD_SIZE
        return pltpu.make_async_copy(
            q_ref.at[:, head * wide:(head + 1) * wide], query.at[:, head * wide:(head + 1) * wide], query_sem.at[head])

    def weight_copy(piece):
        return pltpu.make_async_copy(
            w_ref.at[:, pl.ds(pl.multiple_of(piece * COLUMNS, COLUMNS), COLUMNS)],
            weight.at[piece], weight_sem.at[piece])

    for which in range(2):
        own_copy(which).start()
    for head in range(heads):
        query_copy(head).start()

    def at_head(head):
        return pl.ds(pl.multiple_of(head * HEAD_SIZE, HEAD_SIZE), HEAD_SIZE)

    def span_copy(owner, head, side, send_sem, target):
        chunk = held.at[owner, side, :, :, at_head(head)]
        return pltpu.make_async_remote_copy(
            chunk, chunk, send_sem, span_recv.at[owner, side, head], device_id={"ctx": target}, device_id_type=MESH)

    def first_copy(head, way, target):
        return span_copy(chip, head, core, far_send.at[way, head], target)

    def early_copy(head, way, target):
        for which in range(2):
            pltpu.make_async_remote_copy(
                (k_ref, v_ref)[which].at[:, lanes(head)], held.at[chip, core, which, :, lanes(head)],
                far_send.at[way, head], span_recv.at[chip, core, head],
                device_id={"ctx": target}, device_id_type=MESH).start()

    def each_far(act):
        for step in range(heads):
            head = (step + heads // 2) % heads

            @pl.when((chip == 2) | ((chip == 0) & (step < heads // 2)))
            def _():
                act(step, 1, beside)

            @pl.when(chip == 0)
            def _():
                act(head, 2, across)

            @pl.when(chip == 1)
            def _():
                act(step, 2, across)

        @pl.when(chip == 1)
        def _():
            act(heads - 1, 3, opposite)

    def each_pair(act):
        @pl.when(core == 0)
        def _():
            for head in range(heads):
                act(head, 0, sibling)

    pl.semaphore_wait(barrier, jnp.where(chip == 0, 9, jnp.where(chip == 1, 7, 6)))

    each_far(early_copy)
    for which in range(2):
        own_copy(which).wait()
    each_pair(lambda *way: first_copy(*way).start())

    def stacked(head):
        return jnp.concatenate(
            [query[:, at_head(head * group + member)] for member in range(group)], axis=0)

    half = group * rows // 2
    halves = [slice(part * half, (part + 1) * half) for part in range(2)]

    def block(keys, values, head, first):
        values = values.T
        values = jnp.concatenate([values, jnp.ones((EXTRA, values.shape[1]), values.dtype)], axis=0)
        queries = stacked(head)
        before_it = [None if first else (top[head, :, part], acc[head, :, part]) for part in halves]
        scores = [lax.dot_general(
            keys, queries[part], (((1,), (1,)), ((), ())), preferred_element_type=jnp.float32) for part in halves]
        if first:
            key = lax.broadcasted_iota(jnp.int32, scores[0].shape, 0)
            row = lax.rem(lax.broadcasted_iota(jnp.int32, scores[0].shape, 1), rows)
            scores = [jnp.where(key <= row, each, -1e30) for each in scores]
        highest = [jnp.max(each, axis=0, keepdims=True) for each in scores]
        if not first:
            highest = [jnp.maximum(each[0], now) for each, now in zip(before_it, highest)]
        results = []
        for each, now, known in zip(scores, highest, before_it):
            weights = jnp.exp2((each - now) * factor).astype(jnp.bfloat16)
            summed = jnp.dot(values, weights, preferred_element_type=jnp.float32)
            if not first:
                summed = known[1] * jnp.exp2((known[0] - now) * factor) + summed
            results.append(summed)
        for part, now, summed in zip(halves, highest, results):
            top[head, :, part] = now
            acc[head, :, part] = summed

    for head in range(heads):
        query_copy(head).wait()

    @pl.loop(0, pieces)
    def _(piece):
        weight_copy(piece).start()

    for head in range(heads):
        block(held[chip, core, 0, :, lanes(head)], held[chip, core, 1, :, lanes(head)], head, True)

    @pl.when(core == 1)
    def _():
        for head in range(heads):
            span_copy(chip, head, 0, far_send.at[0, head], sibling).wait_recv()
        for head in range(heads):
            block(held[chip, 0, 0, :, lanes(head)], held[chip, 0, 1, :, lanes(head)], head, False)

    moved, base = 0, 0
    slots = [[], []]
    for side in range(2):
        for origin in (0, 3, 2, 1):
            count = HANDED_OVER[origin][side]
            here = (chip == origin) & (core == side)
            moved = jnp.where(here, count, moved)
            if origin > 0:
                base = jnp.where(here, len(slots[side]), base)
                slots[side] += [(origin, 2 * each + 1) for each in range(count)]
    fed = jnp.where(chip == 1, jnp.where(core == 0, *HANDED_OVER[0]), 0)

    def columns(piece):
        return o_ref.at[:, pl.ds(pl.multiple_of(piece * COLUMNS, COLUMNS), COLUMNS)]

    def out_copy(piece):
        return pltpu.make_async_remote_copy(
            projected.at[piece], columns(piece), out_send.at[piece], out_recv.at[piece],
            device_id={"pipe": following}, device_id_type=MESH)

    def aside_copy(piece):
        slot = base + piece // 2
        return pltpu.make_async_remote_copy(
            projected.at[piece], aside.at[slot], out_send.at[piece], aside_recv.at[slot],
            device_id={"ctx": jnp.where(chip == 0, 2 + core, core)}, device_id_type=MESH)

    def deliver_copy(slot, origin, piece):
        return pltpu.make_async_remote_copy(
            aside.at[slot], columns(piece), deliver_send.at[slot], out_recv.at[piece],
            device_id={"pipe": following, "ctx": origin * 2 + core}, device_id_type=MESH)

    def each_delivered(act):
        for side in range(2):
            @pl.when((chip == 0) & (core == side))
            def _():
                for slot, place in enumerate(slots[side]):
                    act(slot, *place)

    def deliver(slot, origin, piece):
        pltpu.make_async_remote_copy(
            aside.at[slot], aside.at[slot], deliver_send.at[slot], aside_recv.at[slot],
            device_id={"ctx": sibling}, device_id_type=MESH).wait_recv()
        deliver_copy(slot, origin, piece).start()

    def forward(slot):
        deliver(slot, 0, 2 * slot + 1)

    steps = chip * heads

    def at(step):
        later = step - 2 * heads
        owner_last = jnp.where(later < 0, 1 + lax.rem(step, 2), 0)
        head_last = jnp.where(later < 0, step // 2, (1 - lax.rem(later, 2)) * (heads // 2) + later // 2)
        own_third = (step == 0) | ((step > 1) & (lax.rem(step, 2) == 1))
        head_third = jnp.where(step == 1, heads - 1, jnp.where(own_third, lax.rem(step // 2 + heads // 2, heads), step // 2 - 1))
        owner = jnp.where(chip == 3, owner_last, jnp.where((chip == 2) & jnp.logical_not(own_third), 1, 0))
        head = jnp.where(chip == 3, head_last, jnp.where(chip == 2, head_third, step))
        return owner, head

    def relayed(owner, head):
        late = head >= heads // 2
        last = ((owner == 1) & (head < heads - 1)) | ((owner == 0) & late)
        return ((chip == 1) & jnp.logical_not(late)) | ((chip == 2) & (owner == 0) & late) | ((chip == 3) & last)

    def relay_copy(owner, head):
        target = jnp.where((chip == 1) | ((chip == 3) & (owner == 0)), across, beside)
        return span_copy(owner, head, core, relay_send.at[owner, head], target)

    def arrive(step):
        owner, head = at(step)
        span_copy(owner, head, core, pass_send.at[owner, head], sibling).wait_recv()

        @pl.when(relayed(owner, head))
        def _():
            relay_copy(owner, head).start()

        span_copy(owner, head, core, pass_send.at[owner, head], sibling).start()

    @pl.when(chip > 0)
    def _():
        arrive(0)

    @pl.loop(0, steps)
    def _(step):
        @pl.when((step + 1 < steps) & ((chip > 1) | (step == 0)))
        def _():
            arrive(step + 1)

        owner, head = at(step)
        span_copy(owner, head, 1 - core, pass_send.at[owner, head], sibling).wait_recv()
        keys = held[owner, :, 0, :, at_head(head)].reshape(2 * rows, HEAD_SIZE)
        values = held[owner, :, 1, :, at_head(head)].reshape(2 * rows, HEAD_SIZE)
        block(keys, values, head, False)

        @pl.when((chip == 1) & (step == 0))
        def _():
            forward(0)

        @pl.when((chip == 1) & (step == 1))
        def _():
            @pl.loop(1, fed - 1)
            def _(slot):
                forward(slot)

            arrive(step + 1)
            arrive(step + 2)

        @pl.when((chip == 1) & (step == 2))
        def _():
            forward(fed - 1)

    for head in range(heads):
        for member in range(group):
            part = acc[head, :, member * rows:(member + 1) * rows]
            attended[:, lanes(head * group + member)] = (
                part[:HEAD_SIZE] / part[HEAD_SIZE:HEAD_SIZE + 1]).T.astype(jnp.bfloat16)

    @pl.loop(0, pieces)
    def _(piece):
        weight_copy(piece).wait()
        projected[piece] = jnp.dot(
            attended[...], weight[piece], preferred_element_type=jnp.float32).astype(jnp.bfloat16)

        handed = (lax.rem(piece, 2) == 1) & (piece < 2 * moved)

        @pl.when(jnp.logical_not(handed))
        def _():
            out_copy(piece).start()

        @pl.when(handed)
        def _():
            aside_copy(piece).start()

    each_delivered(deliver)

    each_far(lambda *way: first_copy(*way).wait_send())
    each_pair(lambda *way: first_copy(*way).wait_send())

    @pl.loop(0, steps)
    def _(step):
        owner, head = at(step)
        span_copy(owner, head, core, pass_send.at[owner, head], sibling).wait_send()

        @pl.when(relayed(owner, head))
        def _():
            relay_copy(owner, head).wait_send()

    each_delivered(lambda *place: deliver_copy(*place).wait_send())

    @pl.loop(0, fed)
    def _(slot):
        deliver_copy(slot, 0, 2 * slot + 1).wait_send()

    @pl.loop(0, pieces)
    def _(piece):
        out_copy(piece).wait()


def general_device(sections, spans, queries, keys, values, out_weight):
    rows, q_width = queries.shape[1:]
    kv_width = keys.shape[2]
    width = out_weight.shape[2]
    heads = kv_width // HEAD_SIZE
    stack = q_width // kv_width * rows
    pieces = width // COLUMNS
    chips = spans // 2
    across = math.isqrt(chips)
    across = across if chips % across == 0 else chips
    hbm = pl.BlockSpec(memory_space=pltpu.HBM)
    handed = pl.pallas_call(
        functools.partial(general_kernel, sections, spans, across),
        out_shape=jax.ShapeDtypeStruct((rows, width), jnp.bfloat16),
        in_specs=[hbm] * 4,
        out_specs=pl.BlockSpec(memory_space=pl.ANY),
        scratch_shapes=[
            pltpu.VMEM((chips, 2, 2 * rows, kv_width), jnp.bfloat16),
            pltpu.VMEM((pieces, q_width, COLUMNS), jnp.bfloat16),
            pltpu.VMEM((heads, stack, HEAD_SIZE), jnp.bfloat16),
            pltpu.VMEM((heads, HEAD_SIZE + EXTRA, stack), jnp.float32),
            pltpu.VMEM((heads, 1, stack), jnp.float32),
            pltpu.VMEM((rows, q_width), jnp.bfloat16),
            pltpu.VMEM((pieces, rows, COLUMNS), jnp.bfloat16),
            pltpu.SemaphoreType.DMA((2,)),
            pltpu.SemaphoreType.DMA((chips, 2)),
            pltpu.SemaphoreType.DMA((chips, 2)),
            pltpu.SemaphoreType.DMA((chips, chips)),
            pltpu.SemaphoreType.DMA((chips, 2, 2)),
            pltpu.SemaphoreType.DMA((pieces,)),
            pltpu.SemaphoreType.DMA((pieces,)),
            pltpu.SemaphoreType.DMA((pieces,)),
            pltpu.SemaphoreType.DMA((2,)),
            pltpu.SemaphoreType.DMA((q_width // HEAD_SIZE,)),
            pltpu.VMEM((2, MOVED, rows, COLUMNS), jnp.bfloat16),
            pltpu.VMEM((2, MOVED, rows, COLUMNS), jnp.bfloat16),
            pltpu.SemaphoreType.DMA((2, MOVED)),
            pltpu.SemaphoreType.DMA((2, MOVED)),
            pltpu.SemaphoreType.DMA((2, MOVED)),
            pltpu.SemaphoreType.DMA((2, MOVED)),
        ],
        compiler_params=pltpu.CompilerParams(
            collective_id=0, has_side_effects=True, vmem_limit_bytes=VMEM_LIMIT),
    )(*(pltpu.with_memory_space_constraint(each[0], pltpu.HBM) for each in (queries, keys, values, out_weight)))
    return handed[None]


def square_device(sections, queries, keys, values, out_weight):
    rows, q_width = queries.shape[1:]
    kv_width = keys.shape[2]
    width = out_weight.shape[2]
    heads = kv_width // HEAD_SIZE
    stack = q_width // kv_width * rows
    pieces = width // COLUMNS
    slots = max(max(HANDED_OVER[0]), *(sum(counts[side] for counts in HANDED_OVER[1:]) for side in range(2)))
    hbm = pl.BlockSpec(memory_space=pltpu.HBM)
    handed = pl.pallas_call(
        functools.partial(square_kernel, sections),
        out_shape=jax.ShapeDtypeStruct((rows, width), jnp.bfloat16),
        in_specs=[hbm] * 4,
        out_specs=pl.BlockSpec(memory_space=pl.ANY),
        scratch_shapes=[
            pltpu.VMEM((4, 2, 2, rows, kv_width), jnp.bfloat16),
            pltpu.VMEM((pieces, q_width, COLUMNS), jnp.bfloat16),
            pltpu.VMEM((rows, q_width), jnp.bfloat16),
            pltpu.VMEM((heads, HEAD_SIZE + EXTRA, stack), jnp.float32),
            pltpu.VMEM((heads, 1, stack), jnp.float32),
            pltpu.VMEM((rows, q_width), jnp.bfloat16),
            pltpu.VMEM((pieces, rows, COLUMNS), jnp.bfloat16),
            pltpu.VMEM((slots, rows, COLUMNS), jnp.bfloat16),
            pltpu.SemaphoreType.DMA((4, heads)),
            pltpu.SemaphoreType.DMA((4, 2, heads)),
            pltpu.SemaphoreType.DMA((4, heads)),
            pltpu.SemaphoreType.DMA((2, heads)),
            pltpu.SemaphoreType.DMA((2,)),
            pltpu.SemaphoreType.DMA((heads,)),
            pltpu.SemaphoreType.DMA((pieces,)),
            pltpu.SemaphoreType.DMA((pieces,)),
            pltpu.SemaphoreType.DMA((pieces,)),
            pltpu.SemaphoreType.DMA((slots,)),
            pltpu.SemaphoreType.DMA((slots,)),
        ],
        compiler_params=pltpu.CompilerParams(
            collective_id=1, has_side_effects=True, vmem_limit_bytes=VMEM_LIMIT),
    )(*(pltpu.with_memory_space_constraint(each[0], pltpu.HBM) for each in (queries, keys, values, out_weight)))
    return handed[None]


def per_device(sections, spans, *operands):
    if spans == 8:
        return square_device(sections, *operands)
    return general_device(sections, spans, *operands)


def solution(mesh):
    placed = (
        P("pipe", "ctx", None),
        P("pipe", "ctx", None),
        P("pipe", "ctx", None),
        P("pipe", None, None),
    )
    return jax.shard_map(
        functools.partial(per_device, mesh.shape["pipe"], mesh.shape["ctx"]),
        mesh=mesh, in_specs=placed, out_specs=P("pipe", "ctx", None), check_vma=False
    )
```

```python
import functools
import math

import jax
import jax.numpy as jnp
from jax import lax
from jax.experimental import pallas as pl
from jax.experimental.pallas import tpu as pltpu
from jax.sharding import PartitionSpec as P

HEAD_SIZE = 128
COLUMNS = 256
MOVED = 2
HANDED_OVER = ((6, 6), (5, 4), (2, 2), (3, 3))
EXTRA = 16
VMEM_LIMIT = 50 * 1024 * 1024
MESH = pl.DeviceIdType.MESH


def general_kernel(sections, spans, across, q_ref, k_ref, v_ref, w_ref, o_ref, held, weight, stacked, acc, top,
           attended, projected, pair_send, far_send, pass_send, relay_send, span_recv, weight_sem, out_send, out_recv, own_sem, query_sem,
           aside, landed, aside_recv, cross_send, cross_recv, final_send):
    rows, kv_width = k_ref.shape
    q_width = q_ref.shape[1]
    heads = kv_width // HEAD_SIZE
    group = q_width // kv_width
    chips = spans // 2
    pieces = weight.shape[0]
    section = lax.axis_index("pipe")
    me = lax.axis_index("ctx")
    chip, core = me // 2, lax.rem(me, 2)
    line, column = chip // across, lax.rem(chip, across)
    lines = chips // across
    following = lax.rem(section + 1, sections)
    before = lax.rem(section + sections - 1, sections)
    factor = math.log2(math.e) / math.sqrt(HEAD_SIZE)

    barrier = pltpu.get_barrier_semaphore()

    @pl.loop(1, spans)
    def _(step):
        pl.semaphore_signal(barrier, inc=1, device_id={"ctx": lax.rem(me + step, spans)}, device_id_type=MESH)

    for neighbour in (before, following):
        pl.semaphore_signal(barrier, inc=1, device_id={"pipe": neighbour}, device_id_type=MESH)

    def weight_copy(piece):
        return pltpu.make_async_copy(
            w_ref.at[:, pl.ds(pl.multiple_of(piece * COLUMNS, COLUMNS), COLUMNS)],
            weight.at[piece], weight_sem.at[piece])

    def place(owner, side, which):
        return held.at[owner, which, pl.ds(pl.multiple_of(side * rows, rows), rows), :]

    def own_copy(which):
        return pltpu.make_async_copy((k_ref, v_ref)[which], place(chip, core, which), own_sem.at[which])

    def query_copy(head, member):
        at = head * group + member
        return pltpu.make_async_copy(
            q_ref.at[:, at * HEAD_SIZE:(at + 1) * HEAD_SIZE],
            stacked.at[head, member * rows:(member + 1) * rows, :], query_sem.at[at])

    for which in range(2):
        own_copy(which).start()
    for head in range(heads):
        for member in range(group):
            query_copy(head, member).start()

    @pl.loop(0, pieces)
    def _(piece):
        weight_copy(piece).start()

    for which in range(2):
        own_copy(which).wait()

    def pair_copy(which):
        return pltpu.make_async_remote_copy(
            place(chip, core, which), place(chip, core, which), pair_send.at[which],
            span_recv.at[chip, core, which], device_id={"ctx": chip * 2 + 1 - core}, device_id_type=MESH)

    def far_copy(target, which):
        return pltpu.make_async_remote_copy(
            place(chip, core, which), place(chip, core, which), far_send.at[target, which],
            span_recv.at[chip, core, which], device_id={"ctx": target * 2 + core}, device_id_type=MESH)

    def pass_copy(owner, which):
        return pltpu.make_async_remote_copy(
            place(owner, core, which), place(owner, core, which), pass_send.at[owner, which],
            span_recv.at[owner, core, which], device_id={"ctx": chip * 2 + 1 - core}, device_id_type=MESH)

    def relay_copy(owner, target, which):
        return pltpu.make_async_remote_copy(
            place(owner, core, which), place(owner, core, which), relay_send.at[owner, target],
            span_recv.at[owner, core, which], device_id={"ctx": target * 2 + core}, device_id_type=MESH)

    def each_own(act):
        @pl.loop(1, across)
        def _(step):
            other = lax.rem(column + step, across)

            @pl.when((line < lines - 1) | (other > column))
            def _():
                act(line * across + other, 0)

        @pl.loop(line + 1, lines)
        def _(other):
            act(other * across + column, 1)
            act(other * across + column, 0)

        @pl.loop(column + 1, across)
        def _(other):
            act(line * across + other, 1)

    def each_key_source(act):
        @pl.when(line < lines - 1)
        def _():
            @pl.loop(1, across)
            def _(step):
                act(line * across + lax.rem(column + step, across))

    def each_key_relay(owner, act):
        @pl.loop(line + 1, lines)
        def _(other):
            act(owner, other * across + column, 0)

    def each_value_source(act):
        @pl.loop(0, line)
        def _(other):
            act(other * across + column)

    def each_value_relay(owner, act):
        @pl.loop(1, across)
        def _(step):
            act(owner, line * across + lax.rem(column + step, across), 1)

    def wait_span(owner, side, which):
        pltpu.make_async_remote_copy(
            place(owner, side, which), place(owner, side, which), pair_send.at[which],
            span_recv.at[owner, side, which], device_id={"ctx": chip * 2 + 1 - core}, device_id_type=MESH).wait_recv()

    pl.semaphore_wait(barrier, spans + 1)
    for which in range(2):
        pair_copy(which).start()

    each_own(lambda target, which: far_copy(target, which).start())

    for head in range(heads):
        for member in range(group):
            query_copy(head, member).wait()

    def block(owner, head, first):
        lanes = slice(head * HEAD_SIZE, (head + 1) * HEAD_SIZE)
        scores = lax.dot_general(
            held[owner, 0, :, lanes], stacked[head], (((1,), (1,)), ((), ())),
            preferred_element_type=jnp.float32)
        if first:
            key = lax.broadcasted_iota(jnp.int32, scores.shape, 0)
            row = lax.rem(lax.broadcasted_iota(jnp.int32, scores.shape, 1), rows) + core * rows
            scores = jnp.where(key <= row, scores, -1e30)
        highest = jnp.max(scores, axis=0, keepdims=True)
        if not first:
            previous = top[head]
            highest = jnp.maximum(previous, highest)
            rescale = jnp.exp2((previous - highest) * factor)
        top[head] = highest
        weights = jnp.exp2((scores - highest) * factor).astype(jnp.bfloat16)
        values = held[owner, 1, :, lanes].T
        values = jnp.concatenate([values, jnp.ones((EXTRA, values.shape[1]), values.dtype)], axis=0)
        summed = jnp.dot(values, weights, preferred_element_type=jnp.float32)
        if first:
            acc[head] = summed
        else:
            acc[head] = acc[head] * rescale + summed

    for which in range(2):
        wait_span(chip, 1 - core, which)

    for head in range(heads):
        block(chip, head, True)

    def relay_keys(owner):
        wait_span(owner, core, 0)
        each_key_relay(owner, lambda *at: relay_copy(*at).start())

        @pl.when(owner < chip)
        def _():
            pass_copy(owner, 0).start()

    def relay_values(owner):
        wait_span(owner, core, 1)
        each_value_relay(owner, lambda *at: relay_copy(*at).start())
        pass_copy(owner, 1).start()

    each_value_source(relay_values)
    each_key_source(relay_keys)

    @pl.loop(0, chip)
    def _(step):
        owner = chip - 1 - step

        @pl.when((owner // across != line) | (line == lines - 1))
        def _():
            wait_span(owner, core, 0)
            pass_copy(owner, 0).start()

        @pl.when((lax.rem(owner, across) != column) | (owner // across == line))
        def _():
            wait_span(owner, core, 1)
            pass_copy(owner, 1).start()

        for which in range(2):
            wait_span(owner, 1 - core, which)

        for head in range(heads):
            block(owner, head, False)

    for head in range(heads):
        for member in range(group):
            part = acc[head, :, member * rows:(member + 1) * rows]
            attended[:, (head * group + member) * HEAD_SIZE:(head * group + member + 1) * HEAD_SIZE] = (
                part[:HEAD_SIZE] / part[HEAD_SIZE:HEAD_SIZE + 1]).T.astype(jnp.bfloat16)

    def out_copy(piece):
        return pltpu.make_async_remote_copy(
            projected.at[piece],
            o_ref.at[:, pl.ds(pl.multiple_of(piece * COLUMNS, COLUMNS), COLUMNS)],
            out_send.at[piece], out_recv.at[piece], device_id={"pipe": following}, device_id_type=MESH)

    late = chips - chips // 2
    heavy = chip >= late
    slot_of = lax.rem(chip + 2 * chips - late, 2)

    def aside_copy(piece):
        return pltpu.make_async_remote_copy(
            projected.at[piece], aside.at[slot_of, piece], out_send.at[piece],
            aside_recv.at[slot_of, piece],
            device_id={"ctx": (chip - late) // 2 * 2 + core}, device_id_type=MESH)

    def cross_copy(slot, piece):
        return pltpu.make_async_remote_copy(
            aside.at[slot, piece], landed.at[slot, piece], cross_send.at[slot, piece],
            cross_recv.at[slot, piece], device_id={"pipe": following}, device_id_type=MESH)

    def final_copy(slot, piece):
        return pltpu.make_async_remote_copy(
            landed.at[slot, piece],
            o_ref.at[:, pl.ds(pl.multiple_of(piece * COLUMNS, COLUMNS), COLUMNS)],
            final_send.at[slot, piece], out_recv.at[piece],
            device_id={"ctx": (late + chip * 2 + slot) * 2 + core}, device_id_type=MESH)

    def each_carried(act):
        @pl.loop(0, jnp.clip(chips // 2 - chip * 2, 0, 2))
        def _(slot):
            @pl.loop(0, MOVED)
            def _(piece):
                act(slot, piece)

    def carry(slot, piece):
        pltpu.make_async_remote_copy(
            aside.at[slot, piece], aside.at[slot, piece], cross_send.at[slot, piece],
            aside_recv.at[slot, piece], device_id={"pipe": following}, device_id_type=MESH).wait_recv()
        cross_copy(slot, piece).start()

    def deliver(slot, piece):
        cross_copy(slot, piece).wait_recv()
        final_copy(slot, piece).start()

    def settle(slot, piece):
        cross_copy(slot, piece).wait_send()
        final_copy(slot, piece).wait_send()

    @pl.loop(0, pieces)
    def _(piece):
        weight_copy(piece).wait()
        projected[piece] = jnp.dot(
            attended[...], weight[piece], preferred_element_type=jnp.float32).astype(jnp.bfloat16)

        @pl.when(heavy & (piece < MOVED))
        def _():
            aside_copy(piece).start()

        @pl.when(jnp.logical_not(heavy & (piece < MOVED)))
        def _():
            out_copy(piece).start()

    each_carried(carry)
    each_carried(deliver)

    for which in range(2):
        pair_copy(which).wait_send()

    each_own(lambda target, which: far_copy(target, which).wait_send())
    each_key_source(lambda owner: each_key_relay(
        owner, lambda *at: relay_copy(*at).wait_send()))
    each_value_source(lambda owner: each_value_relay(
        owner, lambda *at: relay_copy(*at).wait_send()))

    @pl.loop(0, chip)
    def _(owner):
        for which in range(2):
            pass_copy(owner, which).wait_send()

    each_carried(settle)

    @pl.loop(0, pieces)
    def _(piece):
        out_copy(piece).wait()


def square_kernel(sections, q_ref, k_ref, v_ref, w_ref, o_ref, held, weight, query, acc, top, attended, projected, aside,
                  far_send, span_recv, pass_send, relay_send, own_sem, query_sem, weight_sem, out_send, out_recv,
                  aside_recv, deliver_send):
    rows, kv_width = k_ref.shape
    heads = kv_width // HEAD_SIZE
    group = q_ref.shape[1] // kv_width
    pieces = weight.shape[0]
    section = lax.axis_index("pipe")
    me = lax.axis_index("ctx")
    chip, core = me // 2, lax.rem(me, 2)
    sibling = chip * 2 + 1 - core
    beside = (chip + 1 - 2 * lax.rem(chip, 2)) * 2 + core
    across = lax.rem(chip + 2, 4) * 2 + core
    opposite = (3 - chip) * 2 + core
    following = lax.rem(section + 1, sections)
    before = lax.rem(section + sections - 1, sections)
    factor = math.log2(math.e) / math.sqrt(HEAD_SIZE)

    barrier = pltpu.get_barrier_semaphore()
    for other in (sibling, beside, across, opposite):
        pl.semaphore_signal(barrier, inc=1, device_id={"ctx": other}, device_id_type=MESH)
    for neighbour in (before, following):
        pl.semaphore_signal(barrier, inc=1, device_id={"pipe": neighbour}, device_id_type=MESH)

    pl.semaphore_signal(
        barrier, inc=1, device_id={"pipe": before, "ctx": jnp.where(chip > 0, core, 2 + core)}, device_id_type=MESH)

    def lanes(head):
        return slice(head * HEAD_SIZE, (head + 1) * HEAD_SIZE)

    def own_copy(which):
        return pltpu.make_async_copy((k_ref, v_ref)[which], held.at[chip, core, which], own_sem.at[which])

    def query_copy(head):
        wide = group * HEAD_SIZE
        return pltpu.make_async_copy(
            q_ref.at[:, head * wide:(head + 1) * wide], query.at[:, head * wide:(head + 1) * wide], query_sem.at[head])

    def weight_copy(piece):
        return pltpu.make_async_copy(
            w_ref.at[:, pl.ds(pl.multiple_of(piece * COLUMNS, COLUMNS), COLUMNS)],
            weight.at[piece], weight_sem.at[piece])

    for which in range(2):
        own_copy(which).start()
    for head in range(heads):
        query_copy(head).start()

    def at_head(head):
        return pl.ds(pl.multiple_of(head * HEAD_SIZE, HEAD_SIZE), HEAD_SIZE)

    def span_copy(owner, head, side, send_sem, target):
        chunk = held.at[owner, side, :, :, at_head(head)]
        return pltpu.make_async_remote_copy(
            chunk, chunk, send_sem, span_recv.at[owner, side, head], device_id={"ctx": target}, device_id_type=MESH)

    def first_copy(head, way, target):
        return span_copy(chip, head, core, far_send.at[way, head], target)

    def early_copy(head, way, target):
        for which in range(2):
            pltpu.make_async_remote_copy(
                (k_ref, v_ref)[which].at[:, lanes(head)], held.at[chip, core, which, :, lanes(head)],
                far_send.at[way, head], span_recv.at[chip, core, head],
                device_id={"ctx": target}, device_id_type=MESH).start()

    def each_far(act):
        for step in range(heads):
            head = (step + heads // 2) % heads

            @pl.when((chip == 2) | ((chip == 0) & (step < heads // 2)))
            def _():
                act(step, 1, beside)

            @pl.when(chip == 0)
            def _():
                act(head, 2, across)

            @pl.when(chip == 1)
            def _():
                act(step, 2, across)

        @pl.when(chip == 1)
        def _():
            act(heads - 1, 3, opposite)

    def each_pair(act):
        @pl.when(core == 0)
        def _():
            for head in range(heads):
                act(head, 0, sibling)

    pl.semaphore_wait(barrier, jnp.where(chip == 0, 9, jnp.where(chip == 1, 7, 6)))

    each_far(early_copy)
    for which in range(2):
        own_copy(which).wait()
    each_pair(lambda *way: first_copy(*way).start())

    def stacked(head):
        return jnp.concatenate(
            [query[:, at_head(head * group + member)] for member in range(group)], axis=0)

    half = group * rows // 2
    halves = [slice(part * half, (part + 1) * half) for part in range(2)]

    def block(keys, values, head, first):
        values = values.T
        values = jnp.concatenate([values, jnp.ones((EXTRA, values.shape[1]), values.dtype)], axis=0)
        queries = stacked(head)
        before_it = [None if first else (top[head, :, part], acc[head, :, part]) for part in halves]
        scores = [lax.dot_general(
            keys, queries[part], (((1,), (1,)), ((), ())), preferred_element_type=jnp.float32) for part in halves]
        if first:
            key = lax.broadcasted_iota(jnp.int32, scores[0].shape, 0)
            row = lax.rem(lax.broadcasted_iota(jnp.int32, scores[0].shape, 1), rows)
            scores = [jnp.where(key <= row, each, -1e30) for each in scores]
        highest = [jnp.max(each, axis=0, keepdims=True) for each in scores]
        if not first:
            highest = [jnp.maximum(each[0], now) for each, now in zip(before_it, highest)]
        results = []
        for each, now, known in zip(scores, highest, before_it):
            weights = jnp.exp2((each - now) * factor).astype(jnp.bfloat16)
            summed = jnp.dot(values, weights, preferred_element_type=jnp.float32)
            if not first:
                summed = known[1] * jnp.exp2((known[0] - now) * factor) + summed
            results.append(summed)
        for part, now, summed in zip(halves, highest, results):
            top[head, :, part] = now
            acc[head, :, part] = summed

    for head in range(heads):
        query_copy(head).wait()

    @pl.loop(0, pieces)
    def _(piece):
        weight_copy(piece).start()

    for head in range(heads):
        block(held[chip, core, 0, :, lanes(head)], held[chip, core, 1, :, lanes(head)], head, True)

    @pl.when(core == 1)
    def _():
        for head in range(heads):
            span_copy(chip, head, 0, far_send.at[0, head], sibling).wait_recv()
        for head in range(heads):
            block(held[chip, 0, 0, :, lanes(head)], held[chip, 0, 1, :, lanes(head)], head, False)

    moved, base = 0, 0
    slots = [[], []]
    for side in range(2):
        for origin in (0, 3, 1, 2):
            count = HANDED_OVER[origin][side]
            here = (chip == origin) & (core == side)
            moved = jnp.where(here, count, moved)
            if origin > 0:
                base = jnp.where(here, len(slots[side]), base)
                slots[side] += [(origin, 2 * each + 1) for each in range(count)]
    fed = jnp.where(chip == 1, jnp.where(core == 0, *HANDED_OVER[0]), 0)

    def columns(piece):
        return o_ref.at[:, pl.ds(pl.multiple_of(piece * COLUMNS, COLUMNS), COLUMNS)]

    def out_copy(piece):
        return pltpu.make_async_remote_copy(
            projected.at[piece], columns(piece), out_send.at[piece], out_recv.at[piece],
            device_id={"pipe": following}, device_id_type=MESH)

    def aside_copy(piece):
        slot = base + piece // 2
        return pltpu.make_async_remote_copy(
            projected.at[piece], aside.at[slot], out_send.at[piece], aside_recv.at[slot],
            device_id={"ctx": jnp.where(chip == 0, 2 + core, core)}, device_id_type=MESH)

    def deliver_copy(slot, origin, piece):
        return pltpu.make_async_remote_copy(
            aside.at[slot], columns(piece), deliver_send.at[slot], out_recv.at[piece],
            device_id={"pipe": following, "ctx": origin * 2 + core}, device_id_type=MESH)

    def each_delivered(act):
        for side in range(2):
            @pl.when((chip == 0) & (core == side))
            def _():
                for slot, place in enumerate(slots[side]):
                    act(slot, *place)

    def deliver(slot, origin, piece):
        pltpu.make_async_remote_copy(
            aside.at[slot], aside.at[slot], deliver_send.at[slot], aside_recv.at[slot],
            device_id={"ctx": sibling}, device_id_type=MESH).wait_recv()
        deliver_copy(slot, origin, piece).start()

    def forward(slot):
        deliver(slot, 0, 2 * slot + 1)

    steps = chip * heads

    def at(step):
        later = step - 2 * heads
        owner_last = jnp.where(later < 0, 1 + lax.rem(step, 2), 0)
        head_last = jnp.where(later < 0, step // 2, (1 - lax.rem(later, 2)) * (heads // 2) + later // 2)
        own_third = (step == 0) | ((step > 1) & (lax.rem(step, 2) == 1))
        head_third = jnp.where(step == 1, heads - 1, jnp.where(own_third, lax.rem(step // 2 + heads // 2, heads), step // 2 - 1))
        owner = jnp.where(chip == 3, owner_last, jnp.where((chip == 2) & jnp.logical_not(own_third), 1, 0))
        head = jnp.where(chip == 3, head_last, jnp.where(chip == 2, head_third, step))
        return owner, head

    def relayed(owner, head):
        late = head >= heads // 2
        last = ((owner == 1) & (head < heads - 1)) | ((owner == 0) & late)
        return ((chip == 1) & jnp.logical_not(late)) | ((chip == 2) & (owner == 0) & late) | ((chip == 3) & last)

    def relay_copy(owner, head):
        target = jnp.where((chip == 1) | ((chip == 3) & (owner == 0)), across, beside)
        return span_copy(owner, head, core, relay_send.at[owner, head], target)

    def arrive(step):
        owner, head = at(step)
        span_copy(owner, head, core, pass_send.at[owner, head], sibling).wait_recv()

        @pl.when(relayed(owner, head))
        def _():
            relay_copy(owner, head).start()

        span_copy(owner, head, core, pass_send.at[owner, head], sibling).start()

    @pl.when(chip > 0)
    def _():
        arrive(0)

    @pl.loop(0, steps)
    def _(step):
        @pl.when((step + 1 < steps) & ((chip > 1) | (step == 0)))
        def _():
            arrive(step + 1)

        owner, head = at(step)
        span_copy(owner, head, 1 - core, pass_send.at[owner, head], sibling).wait_recv()
        keys = held[owner, :, 0, :, at_head(head)].reshape(2 * rows, HEAD_SIZE)
        values = held[owner, :, 1, :, at_head(head)].reshape(2 * rows, HEAD_SIZE)
        block(keys, values, head, False)

        @pl.when((chip == 1) & (step == 0))
        def _():
            forward(0)

        @pl.when((chip == 1) & (step == 1))
        def _():
            @pl.loop(1, fed - 1)
            def _(slot):
                forward(slot)

            arrive(step + 1)
            arrive(step + 2)

        @pl.when((chip == 1) & (step == 2))
        def _():
            forward(fed - 1)

    for head in range(heads):
        for member in range(group):
            part = acc[head, :, member * rows:(member + 1) * rows]
            attended[:, lanes(head * group + member)] = (
                part[:HEAD_SIZE] / part[HEAD_SIZE:HEAD_SIZE + 1]).T.astype(jnp.bfloat16)

    @pl.loop(0, pieces)
    def _(piece):
        weight_copy(piece).wait()
        projected[piece] = jnp.dot(
            attended[...], weight[piece], preferred_element_type=jnp.float32).astype(jnp.bfloat16)

        handed = (lax.rem(piece, 2) == 1) & (piece < 2 * moved)

        @pl.when(jnp.logical_not(handed))
        def _():
            out_copy(piece).start()

        @pl.when(handed)
        def _():
            aside_copy(piece).start()

    each_delivered(deliver)

    each_far(lambda *way: first_copy(*way).wait_send())
    each_pair(lambda *way: first_copy(*way).wait_send())

    @pl.loop(0, steps)
    def _(step):
        owner, head = at(step)
        span_copy(owner, head, core, pass_send.at[owner, head], sibling).wait_send()

        @pl.when(relayed(owner, head))
        def _():
            relay_copy(owner, head).wait_send()

    each_delivered(lambda *place: deliver_copy(*place).wait_send())

    @pl.loop(0, fed)
    def _(slot):
        deliver_copy(slot, 0, 2 * slot + 1).wait_send()

    @pl.loop(0, pieces)
    def _(piece):
        out_copy(piece).wait()


def general_device(sections, spans, queries, keys, values, out_weight):
    rows, q_width = queries.shape[1:]
    kv_width = keys.shape[2]
    width = out_weight.shape[2]
    heads = kv_width // HEAD_SIZE
    stack = q_width // kv_width * rows
    pieces = width // COLUMNS
    chips = spans // 2
    across = math.isqrt(chips)
    across = across if chips % across == 0 else chips
    hbm = pl.BlockSpec(memory_space=pltpu.HBM)
    handed = pl.pallas_call(
        functools.partial(general_kernel, sections, spans, across),
        out_shape=jax.ShapeDtypeStruct((rows, width), jnp.bfloat16),
        in_specs=[hbm] * 4,
        out_specs=pl.BlockSpec(memory_space=pl.ANY),
        scratch_shapes=[
            pltpu.VMEM((chips, 2, 2 * rows, kv_width), jnp.bfloat16),
            pltpu.VMEM((pieces, q_width, COLUMNS), jnp.bfloat16),
            pltpu.VMEM((heads, stack, HEAD_SIZE), jnp.bfloat16),
            pltpu.VMEM((heads, HEAD_SIZE + EXTRA, stack), jnp.float32),
            pltpu.VMEM((heads, 1, stack), jnp.float32),
            pltpu.VMEM((rows, q_width), jnp.bfloat16),
            pltpu.VMEM((pieces, rows, COLUMNS), jnp.bfloat16),
            pltpu.SemaphoreType.DMA((2,)),
            pltpu.SemaphoreType.DMA((chips, 2)),
            pltpu.SemaphoreType.DMA((chips, 2)),
            pltpu.SemaphoreType.DMA((chips, chips)),
            pltpu.SemaphoreType.DMA((chips, 2, 2)),
            pltpu.SemaphoreType.DMA((pieces,)),
            pltpu.SemaphoreType.DMA((pieces,)),
            pltpu.SemaphoreType.DMA((pieces,)),
            pltpu.SemaphoreType.DMA((2,)),
            pltpu.SemaphoreType.DMA((q_width // HEAD_SIZE,)),
            pltpu.VMEM((2, MOVED, rows, COLUMNS), jnp.bfloat16),
            pltpu.VMEM((2, MOVED, rows, COLUMNS), jnp.bfloat16),
            pltpu.SemaphoreType.DMA((2, MOVED)),
            pltpu.SemaphoreType.DMA((2, MOVED)),
            pltpu.SemaphoreType.DMA((2, MOVED)),
            pltpu.SemaphoreType.DMA((2, MOVED)),
        ],
        compiler_params=pltpu.CompilerParams(
            collective_id=0, has_side_effects=True, vmem_limit_bytes=VMEM_LIMIT),
    )(*(pltpu.with_memory_space_constraint(each[0], pltpu.HBM) for each in (queries, keys, values, out_weight)))
    return handed[None]


def square_device(sections, queries, keys, values, out_weight):
    rows, q_width = queries.shape[1:]
    kv_width = keys.shape[2]
    width = out_weight.shape[2]
    heads = kv_width // HEAD_SIZE
    stack = q_width // kv_width * rows
    pieces = width // COLUMNS
    slots = max(max(HANDED_OVER[0]), *(sum(counts[side] for counts in HANDED_OVER[1:]) for side in range(2)))
    hbm = pl.BlockSpec(memory_space=pltpu.HBM)
    handed = pl.pallas_call(
        functools.partial(square_kernel, sections),
        out_shape=jax.ShapeDtypeStruct((rows, width), jnp.bfloat16),
        in_specs=[hbm] * 4,
        out_specs=pl.BlockSpec(memory_space=pl.ANY),
        scratch_shapes=[
            pltpu.VMEM((4, 2, 2, rows, kv_width), jnp.bfloat16),
            pltpu.VMEM((pieces, q_width, COLUMNS), jnp.bfloat16),
            pltpu.VMEM((rows, q_width), jnp.bfloat16),
            pltpu.VMEM((heads, HEAD_SIZE + EXTRA, stack), jnp.float32),
            pltpu.VMEM((heads, 1, stack), jnp.float32),
            pltpu.VMEM((rows, q_width), jnp.bfloat16),
            pltpu.VMEM((pieces, rows, COLUMNS), jnp.bfloat16),
            pltpu.VMEM((slots, rows, COLUMNS), jnp.bfloat16),
            pltpu.SemaphoreType.DMA((4, heads)),
            pltpu.SemaphoreType.DMA((4, 2, heads)),
            pltpu.SemaphoreType.DMA((4, heads)),
            pltpu.SemaphoreType.DMA((2, heads)),
            pltpu.SemaphoreType.DMA((2,)),
            pltpu.SemaphoreType.DMA((heads,)),
            pltpu.SemaphoreType.DMA((pieces,)),
            pltpu.SemaphoreType.DMA((pieces,)),
            pltpu.SemaphoreType.DMA((pieces,)),
            pltpu.SemaphoreType.DMA((slots,)),
            pltpu.SemaphoreType.DMA((slots,)),
        ],
        compiler_params=pltpu.CompilerParams(
            collective_id=1, has_side_effects=True, vmem_limit_bytes=VMEM_LIMIT),
    )(*(pltpu.with_memory_space_constraint(each[0], pltpu.HBM) for each in (queries, keys, values, out_weight)))
    return handed[None]


def per_device(sections, spans, *operands):
    if spans == 8:
        return square_device(sections, *operands)
    return general_device(sections, spans, *operands)


def solution(mesh):
    placed = (
        P("pipe", "ctx", None),
        P("pipe", "ctx", None),
        P("pipe", "ctx", None),
        P("pipe", None, None),
    )
    return jax.shard_map(
        functools.partial(per_device, mesh.shape["pipe"], mesh.shape["ctx"]),
        mesh=mesh, in_specs=placed, out_specs=P("pipe", "ctx", None), check_vma=False
    )
```

```python
import functools
import math

import jax
import jax.numpy as jnp
from jax import lax
from jax.experimental import pallas as pl
from jax.experimental.pallas import tpu as pltpu
from jax.sharding import PartitionSpec as P

HEAD_SIZE = 128
COLUMNS = 256
MOVED = 2
HANDED_OVER = ((6, 6), (5, 4), (2, 2), (3, 3))
EXTRA = 16
VMEM_LIMIT = 50 * 1024 * 1024
MESH = pl.DeviceIdType.MESH


def general_kernel(sections, spans, across, q_ref, k_ref, v_ref, w_ref, o_ref, held, weight, stacked, acc, top,
           attended, projected, pair_send, far_send, pass_send, relay_send, span_recv, weight_sem, out_send, out_recv, own_sem, query_sem,
           aside, landed, aside_recv, cross_send, cross_recv, final_send):
    rows, kv_width = k_ref.shape
    q_width = q_ref.shape[1]
    heads = kv_width // HEAD_SIZE
    group = q_width // kv_width
    chips = spans // 2
    pieces = weight.shape[0]
    section = lax.axis_index("pipe")
    me = lax.axis_index("ctx")
    chip, core = me // 2, lax.rem(me, 2)
    line, column = chip // across, lax.rem(chip, across)
    lines = chips // across
    following = lax.rem(section + 1, sections)
    before = lax.rem(section + sections - 1, sections)
    factor = math.log2(math.e) / math.sqrt(HEAD_SIZE)

    barrier = pltpu.get_barrier_semaphore()

    @pl.loop(1, spans)
    def _(step):
        pl.semaphore_signal(barrier, inc=1, device_id={"ctx": lax.rem(me + step, spans)}, device_id_type=MESH)

    for neighbour in (before, following):
        pl.semaphore_signal(barrier, inc=1, device_id={"pipe": neighbour}, device_id_type=MESH)

    def weight_copy(piece):
        return pltpu.make_async_copy(
            w_ref.at[:, pl.ds(pl.multiple_of(piece * COLUMNS, COLUMNS), COLUMNS)],
            weight.at[piece], weight_sem.at[piece])

    def place(owner, side, which):
        return held.at[owner, which, pl.ds(pl.multiple_of(side * rows, rows), rows), :]

    def own_copy(which):
        return pltpu.make_async_copy((k_ref, v_ref)[which], place(chip, core, which), own_sem.at[which])

    def query_copy(head, member):
        at = head * group + member
        return pltpu.make_async_copy(
            q_ref.at[:, at * HEAD_SIZE:(at + 1) * HEAD_SIZE],
            stacked.at[head, member * rows:(member + 1) * rows, :], query_sem.at[at])

    for which in range(2):
        own_copy(which).start()
    for head in range(heads):
        for member in range(group):
            query_copy(head, member).start()

    @pl.loop(0, pieces)
    def _(piece):
        weight_copy(piece).start()

    for which in range(2):
        own_copy(which).wait()

    def pair_copy(which):
        return pltpu.make_async_remote_copy(
            place(chip, core, which), place(chip, core, which), pair_send.at[which],
            span_recv.at[chip, core, which], device_id={"ctx": chip * 2 + 1 - core}, device_id_type=MESH)

    def far_copy(target, which):
        return pltpu.make_async_remote_copy(
            place(chip, core, which), place(chip, core, which), far_send.at[target, which],
            span_recv.at[chip, core, which], device_id={"ctx": target * 2 + core}, device_id_type=MESH)

    def pass_copy(owner, which):
        return pltpu.make_async_remote_copy(
            place(owner, core, which), place(owner, core, which), pass_send.at[owner, which],
            span_recv.at[owner, core, which], device_id={"ctx": chip * 2 + 1 - core}, device_id_type=MESH)

    def relay_copy(owner, target, which):
        return pltpu.make_async_remote_copy(
            place(owner, core, which), place(owner, core, which), relay_send.at[owner, target],
            span_recv.at[owner, core, which], device_id={"ctx": target * 2 + core}, device_id_type=MESH)

    def each_own(act):
        @pl.loop(1, across)
        def _(step):
            other = lax.rem(column + step, across)

            @pl.when((line < lines - 1) | (other > column))
            def _():
                act(line * across + other, 0)

        @pl.loop(line + 1, lines)
        def _(other):
            act(other * across + column, 1)
            act(other * across + column, 0)

        @pl.loop(column + 1, across)
        def _(other):
            act(line * across + other, 1)

    def each_key_source(act):
        @pl.when(line < lines - 1)
        def _():
            @pl.loop(1, across)
            def _(step):
                act(line * across + lax.rem(column + step, across))

    def each_key_relay(owner, act):
        @pl.loop(line + 1, lines)
        def _(other):
            act(owner, other * across + column, 0)

    def each_value_source(act):
        @pl.loop(0, line)
        def _(other):
            act(other * across + column)

    def each_value_relay(owner, act):
        @pl.loop(1, across)
        def _(step):
            act(owner, line * across + lax.rem(column + step, across), 1)

    def wait_span(owner, side, which):
        pltpu.make_async_remote_copy(
            place(owner, side, which), place(owner, side, which), pair_send.at[which],
            span_recv.at[owner, side, which], device_id={"ctx": chip * 2 + 1 - core}, device_id_type=MESH).wait_recv()

    pl.semaphore_wait(barrier, spans + 1)
    for which in range(2):
        pair_copy(which).start()

    each_own(lambda target, which: far_copy(target, which).start())

    for head in range(heads):
        for member in range(group):
            query_copy(head, member).wait()

    def block(owner, head, first):
        lanes = slice(head * HEAD_SIZE, (head + 1) * HEAD_SIZE)
        scores = lax.dot_general(
            held[owner, 0, :, lanes], stacked[head], (((1,), (1,)), ((), ())),
            preferred_element_type=jnp.float32)
        if first:
            key = lax.broadcasted_iota(jnp.int32, scores.shape, 0)
            row = lax.rem(lax.broadcasted_iota(jnp.int32, scores.shape, 1), rows) + core * rows
            scores = jnp.where(key <= row, scores, -1e30)
        highest = jnp.max(scores, axis=0, keepdims=True)
        if not first:
            previous = top[head]
            highest = jnp.maximum(previous, highest)
            rescale = jnp.exp2((previous - highest) * factor)
        top[head] = highest
        weights = jnp.exp2((scores - highest) * factor).astype(jnp.bfloat16)
        values = held[owner, 1, :, lanes].T
        values = jnp.concatenate([values, jnp.ones((EXTRA, values.shape[1]), values.dtype)], axis=0)
        summed = jnp.dot(values, weights, preferred_element_type=jnp.float32)
        if first:
            acc[head] = summed
        else:
            acc[head] = acc[head] * rescale + summed

    for which in range(2):
        wait_span(chip, 1 - core, which)

    for head in range(heads):
        block(chip, head, True)

    def relay_keys(owner):
        wait_span(owner, core, 0)
        each_key_relay(owner, lambda *at: relay_copy(*at).start())

        @pl.when(owner < chip)
        def _():
            pass_copy(owner, 0).start()

    def relay_values(owner):
        wait_span(owner, core, 1)
        each_value_relay(owner, lambda *at: relay_copy(*at).start())
        pass_copy(owner, 1).start()

    each_value_source(relay_values)
    each_key_source(relay_keys)

    @pl.loop(0, chip)
    def _(step):
        owner = chip - 1 - step

        @pl.when((owner // across != line) | (line == lines - 1))
        def _():
            wait_span(owner, core, 0)
            pass_copy(owner, 0).start()

        @pl.when((lax.rem(owner, across) != column) | (owner // across == line))
        def _():
            wait_span(owner, core, 1)
            pass_copy(owner, 1).start()

        for which in range(2):
            wait_span(owner, 1 - core, which)

        for head in range(heads):
            block(owner, head, False)

    for head in range(heads):
        for member in range(group):
            part = acc[head, :, member * rows:(member + 1) * rows]
            attended[:, (head * group + member) * HEAD_SIZE:(head * group + member + 1) * HEAD_SIZE] = (
                part[:HEAD_SIZE] / part[HEAD_SIZE:HEAD_SIZE + 1]).T.astype(jnp.bfloat16)

    def out_copy(piece):
        return pltpu.make_async_remote_copy(
            projected.at[piece],
            o_ref.at[:, pl.ds(pl.multiple_of(piece * COLUMNS, COLUMNS), COLUMNS)],
            out_send.at[piece], out_recv.at[piece], device_id={"pipe": following}, device_id_type=MESH)

    late = chips - chips // 2
    heavy = chip >= late
    slot_of = lax.rem(chip + 2 * chips - late, 2)

    def aside_copy(piece):
        return pltpu.make_async_remote_copy(
            projected.at[piece], aside.at[slot_of, piece], out_send.at[piece],
            aside_recv.at[slot_of, piece],
            device_id={"ctx": (chip - late) // 2 * 2 + core}, device_id_type=MESH)

    def cross_copy(slot, piece):
        return pltpu.make_async_remote_copy(
            aside.at[slot, piece], landed.at[slot, piece], cross_send.at[slot, piece],
            cross_recv.at[slot, piece], device_id={"pipe": following}, device_id_type=MESH)

    def final_copy(slot, piece):
        return pltpu.make_async_remote_copy(
            landed.at[slot, piece],
            o_ref.at[:, pl.ds(pl.multiple_of(piece * COLUMNS, COLUMNS), COLUMNS)],
            final_send.at[slot, piece], out_recv.at[piece],
            device_id={"ctx": (late + chip * 2 + slot) * 2 + core}, device_id_type=MESH)

    def each_carried(act):
        @pl.loop(0, jnp.clip(chips // 2 - chip * 2, 0, 2))
        def _(slot):
            @pl.loop(0, MOVED)
            def _(piece):
                act(slot, piece)

    def carry(slot, piece):
        pltpu.make_async_remote_copy(
            aside.at[slot, piece], aside.at[slot, piece], cross_send.at[slot, piece],
            aside_recv.at[slot, piece], device_id={"pipe": following}, device_id_type=MESH).wait_recv()
        cross_copy(slot, piece).start()

    def deliver(slot, piece):
        cross_copy(slot, piece).wait_recv()
        final_copy(slot, piece).start()

    def settle(slot, piece):
        cross_copy(slot, piece).wait_send()
        final_copy(slot, piece).wait_send()

    @pl.loop(0, pieces)
    def _(piece):
        weight_copy(piece).wait()
        projected[piece] = jnp.dot(
            attended[...], weight[piece], preferred_element_type=jnp.float32).astype(jnp.bfloat16)

        @pl.when(heavy & (piece < MOVED))
        def _():
            aside_copy(piece).start()

        @pl.when(jnp.logical_not(heavy & (piece < MOVED)))
        def _():
            out_copy(piece).start()

    each_carried(carry)
    each_carried(deliver)

    for which in range(2):
        pair_copy(which).wait_send()

    each_own(lambda target, which: far_copy(target, which).wait_send())
    each_key_source(lambda owner: each_key_relay(
        owner, lambda *at: relay_copy(*at).wait_send()))
    each_value_source(lambda owner: each_value_relay(
        owner, lambda *at: relay_copy(*at).wait_send()))

    @pl.loop(0, chip)
    def _(owner):
        for which in range(2):
            pass_copy(owner, which).wait_send()

    each_carried(settle)

    @pl.loop(0, pieces)
    def _(piece):
        out_copy(piece).wait()


def square_kernel(sections, q_ref, k_ref, v_ref, w_ref, o_ref, held, weight, query, acc, top, attended, projected, aside,
                  far_send, span_recv, pass_send, relay_send, own_sem, query_sem, weight_sem, out_send, out_recv,
                  aside_recv, deliver_send):
    rows, kv_width = k_ref.shape
    heads = kv_width // HEAD_SIZE
    group = q_ref.shape[1] // kv_width
    pieces = weight.shape[0]
    section = lax.axis_index("pipe")
    me = lax.axis_index("ctx")
    chip, core = me // 2, lax.rem(me, 2)
    sibling = chip * 2 + 1 - core
    beside = (chip + 1 - 2 * lax.rem(chip, 2)) * 2 + core
    across = lax.rem(chip + 2, 4) * 2 + core
    opposite = (3 - chip) * 2 + core
    following = lax.rem(section + 1, sections)
    before = lax.rem(section + sections - 1, sections)
    factor = math.log2(math.e) / math.sqrt(HEAD_SIZE)

    barrier = pltpu.get_barrier_semaphore()
    for other in (sibling, beside, across, opposite):
        pl.semaphore_signal(barrier, inc=1, device_id={"ctx": other}, device_id_type=MESH)
    for neighbour in (before, following):
        pl.semaphore_signal(barrier, inc=1, device_id={"pipe": neighbour}, device_id_type=MESH)

    pl.semaphore_signal(
        barrier, inc=1, device_id={"pipe": before, "ctx": jnp.where(chip > 0, core, 2 + core)}, device_id_type=MESH)

    def lanes(head):
        return slice(head * HEAD_SIZE, (head + 1) * HEAD_SIZE)

    def own_copy(which):
        return pltpu.make_async_copy((k_ref, v_ref)[which], held.at[chip, core, which], own_sem.at[which])

    def query_copy(head):
        wide = group * HEAD_SIZE
        return pltpu.make_async_copy(
            q_ref.at[:, head * wide:(head + 1) * wide], query.at[:, head * wide:(head + 1) * wide], query_sem.at[head])

    def weight_copy(piece):
        return pltpu.make_async_copy(
            w_ref.at[:, pl.ds(pl.multiple_of(piece * COLUMNS, COLUMNS), COLUMNS)],
            weight.at[piece], weight_sem.at[piece])

    for which in range(2):
        own_copy(which).start()
    for head in range(heads):
        query_copy(head).start()

    def at_head(head):
        return pl.ds(pl.multiple_of(head * HEAD_SIZE, HEAD_SIZE), HEAD_SIZE)

    def span_copy(owner, head, side, send_sem, target):
        chunk = held.at[owner, side, :, :, at_head(head)]
        return pltpu.make_async_remote_copy(
            chunk, chunk, send_sem, span_recv.at[owner, side, head], device_id={"ctx": target}, device_id_type=MESH)

    def first_copy(head, way, target):
        return span_copy(chip, head, core, far_send.at[way, head], target)

    def early_copy(head, way, target):
        for which in range(2):
            pltpu.make_async_remote_copy(
                (k_ref, v_ref)[which].at[:, lanes(head)], held.at[chip, core, which, :, lanes(head)],
                far_send.at[way, head], span_recv.at[chip, core, head],
                device_id={"ctx": target}, device_id_type=MESH).start()

    def each_far(act):
        for step in range(heads):
            head = (step + heads // 2) % heads

            @pl.when((chip == 2) | ((chip == 0) & (step < heads // 2)))
            def _():
                act(step, 1, beside)

            @pl.when(chip == 0)
            def _():
                act(head, 2, across)

            @pl.when(chip == 1)
            def _():
                act(step, 2, across)

        @pl.when(chip == 1)
        def _():
            act(heads - 1, 3, opposite)

    def each_pair(act):
        @pl.when(core == 0)
        def _():
            for head in range(heads):
                act(head, 0, sibling)

    pl.semaphore_wait(barrier, jnp.where(chip == 0, 9, jnp.where(chip == 1, 7, 6)))

    each_far(early_copy)
    for which in range(2):
        own_copy(which).wait()
    each_pair(lambda *way: first_copy(*way).start())

    def stacked(head):
        return jnp.concatenate(
            [query[:, at_head(head * group + member)] for member in range(group)], axis=0)

    half = group * rows // 2
    halves = [slice(part * half, (part + 1) * half) for part in range(2)]

    def block(keys, values, head, first):
        values = values.T
        values = jnp.concatenate([values, jnp.ones((EXTRA, values.shape[1]), values.dtype)], axis=0)
        queries = stacked(head)
        before_it = [None if first else (top[head, :, part], acc[head, :, part]) for part in halves]
        scores = [lax.dot_general(
            keys, queries[part], (((1,), (1,)), ((), ())), preferred_element_type=jnp.float32) for part in halves]
        if first:
            key = lax.broadcasted_iota(jnp.int32, scores[0].shape, 0)
            row = lax.rem(lax.broadcasted_iota(jnp.int32, scores[0].shape, 1), rows)
            scores = [jnp.where(key <= row, each, -1e30) for each in scores]
        highest = [jnp.max(each, axis=0, keepdims=True) for each in scores]
        if not first:
            highest = [jnp.maximum(each[0], now) for each, now in zip(before_it, highest)]
        results = []
        for each, now, known in zip(scores, highest, before_it):
            weights = jnp.exp2((each - now) * factor).astype(jnp.bfloat16)
            summed = jnp.dot(values, weights, preferred_element_type=jnp.float32)
            if not first:
                summed = known[1] * jnp.exp2((known[0] - now) * factor) + summed
            results.append(summed)
        for part, now, summed in zip(halves, highest, results):
            top[head, :, part] = now
            acc[head, :, part] = summed

    for head in range(heads):
        query_copy(head).wait()

    @pl.loop(0, pieces)
    def _(piece):
        weight_copy(piece).start()

    for head in range(heads):
        block(held[chip, core, 0, :, lanes(head)], held[chip, core, 1, :, lanes(head)], head, True)

    @pl.when(core == 1)
    def _():
        for head in range(heads):
            span_copy(chip, head, 0, far_send.at[0, head], sibling).wait_recv()
        for head in range(heads):
            block(held[chip, 0, 0, :, lanes(head)], held[chip, 0, 1, :, lanes(head)], head, False)

    moved, base = 0, 0
    slots = [[], []]
    for side in range(2):
        for origin in (0, 3, 1, 2):
            count = HANDED_OVER[origin][side]
            here = (chip == origin) & (core == side)
            moved = jnp.where(here, count, moved)
            if origin > 0:
                base = jnp.where(here, len(slots[side]), base)
                slots[side] += [(origin, 2 * each + 1) for each in range(count)]
    fed = jnp.where(chip == 1, jnp.where(core == 0, *HANDED_OVER[0]), 0)

    def columns(piece):
        return o_ref.at[:, pl.ds(pl.multiple_of(piece * COLUMNS, COLUMNS), COLUMNS)]

    def out_copy(piece):
        return pltpu.make_async_remote_copy(
            projected.at[piece], columns(piece), out_send.at[piece], out_recv.at[piece],
            device_id={"pipe": following}, device_id_type=MESH)

    def aside_copy(piece):
        slot = base + piece // 2
        return pltpu.make_async_remote_copy(
            projected.at[piece], aside.at[slot], out_send.at[piece], aside_recv.at[slot],
            device_id={"ctx": jnp.where(chip == 0, 2 + core, core)}, device_id_type=MESH)

    def deliver_copy(slot, origin, piece):
        return pltpu.make_async_remote_copy(
            aside.at[slot], columns(piece), deliver_send.at[slot], out_recv.at[piece],
            device_id={"pipe": following, "ctx": origin * 2 + core}, device_id_type=MESH)

    def each_delivered(act):
        for side in range(2):
            @pl.when((chip == 0) & (core == side))
            def _():
                for slot, place in enumerate(slots[side]):
                    act(slot, *place)

    def deliver(slot, origin, piece):
        pltpu.make_async_remote_copy(
            aside.at[slot], aside.at[slot], deliver_send.at[slot], aside_recv.at[slot],
            device_id={"ctx": sibling}, device_id_type=MESH).wait_recv()
        deliver_copy(slot, origin, piece).start()

    def forward(slot):
        deliver(slot, 0, 2 * slot + 1)

    steps = chip * heads

    def at(step):
        later = step - 2 * heads
        owner_last = jnp.where(later < 0, 1 + lax.rem(step, 2), 0)
        head_last = jnp.where(later < 0, step // 2, (1 - lax.rem(later, 2)) * (heads // 2) + later // 2)
        own_third = (step == 0) | ((step > 1) & (lax.rem(step, 2) == 1))
        head_third = jnp.where(step == 1, heads - 1, jnp.where(own_third, lax.rem(step // 2 + heads // 2, heads), step // 2 - 1))
        owner = jnp.where(chip == 3, owner_last, jnp.where((chip == 2) & jnp.logical_not(own_third), 1, 0))
        head = jnp.where(chip == 3, head_last, jnp.where(chip == 2, head_third, step))
        return owner, head

    def relayed(owner, head):
        late = head >= heads // 2
        last = ((owner == 1) & (head < heads - 1)) | ((owner == 0) & late)
        return ((chip == 1) & jnp.logical_not(late)) | ((chip == 2) & (owner == 0) & late) | ((chip == 3) & last)

    def relay_copy(owner, head):
        target = jnp.where((chip == 1) | ((chip == 3) & (owner == 0)), across, beside)
        return span_copy(owner, head, core, relay_send.at[owner, head], target)

    def arrive(step):
        owner, head = at(step)
        span_copy(owner, head, core, pass_send.at[owner, head], sibling).wait_recv()

        span_copy(owner, head, core, pass_send.at[owner, head], sibling).start()

        @pl.when(relayed(owner, head))
        def _():
            relay_copy(owner, head).start()

    @pl.when(chip > 0)
    def _():
        arrive(0)

    @pl.loop(0, steps)
    def _(step):
        @pl.when((step + 1 < steps) & ((chip > 1) | (step == 0)))
        def _():
            arrive(step + 1)

        owner, head = at(step)
        span_copy(owner, head, 1 - core, pass_send.at[owner, head], sibling).wait_recv()
        keys = held[owner, :, 0, :, at_head(head)].reshape(2 * rows, HEAD_SIZE)
        values = held[owner, :, 1, :, at_head(head)].reshape(2 * rows, HEAD_SIZE)
        block(keys, values, head, False)

        @pl.when((chip == 1) & (step == 0))
        def _():
            forward(0)

        @pl.when((chip == 1) & (step == 1))
        def _():
            @pl.loop(1, fed - 1)
            def _(slot):
                forward(slot)

            arrive(step + 1)
            arrive(step + 2)

        @pl.when((chip == 1) & (step == 2))
        def _():
            forward(fed - 1)

    for head in range(heads):
        for member in range(group):
            part = acc[head, :, member * rows:(member + 1) * rows]
            attended[:, lanes(head * group + member)] = (
                part[:HEAD_SIZE] / part[HEAD_SIZE:HEAD_SIZE + 1]).T.astype(jnp.bfloat16)

    @pl.loop(0, pieces)
    def _(piece):
        weight_copy(piece).wait()
        projected[piece] = jnp.dot(
            attended[...], weight[piece], preferred_element_type=jnp.float32).astype(jnp.bfloat16)

        handed = (lax.rem(piece, 2) == 1) & (piece < 2 * moved)

        @pl.when(jnp.logical_not(handed))
        def _():
            out_copy(piece).start()

        @pl.when(handed)
        def _():
            aside_copy(piece).start()

    each_delivered(deliver)

    each_far(lambda *way: first_copy(*way).wait_send())
    each_pair(lambda *way: first_copy(*way).wait_send())

    @pl.loop(0, steps)
    def _(step):
        owner, head = at(step)
        span_copy(owner, head, core, pass_send.at[owner, head], sibling).wait_send()

        @pl.when(relayed(owner, head))
        def _():
            relay_copy(owner, head).wait_send()

    each_delivered(lambda *place: deliver_copy(*place).wait_send())

    @pl.loop(0, fed)
    def _(slot):
        deliver_copy(slot, 0, 2 * slot + 1).wait_send()

    @pl.loop(0, pieces)
    def _(piece):
        out_copy(piece).wait()


def general_device(sections, spans, queries, keys, values, out_weight):
    rows, q_width = queries.shape[1:]
    kv_width = keys.shape[2]
    width = out_weight.shape[2]
    heads = kv_width // HEAD_SIZE
    stack = q_width // kv_width * rows
    pieces = width // COLUMNS
    chips = spans // 2
    across = math.isqrt(chips)
    across = across if chips % across == 0 else chips
    hbm = pl.BlockSpec(memory_space=pltpu.HBM)
    handed = pl.pallas_call(
        functools.partial(general_kernel, sections, spans, across),
        out_shape=jax.ShapeDtypeStruct((rows, width), jnp.bfloat16),
        in_specs=[hbm] * 4,
        out_specs=pl.BlockSpec(memory_space=pl.ANY),
        scratch_shapes=[
            pltpu.VMEM((chips, 2, 2 * rows, kv_width), jnp.bfloat16),
            pltpu.VMEM((pieces, q_width, COLUMNS), jnp.bfloat16),
            pltpu.VMEM((heads, stack, HEAD_SIZE), jnp.bfloat16),
            pltpu.VMEM((heads, HEAD_SIZE + EXTRA, stack), jnp.float32),
            pltpu.VMEM((heads, 1, stack), jnp.float32),
            pltpu.VMEM((rows, q_width), jnp.bfloat16),
            pltpu.VMEM((pieces, rows, COLUMNS), jnp.bfloat16),
            pltpu.SemaphoreType.DMA((2,)),
            pltpu.SemaphoreType.DMA((chips, 2)),
            pltpu.SemaphoreType.DMA((chips, 2)),
            pltpu.SemaphoreType.DMA((chips, chips)),
            pltpu.SemaphoreType.DMA((chips, 2, 2)),
            pltpu.SemaphoreType.DMA((pieces,)),
            pltpu.SemaphoreType.DMA((pieces,)),
            pltpu.SemaphoreType.DMA((pieces,)),
            pltpu.SemaphoreType.DMA((2,)),
            pltpu.SemaphoreType.DMA((q_width // HEAD_SIZE,)),
            pltpu.VMEM((2, MOVED, rows, COLUMNS), jnp.bfloat16),
            pltpu.VMEM((2, MOVED, rows, COLUMNS), jnp.bfloat16),
            pltpu.SemaphoreType.DMA((2, MOVED)),
            pltpu.SemaphoreType.DMA((2, MOVED)),
            pltpu.SemaphoreType.DMA((2, MOVED)),
            pltpu.SemaphoreType.DMA((2, MOVED)),
        ],
        compiler_params=pltpu.CompilerParams(
            collective_id=0, has_side_effects=True, vmem_limit_bytes=VMEM_LIMIT),
    )(*(pltpu.with_memory_space_constraint(each[0], pltpu.HBM) for each in (queries, keys, values, out_weight)))
    return handed[None]


def square_device(sections, queries, keys, values, out_weight):
    rows, q_width = queries.shape[1:]
    kv_width = keys.shape[2]
    width = out_weight.shape[2]
    heads = kv_width // HEAD_SIZE
    stack = q_width // kv_width * rows
    pieces = width // COLUMNS
    slots = max(max(HANDED_OVER[0]), *(sum(counts[side] for counts in HANDED_OVER[1:]) for side in range(2)))
    hbm = pl.BlockSpec(memory_space=pltpu.HBM)
    handed = pl.pallas_call(
        functools.partial(square_kernel, sections),
        out_shape=jax.ShapeDtypeStruct((rows, width), jnp.bfloat16),
        in_specs=[hbm] * 4,
        out_specs=pl.BlockSpec(memory_space=pl.ANY),
        scratch_shapes=[
            pltpu.VMEM((4, 2, 2, rows, kv_width), jnp.bfloat16),
            pltpu.VMEM((pieces, q_width, COLUMNS), jnp.bfloat16),
            pltpu.VMEM((rows, q_width), jnp.bfloat16),
            pltpu.VMEM((heads, HEAD_SIZE + EXTRA, stack), jnp.float32),
            pltpu.VMEM((heads, 1, stack), jnp.float32),
            pltpu.VMEM((rows, q_width), jnp.bfloat16),
            pltpu.VMEM((pieces, rows, COLUMNS), jnp.bfloat16),
            pltpu.VMEM((slots, rows, COLUMNS), jnp.bfloat16),
            pltpu.SemaphoreType.DMA((4, heads)),
            pltpu.SemaphoreType.DMA((4, 2, heads)),
            pltpu.SemaphoreType.DMA((4, heads)),
            pltpu.SemaphoreType.DMA((2, heads)),
            pltpu.SemaphoreType.DMA((2,)),
            pltpu.SemaphoreType.DMA((heads,)),
            pltpu.SemaphoreType.DMA((pieces,)),
            pltpu.SemaphoreType.DMA((pieces,)),
            pltpu.SemaphoreType.DMA((pieces,)),
            pltpu.SemaphoreType.DMA((slots,)),
            pltpu.SemaphoreType.DMA((slots,)),
        ],
        compiler_params=pltpu.CompilerParams(
            collective_id=1, has_side_effects=True, vmem_limit_bytes=VMEM_LIMIT),
    )(*(pltpu.with_memory_space_constraint(each[0], pltpu.HBM) for each in (queries, keys, values, out_weight)))
    return handed[None]


def per_device(sections, spans, *operands):
    if spans == 8:
        return square_device(sections, *operands)
    return general_device(sections, spans, *operands)


def solution(mesh):
    placed = (
        P("pipe", "ctx", None),
        P("pipe", "ctx", None),
        P("pipe", "ctx", None),
        P("pipe", None, None),
    )
    return jax.shard_map(
        functools.partial(per_device, mesh.shape["pipe"], mesh.shape["ctx"]),
        mesh=mesh, in_specs=placed, out_specs=P("pipe", "ctx", None), check_vma=False
    )
```

```python
import functools
import math

import jax
import jax.numpy as jnp
from jax import lax
from jax.experimental import pallas as pl
from jax.experimental.pallas import tpu as pltpu
from jax.sharding import PartitionSpec as P

HEAD_SIZE = 128
COLUMNS = 256
MOVED = 2
HANDED_OVER = ((6, 6), (4, 5), (2, 2), (3, 3))
EXTRA = 16
VMEM_LIMIT = 50 * 1024 * 1024
MESH = pl.DeviceIdType.MESH


def general_kernel(sections, spans, across, q_ref, k_ref, v_ref, w_ref, o_ref, held, weight, stacked, acc, top,
           attended, projected, pair_send, far_send, pass_send, relay_send, span_recv, weight_sem, out_send, out_recv, own_sem, query_sem,
           aside, landed, aside_recv, cross_send, cross_recv, final_send):
    rows, kv_width = k_ref.shape
    q_width = q_ref.shape[1]
    heads = kv_width // HEAD_SIZE
    group = q_width // kv_width
    chips = spans // 2
    pieces = weight.shape[0]
    section = lax.axis_index("pipe")
    me = lax.axis_index("ctx")
    chip, core = me // 2, lax.rem(me, 2)
    line, column = chip // across, lax.rem(chip, across)
    lines = chips // across
    following = lax.rem(section + 1, sections)
    before = lax.rem(section + sections - 1, sections)
    factor = math.log2(math.e) / math.sqrt(HEAD_SIZE)

    barrier = pltpu.get_barrier_semaphore()

    @pl.loop(1, spans)
    def _(step):
        pl.semaphore_signal(barrier, inc=1, device_id={"ctx": lax.rem(me + step, spans)}, device_id_type=MESH)

    for neighbour in (before, following):
        pl.semaphore_signal(barrier, inc=1, device_id={"pipe": neighbour}, device_id_type=MESH)

    def weight_copy(piece):
        return pltpu.make_async_copy(
            w_ref.at[:, pl.ds(pl.multiple_of(piece * COLUMNS, COLUMNS), COLUMNS)],
            weight.at[piece], weight_sem.at[piece])

    def place(owner, side, which):
        return held.at[owner, which, pl.ds(pl.multiple_of(side * rows, rows), rows), :]

    def own_copy(which):
        return pltpu.make_async_copy((k_ref, v_ref)[which], place(chip, core, which), own_sem.at[which])

    def query_copy(head, member):
        at = head * group + member
        return pltpu.make_async_copy(
            q_ref.at[:, at * HEAD_SIZE:(at + 1) * HEAD_SIZE],
            stacked.at[head, member * rows:(member + 1) * rows, :], query_sem.at[at])

    for which in range(2):
        own_copy(which).start()
    for head in range(heads):
        for member in range(group):
            query_copy(head, member).start()

    @pl.loop(0, pieces)
    def _(piece):
        weight_copy(piece).start()

    for which in range(2):
        own_copy(which).wait()

    def pair_copy(which):
        return pltpu.make_async_remote_copy(
            place(chip, core, which), place(chip, core, which), pair_send.at[which],
            span_recv.at[chip, core, which], device_id={"ctx": chip * 2 + 1 - core}, device_id_type=MESH)

    def far_copy(target, which):
        return pltpu.make_async_remote_copy(
            place(chip, core, which), place(chip, core, which), far_send.at[target, which],
            span_recv.at[chip, core, which], device_id={"ctx": target * 2 + core}, device_id_type=MESH)

    def pass_copy(owner, which):
        return pltpu.make_async_remote_copy(
            place(owner, core, which), place(owner, core, which), pass_send.at[owner, which],
            span_recv.at[owner, core, which], device_id={"ctx": chip * 2 + 1 - core}, device_id_type=MESH)

    def relay_copy(owner, target, which):
        return pltpu.make_async_remote_copy(
            place(owner, core, which), place(owner, core, which), relay_send.at[owner, target],
            span_recv.at[owner, core, which], device_id={"ctx": target * 2 + core}, device_id_type=MESH)

    def each_own(act):
        @pl.loop(1, across)
        def _(step):
            other = lax.rem(column + step, across)

            @pl.when((line < lines - 1) | (other > column))
            def _():
                act(line * across + other, 0)

        @pl.loop(line + 1, lines)
        def _(other):
            act(other * across + column, 1)
            act(other * across + column, 0)

        @pl.loop(column + 1, across)
        def _(other):
            act(line * across + other, 1)

    def each_key_source(act):
        @pl.when(line < lines - 1)
        def _():
            @pl.loop(1, across)
            def _(step):
                act(line * across + lax.rem(column + step, across))

    def each_key_relay(owner, act):
        @pl.loop(line + 1, lines)
        def _(other):
            act(owner, other * across + column, 0)

    def each_value_source(act):
        @pl.loop(0, line)
        def _(other):
            act(other * across + column)

    def each_value_relay(owner, act):
        @pl.loop(1, across)
        def _(step):
            act(owner, line * across + lax.rem(column + step, across), 1)

    def wait_span(owner, side, which):
        pltpu.make_async_remote_copy(
            place(owner, side, which), place(owner, side, which), pair_send.at[which],
            span_recv.at[owner, side, which], device_id={"ctx": chip * 2 + 1 - core}, device_id_type=MESH).wait_recv()

    pl.semaphore_wait(barrier, spans + 1)
    for which in range(2):
        pair_copy(which).start()

    each_own(lambda target, which: far_copy(target, which).start())

    for head in range(heads):
        for member in range(group):
            query_copy(head, member).wait()

    def block(owner, head, first):
        lanes = slice(head * HEAD_SIZE, (head + 1) * HEAD_SIZE)
        scores = lax.dot_general(
            held[owner, 0, :, lanes], stacked[head], (((1,), (1,)), ((), ())),
            preferred_element_type=jnp.float32)
        if first:
            key = lax.broadcasted_iota(jnp.int32, scores.shape, 0)
            row = lax.rem(lax.broadcasted_iota(jnp.int32, scores.shape, 1), rows) + core * rows
            scores = jnp.where(key <= row, scores, -1e30)
        highest = jnp.max(scores, axis=0, keepdims=True)
        if not first:
            previous = top[head]
            highest = jnp.maximum(previous, highest)
            rescale = jnp.exp2((previous - highest) * factor)
        top[head] = highest
        weights = jnp.exp2((scores - highest) * factor).astype(jnp.bfloat16)
        values = held[owner, 1, :, lanes].T
        values = jnp.concatenate([values, jnp.ones((EXTRA, values.shape[1]), values.dtype)], axis=0)
        summed = jnp.dot(values, weights, preferred_element_type=jnp.float32)
        if first:
            acc[head] = summed
        else:
            acc[head] = acc[head] * rescale + summed

    for which in range(2):
        wait_span(chip, 1 - core, which)

    for head in range(heads):
        block(chip, head, True)

    def relay_keys(owner):
        wait_span(owner, core, 0)
        each_key_relay(owner, lambda *at: relay_copy(*at).start())

        @pl.when(owner < chip)
        def _():
            pass_copy(owner, 0).start()

    def relay_values(owner):
        wait_span(owner, core, 1)
        each_value_relay(owner, lambda *at: relay_copy(*at).start())
        pass_copy(owner, 1).start()

    each_value_source(relay_values)
    each_key_source(relay_keys)

    @pl.loop(0, chip)
    def _(step):
        owner = chip - 1 - step

        @pl.when((owner // across != line) | (line == lines - 1))
        def _():
            wait_span(owner, core, 0)
            pass_copy(owner, 0).start()

        @pl.when((lax.rem(owner, across) != column) | (owner // across == line))
        def _():
            wait_span(owner, core, 1)
            pass_copy(owner, 1).start()

        for which in range(2):
            wait_span(owner, 1 - core, which)

        for head in range(heads):
            block(owner, head, False)

    for head in range(heads):
        for member in range(group):
            part = acc[head, :, member * rows:(member + 1) * rows]
            attended[:, (head * group + member) * HEAD_SIZE:(head * group + member + 1) * HEAD_SIZE] = (
                part[:HEAD_SIZE] / part[HEAD_SIZE:HEAD_SIZE + 1]).T.astype(jnp.bfloat16)

    def out_copy(piece):
        return pltpu.make_async_remote_copy(
            projected.at[piece],
            o_ref.at[:, pl.ds(pl.multiple_of(piece * COLUMNS, COLUMNS), COLUMNS)],
            out_send.at[piece], out_recv.at[piece], device_id={"pipe": following}, device_id_type=MESH)

    late = chips - chips // 2
    heavy = chip >= late
    slot_of = lax.rem(chip + 2 * chips - late, 2)

    def aside_copy(piece):
        return pltpu.make_async_remote_copy(
            projected.at[piece], aside.at[slot_of, piece], out_send.at[piece],
            aside_recv.at[slot_of, piece],
            device_id={"ctx": (chip - late) // 2 * 2 + core}, device_id_type=MESH)

    def cross_copy(slot, piece):
        return pltpu.make_async_remote_copy(
            aside.at[slot, piece], landed.at[slot, piece], cross_send.at[slot, piece],
            cross_recv.at[slot, piece], device_id={"pipe": following}, device_id_type=MESH)

    def final_copy(slot, piece):
        return pltpu.make_async_remote_copy(
            landed.at[slot, piece],
            o_ref.at[:, pl.ds(pl.multiple_of(piece * COLUMNS, COLUMNS), COLUMNS)],
            final_send.at[slot, piece], out_recv.at[piece],
            device_id={"ctx": (late + chip * 2 + slot) * 2 + core}, device_id_type=MESH)

    def each_carried(act):
        @pl.loop(0, jnp.clip(chips // 2 - chip * 2, 0, 2))
        def _(slot):
            @pl.loop(0, MOVED)
            def _(piece):
                act(slot, piece)

    def carry(slot, piece):
        pltpu.make_async_remote_copy(
            aside.at[slot, piece], aside.at[slot, piece], cross_send.at[slot, piece],
            aside_recv.at[slot, piece], device_id={"pipe": following}, device_id_type=MESH).wait_recv()
        cross_copy(slot, piece).start()

    def deliver(slot, piece):
        cross_copy(slot, piece).wait_recv()
        final_copy(slot, piece).start()

    def settle(slot, piece):
        cross_copy(slot, piece).wait_send()
        final_copy(slot, piece).wait_send()

    @pl.loop(0, pieces)
    def _(piece):
        weight_copy(piece).wait()
        projected[piece] = jnp.dot(
            attended[...], weight[piece], preferred_element_type=jnp.float32).astype(jnp.bfloat16)

        @pl.when(heavy & (piece < MOVED))
        def _():
            aside_copy(piece).start()

        @pl.when(jnp.logical_not(heavy & (piece < MOVED)))
        def _():
            out_copy(piece).start()

    each_carried(carry)
    each_carried(deliver)

    for which in range(2):
        pair_copy(which).wait_send()

    each_own(lambda target, which: far_copy(target, which).wait_send())
    each_key_source(lambda owner: each_key_relay(
        owner, lambda *at: relay_copy(*at).wait_send()))
    each_value_source(lambda owner: each_value_relay(
        owner, lambda *at: relay_copy(*at).wait_send()))

    @pl.loop(0, chip)
    def _(owner):
        for which in range(2):
            pass_copy(owner, which).wait_send()

    each_carried(settle)

    @pl.loop(0, pieces)
    def _(piece):
        out_copy(piece).wait()


def square_kernel(sections, q_ref, k_ref, v_ref, w_ref, o_ref, held, weight, query, acc, top, attended, projected, aside,
                  far_send, span_recv, pass_send, relay_send, own_sem, query_sem, weight_sem, out_send, out_recv,
                  aside_recv, deliver_send):
    rows, kv_width = k_ref.shape
    heads = kv_width // HEAD_SIZE
    group = q_ref.shape[1] // kv_width
    pieces = weight.shape[0]
    section = lax.axis_index("pipe")
    me = lax.axis_index("ctx")
    chip, core = me // 2, lax.rem(me, 2)
    sibling = chip * 2 + 1 - core
    beside = (chip + 1 - 2 * lax.rem(chip, 2)) * 2 + core
    across = lax.rem(chip + 2, 4) * 2 + core
    opposite = (3 - chip) * 2 + core
    following = lax.rem(section + 1, sections)
    before = lax.rem(section + sections - 1, sections)
    factor = math.log2(math.e) / math.sqrt(HEAD_SIZE)

    barrier = pltpu.get_barrier_semaphore()
    for other in (sibling, beside, across, opposite):
        pl.semaphore_signal(barrier, inc=1, device_id={"ctx": other}, device_id_type=MESH)
    for neighbour in (before, following):
        pl.semaphore_signal(barrier, inc=1, device_id={"pipe": neighbour}, device_id_type=MESH)

    pl.semaphore_signal(
        barrier, inc=1, device_id={"pipe": before, "ctx": jnp.where(chip > 0, core, 2 + core)}, device_id_type=MESH)

    def lanes(head):
        return slice(head * HEAD_SIZE, (head + 1) * HEAD_SIZE)

    def own_copy(which):
        return pltpu.make_async_copy((k_ref, v_ref)[which], held.at[chip, core, which], own_sem.at[which])

    def query_copy(head):
        wide = group * HEAD_SIZE
        return pltpu.make_async_copy(
            q_ref.at[:, head * wide:(head + 1) * wide], query.at[:, head * wide:(head + 1) * wide], query_sem.at[head])

    def weight_copy(piece):
        return pltpu.make_async_copy(
            w_ref.at[:, pl.ds(pl.multiple_of(piece * COLUMNS, COLUMNS), COLUMNS)],
            weight.at[piece], weight_sem.at[piece])

    for which in range(2):
        own_copy(which).start()
    for head in range(heads):
        query_copy(head).start()

    def at_head(head):
        return pl.ds(pl.multiple_of(head * HEAD_SIZE, HEAD_SIZE), HEAD_SIZE)

    def span_copy(owner, head, side, send_sem, target):
        chunk = held.at[owner, side, :, :, at_head(head)]
        return pltpu.make_async_remote_copy(
            chunk, chunk, send_sem, span_recv.at[owner, side, head], device_id={"ctx": target}, device_id_type=MESH)

    def first_copy(head, way, target):
        return span_copy(chip, head, core, far_send.at[way, head], target)

    def early_copy(head, way, target):
        for which in range(2):
            pltpu.make_async_remote_copy(
                (k_ref, v_ref)[which].at[:, lanes(head)], held.at[chip, core, which, :, lanes(head)],
                far_send.at[way, head], span_recv.at[chip, core, head],
                device_id={"ctx": target}, device_id_type=MESH).start()

    def each_far(act):
        for step in range(heads):
            head = (step + heads // 2) % heads

            @pl.when((chip == 2) | ((chip == 0) & (step < heads // 2)))
            def _():
                act(step, 1, beside)

            @pl.when(chip == 0)
            def _():
                act(head, 2, across)

            @pl.when(chip == 1)
            def _():
                act(step, 2, across)

        @pl.when(chip == 1)
        def _():
            act(heads - 1, 3, opposite)

    def each_pair(act):
        @pl.when(core == 0)
        def _():
            for head in range(heads):
                act(head, 0, sibling)

    pl.semaphore_wait(barrier, jnp.where(chip == 0, 9, jnp.where(chip == 1, 7, 6)))

    each_far(early_copy)
    for which in range(2):
        own_copy(which).wait()
    each_pair(lambda *way: first_copy(*way).start())

    def stacked(head):
        return jnp.concatenate(
            [query[:, at_head(head * group + member)] for member in range(group)], axis=0)

    half = group * rows // 2
    halves = [slice(part * half, (part + 1) * half) for part in range(2)]

    def block(keys, values, head, first):
        values = values.T
        values = jnp.concatenate([values, jnp.ones((EXTRA, values.shape[1]), values.dtype)], axis=0)
        queries = stacked(head)
        before_it = [None if first else (top[head, :, part], acc[head, :, part]) for part in halves]
        scores = [lax.dot_general(
            keys, queries[part], (((1,), (1,)), ((), ())), preferred_element_type=jnp.float32) for part in halves]
        if first:
            key = lax.broadcasted_iota(jnp.int32, scores[0].shape, 0)
            row = lax.rem(lax.broadcasted_iota(jnp.int32, scores[0].shape, 1), rows)
            scores = [jnp.where(key <= row, each, -1e30) for each in scores]
        highest = [jnp.max(each, axis=0, keepdims=True) for each in scores]
        if not first:
            highest = [jnp.maximum(each[0], now) for each, now in zip(before_it, highest)]
        results = []
        for each, now, known in zip(scores, highest, before_it):
            weights = jnp.exp2((each - now) * factor).astype(jnp.bfloat16)
            summed = jnp.dot(values, weights, preferred_element_type=jnp.float32)
            if not first:
                summed = known[1] * jnp.exp2((known[0] - now) * factor) + summed
            results.append(summed)
        for part, now, summed in zip(halves, highest, results):
            top[head, :, part] = now
            acc[head, :, part] = summed

    for head in range(heads):
        query_copy(head).wait()

    @pl.loop(0, pieces)
    def _(piece):
        weight_copy(piece).start()

    for head in range(heads):
        block(held[chip, core, 0, :, lanes(head)], held[chip, core, 1, :, lanes(head)], head, True)

    @pl.when(core == 1)
    def _():
        for head in range(heads):
            span_copy(chip, head, 0, far_send.at[0, head], sibling).wait_recv()
        for head in range(heads):
            block(held[chip, 0, 0, :, lanes(head)], held[chip, 0, 1, :, lanes(head)], head, False)

    moved, base = 0, 0
    slots = [[], []]
    for side in range(2):
        for origin in (0, 3, 1, 2):
            count = HANDED_OVER[origin][side]
            here = (chip == origin) & (core == side)
            moved = jnp.where(here, count, moved)
            if origin > 0:
                base = jnp.where(here, len(slots[side]), base)
                slots[side] += [(origin, 2 * each + 1) for each in range(count)]
    fed = jnp.where(chip == 1, jnp.where(core == 0, *HANDED_OVER[0]), 0)

    def columns(piece):
        return o_ref.at[:, pl.ds(pl.multiple_of(piece * COLUMNS, COLUMNS), COLUMNS)]

    def out_copy(piece):
        return pltpu.make_async_remote_copy(
            projected.at[piece], columns(piece), out_send.at[piece], out_recv.at[piece],
            device_id={"pipe": following}, device_id_type=MESH)

    def aside_copy(piece):
        slot = base + piece // 2
        return pltpu.make_async_remote_copy(
            projected.at[piece], aside.at[slot], out_send.at[piece], aside_recv.at[slot],
            device_id={"ctx": jnp.where(chip == 0, 2 + core, core)}, device_id_type=MESH)

    def deliver_copy(slot, origin, piece):
        return pltpu.make_async_remote_copy(
            aside.at[slot], columns(piece), deliver_send.at[slot], out_recv.at[piece],
            device_id={"pipe": following, "ctx": origin * 2 + core}, device_id_type=MESH)

    def each_delivered(act):
        for side in range(2):
            @pl.when((chip == 0) & (core == side))
            def _():
                for slot, place in enumerate(slots[side]):
                    act(slot, *place)

    def deliver(slot, origin, piece):
        pltpu.make_async_remote_copy(
            aside.at[slot], aside.at[slot], deliver_send.at[slot], aside_recv.at[slot],
            device_id={"ctx": sibling}, device_id_type=MESH).wait_recv()
        deliver_copy(slot, origin, piece).start()

    def forward(slot):
        deliver(slot, 0, 2 * slot + 1)

    steps = chip * heads

    def at(step):
        later = step - 2 * heads
        owner_last = jnp.where(later < 0, 1 + lax.rem(step, 2), 0)
        head_last = jnp.where(later < 0, step // 2, (1 - lax.rem(later, 2)) * (heads // 2) + later // 2)
        own_third = (step == 0) | ((step > 1) & (lax.rem(step, 2) == 1))
        head_third = jnp.where(step == 1, heads - 1, jnp.where(own_third, lax.rem(step // 2 + heads // 2, heads), step // 2 - 1))
        owner = jnp.where(chip == 3, owner_last, jnp.where((chip == 2) & jnp.logical_not(own_third), 1, 0))
        head = jnp.where(chip == 3, head_last, jnp.where(chip == 2, head_third, step))
        return owner, head

    def relayed(owner, head):
        late = head >= heads // 2
        last = ((owner == 1) & (head < heads - 1)) | ((owner == 0) & late)
        return ((chip == 1) & jnp.logical_not(late)) | ((chip == 2) & (owner == 0) & late) | ((chip == 3) & last)

    def relay_copy(owner, head):
        target = jnp.where((chip == 1) | ((chip == 3) & (owner == 0)), across, beside)
        return span_copy(owner, head, core, relay_send.at[owner, head], target)

    def arrive(step):
        owner, head = at(step)
        span_copy(owner, head, core, pass_send.at[owner, head], sibling).wait_recv()

        span_copy(owner, head, core, pass_send.at[owner, head], sibling).start()

        @pl.when(relayed(owner, head))
        def _():
            relay_copy(owner, head).start()

    @pl.when(chip > 0)
    def _():
        arrive(0)

    @pl.loop(0, steps)
    def _(step):
        @pl.when((step + 1 < steps) & ((chip > 1) | (step == 0)))
        def _():
            arrive(step + 1)

        owner, head = at(step)
        span_copy(owner, head, 1 - core, pass_send.at[owner, head], sibling).wait_recv()
        keys = held[owner, :, 0, :, at_head(head)].reshape(2 * rows, HEAD_SIZE)
        values = held[owner, :, 1, :, at_head(head)].reshape(2 * rows, HEAD_SIZE)
        block(keys, values, head, False)

        @pl.when((chip == 1) & (step == 0))
        def _():
            forward(0)

        @pl.when((chip == 1) & (step == 1))
        def _():
            @pl.loop(1, fed - 1)
            def _(slot):
                forward(slot)

            arrive(step + 1)
            arrive(step + 2)

        @pl.when((chip == 1) & (step == 2))
        def _():
            forward(fed - 1)

    for head in range(heads):
        for member in range(group):
            part = acc[head, :, member * rows:(member + 1) * rows]
            attended[:, lanes(head * group + member)] = (
                part[:HEAD_SIZE] / part[HEAD_SIZE:HEAD_SIZE + 1]).T.astype(jnp.bfloat16)

    @pl.loop(0, pieces)
    def _(piece):
        weight_copy(piece).wait()
        projected[piece] = jnp.dot(
            attended[...], weight[piece], preferred_element_type=jnp.float32).astype(jnp.bfloat16)

        handed = (lax.rem(piece, 2) == 1) & (piece < 2 * moved)

        @pl.when(jnp.logical_not(handed))
        def _():
            out_copy(piece).start()

        @pl.when(handed)
        def _():
            aside_copy(piece).start()

    each_delivered(deliver)

    each_far(lambda *way: first_copy(*way).wait_send())
    each_pair(lambda *way: first_copy(*way).wait_send())

    @pl.loop(0, steps)
    def _(step):
        owner, head = at(step)
        span_copy(owner, head, core, pass_send.at[owner, head], sibling).wait_send()

        @pl.when(relayed(owner, head))
        def _():
            relay_copy(owner, head).wait_send()

    each_delivered(lambda *place: deliver_copy(*place).wait_send())

    @pl.loop(0, fed)
    def _(slot):
        deliver_copy(slot, 0, 2 * slot + 1).wait_send()

    @pl.loop(0, pieces)
    def _(piece):
        out_copy(piece).wait()


def general_device(sections, spans, queries, keys, values, out_weight):
    rows, q_width = queries.shape[1:]
    kv_width = keys.shape[2]
    width = out_weight.shape[2]
    heads = kv_width // HEAD_SIZE
    stack = q_width // kv_width * rows
    pieces = width // COLUMNS
    chips = spans // 2
    across = math.isqrt(chips)
    across = across if chips % across == 0 else chips
    hbm = pl.BlockSpec(memory_space=pltpu.HBM)
    handed = pl.pallas_call(
        functools.partial(general_kernel, sections, spans, across),
        out_shape=jax.ShapeDtypeStruct((rows, width), jnp.bfloat16),
        in_specs=[hbm] * 4,
        out_specs=pl.BlockSpec(memory_space=pl.ANY),
        scratch_shapes=[
            pltpu.VMEM((chips, 2, 2 * rows, kv_width), jnp.bfloat16),
            pltpu.VMEM((pieces, q_width, COLUMNS), jnp.bfloat16),
            pltpu.VMEM((heads, stack, HEAD_SIZE), jnp.bfloat16),
            pltpu.VMEM((heads, HEAD_SIZE + EXTRA, stack), jnp.float32),
            pltpu.VMEM((heads, 1, stack), jnp.float32),
            pltpu.VMEM((rows, q_width), jnp.bfloat16),
            pltpu.VMEM((pieces, rows, COLUMNS), jnp.bfloat16),
            pltpu.SemaphoreType.DMA((2,)),
            pltpu.SemaphoreType.DMA((chips, 2)),
            pltpu.SemaphoreType.DMA((chips, 2)),
            pltpu.SemaphoreType.DMA((chips, chips)),
            pltpu.SemaphoreType.DMA((chips, 2, 2)),
            pltpu.SemaphoreType.DMA((pieces,)),
            pltpu.SemaphoreType.DMA((pieces,)),
            pltpu.SemaphoreType.DMA((pieces,)),
            pltpu.SemaphoreType.DMA((2,)),
            pltpu.SemaphoreType.DMA((q_width // HEAD_SIZE,)),
            pltpu.VMEM((2, MOVED, rows, COLUMNS), jnp.bfloat16),
            pltpu.VMEM((2, MOVED, rows, COLUMNS), jnp.bfloat16),
            pltpu.SemaphoreType.DMA((2, MOVED)),
            pltpu.SemaphoreType.DMA((2, MOVED)),
            pltpu.SemaphoreType.DMA((2, MOVED)),
            pltpu.SemaphoreType.DMA((2, MOVED)),
        ],
        compiler_params=pltpu.CompilerParams(
            collective_id=0, has_side_effects=True, vmem_limit_bytes=VMEM_LIMIT),
    )(*(pltpu.with_memory_space_constraint(each[0], pltpu.HBM) for each in (queries, keys, values, out_weight)))
    return handed[None]


def square_device(sections, queries, keys, values, out_weight):
    rows, q_width = queries.shape[1:]
    kv_width = keys.shape[2]
    width = out_weight.shape[2]
    heads = kv_width // HEAD_SIZE
    stack = q_width // kv_width * rows
    pieces = width // COLUMNS
    slots = max(max(HANDED_OVER[0]), *(sum(counts[side] for counts in HANDED_OVER[1:]) for side in range(2)))
    hbm = pl.BlockSpec(memory_space=pltpu.HBM)
    handed = pl.pallas_call(
        functools.partial(square_kernel, sections),
        out_shape=jax.ShapeDtypeStruct((rows, width), jnp.bfloat16),
        in_specs=[hbm] * 4,
        out_specs=pl.BlockSpec(memory_space=pl.ANY),
        scratch_shapes=[
            pltpu.VMEM((4, 2, 2, rows, kv_width), jnp.bfloat16),
            pltpu.VMEM((pieces, q_width, COLUMNS), jnp.bfloat16),
            pltpu.VMEM((rows, q_width), jnp.bfloat16),
            pltpu.VMEM((heads, HEAD_SIZE + EXTRA, stack), jnp.float32),
            pltpu.VMEM((heads, 1, stack), jnp.float32),
            pltpu.VMEM((rows, q_width), jnp.bfloat16),
            pltpu.VMEM((pieces, rows, COLUMNS), jnp.bfloat16),
            pltpu.VMEM((slots, rows, COLUMNS), jnp.bfloat16),
            pltpu.SemaphoreType.DMA((4, heads)),
            pltpu.SemaphoreType.DMA((4, 2, heads)),
            pltpu.SemaphoreType.DMA((4, heads)),
            pltpu.SemaphoreType.DMA((2, heads)),
            pltpu.SemaphoreType.DMA((2,)),
            pltpu.SemaphoreType.DMA((heads,)),
            pltpu.SemaphoreType.DMA((pieces,)),
            pltpu.SemaphoreType.DMA((pieces,)),
            pltpu.SemaphoreType.DMA((pieces,)),
            pltpu.SemaphoreType.DMA((slots,)),
            pltpu.SemaphoreType.DMA((slots,)),
        ],
        compiler_params=pltpu.CompilerParams(
            collective_id=1, has_side_effects=True, vmem_limit_bytes=VMEM_LIMIT),
    )(*(pltpu.with_memory_space_constraint(each[0], pltpu.HBM) for each in (queries, keys, values, out_weight)))
    return handed[None]


def per_device(sections, spans, *operands):
    if spans == 8:
        return square_device(sections, *operands)
    return general_device(sections, spans, *operands)


def solution(mesh):
    placed = (
        P("pipe", "ctx", None),
        P("pipe", "ctx", None),
        P("pipe", "ctx", None),
        P("pipe", None, None),
    )
    return jax.shard_map(
        functools.partial(per_device, mesh.shape["pipe"], mesh.shape["ctx"]),
        mesh=mesh, in_specs=placed, out_specs=P("pipe", "ctx", None), check_vma=False
    )
```
